32 devices in a mesh: dp: 8 (over z, x), tensor: 4 (over y, core).
Axes of the slice: x: 2, y: 2, z: 4, core: 2. Of those that a mesh axis runs over, the one named last changes fastest.
Arguments:
- tokens: bfloat16 [16384, 1024], P(('dp', 'tensor')), may hold values from -6 to 6
- doc_ids: int32 [16, 1024], P('dp'), may hold values from 0 to 7, never falling along the last dimension, each value on 1 to 800 neighbouring positions
- mixer_norm: bfloat16 [1024], P('dp'), may hold values from 0.25 to 1.75
- in_weight: bfloat16 [1024, 3, 1024], P('dp', None, 'tensor'), may hold values from -0.1875 to 0.1875
- conv_weight: bfloat16 [3, 1024], P(None, 'dp'), may hold values from -3.5 to 3.5
- out_weight: bfloat16 [1024, 1024], P('tensor', 'dp'), may hold values from -0.1875 to 0.1875
- feed_norm: bfloat16 [1024], P('dp'), may hold values from 0.25 to 1.75
- gate_weight: bfloat16 [1024, 4608], P('dp', 'tensor'), may hold values from -0.1875 to 0.1875
- up_weight: bfloat16 [1024, 4608], P('dp', 'tensor'), may hold values from -0.1875 to 0.1875
- down_weight: bfloat16 [4608, 1024], P('tensor', 'dp'), may hold values from -0.09375 to 0.09375
- out_grad: bfloat16 [16384, 1024], P(('dp', 'tensor')), may hold values from -6 to 6
Outputs:
- output: bfloat16 [16384, 1024], P(('dp', 'tensor'))
- input_grad: bfloat16 [16384, 1024], P(('dp', 'tensor'))
- mixer_norm_grad: float32 [1024], P('dp')
- in_weight_grad: float32 [1024, 3, 1024], P('dp', None, 'tensor')
- conv_weight_grad: float32 [3, 1024], P(None, 'dp')
- out_weight_grad: float32 [1024, 1024], P('tensor', 'dp')
- feed_norm_grad: float32 [1024], P('dp')
- gate_weight_grad: float32 [1024, 4608], P('dp', 'tensor')
- up_weight_grad: float32 [1024, 4608], P('dp', 'tensor')
- down_weight_grad: float32 [4608, 1024], P('tensor', 'dp')
The draws below stay inside these ranges and needn't reach their ends.
Inputs may be any that keep to these rules, and one draw needn't show every extreme that they name: `doc_ids`: within each sequence the document numbers never fall; a document covers 1 to 800 consecutive tokens and one covers exactly 800.
All inputs are finite; a program needn't handle non-finite values.
Results may differ from the reference program's by a relative error of at most 0.015.
Values may be sent and summed in bfloat16 or wider, within the bound.
A program may use at most 128 MiB of HBM per device.

```python
import math
import jax
import jax.numpy as jnp
import numpy as np
from jax import lax

D = 1024
FF = 4608
KW = 3
SEQ_LEN = 1024
SEQ_GROUP = 2
SEQS = 16
TOKENS = 16384
DOC_MOST = 800
SEG_COUNT = 8
N_DP = 8


def strengthened(values, key, source, target, parts, factor):
    owner, partner = [(jnp.arange(values.shape[position]) // (values.shape[position] // parts)).reshape([-1 if axis == position else 1 for axis in range(values.ndim)]) for position in (source, target)]
    chosen = jax.random.permutation(key, parts)[partner]
    strong = (owner == chosen) | (owner == (partner + parts // 2) % parts)
    return jnp.where(strong, factor * values, values)


def block_levels(rng, dims, pieces, least, largest):
    loudness, own = 1.0, jax.random.fold_in(rng, 6)
    for dim, blocks in pieces:
        steps = jnp.exp(jax.random.uniform(jax.random.fold_in(own, dim), (blocks,), jnp.float32, least / len(pieces), largest / len(pieces)))
        loudness = loudness * jnp.repeat(steps, dims[dim] // blocks).reshape([-1 if axis == dim else 1 for axis in range(len(dims))])
    return loudness


def length_profile(number_of, total, reach, slope):
    portions = [(1 << 20) // math.isqrt(standing ** slope) + 1 for standing in range(2, number_of + 1)]
    spare, holding = total - reach - (number_of - 1), [1] * (number_of - 1)
    while spare > 0:
        free = [i for i in range(number_of - 1) if holding[i] < reach]
        mass, budget = sum([portions[i] for i in free]), spare
        for i in free:
            addition = min(reach - holding[i], max(1, budget * portions[i] // mass), spare)
            holding[i] = holding[i] + addition
            spare = spare - addition
    return np.array([reach] + holding)


def ragged(stream_key, amount, total, most, slope):
    if amount == 2:
        one = jax.random.randint(stream_key, (), max(1, total - most), min(most, total - 1) + 1)
        return jnp.stack([one, total - one])
    tallies = jnp.asarray(length_profile(amount, total, most, slope), jnp.int32)
    couples = (amount - 1) // 2
    giver, receiver = tallies[1:1 + 2 * couples:2], tallies[2:2 + 2 * couples:2]
    room = jnp.minimum(giver - 1, most - receiver)
    shifted = jax.random.randint(jax.random.fold_in(stream_key, 1), (couples,), 0, 1 << 20) % (room + 1)
    tallies = tallies.at[1:1 + 2 * couples:2].set(giver - shifted).at[2:2 + 2 * couples:2].set(receiver + shifted)
    return tallies[jax.random.permutation(jax.random.fold_in(stream_key, 2), amount)]


def gaussian(rng, shape, spread, bound, shards=(), held_as=jnp.bfloat16):
    values = spread * jax.random.normal(rng, shape, jnp.float32)
    if shards:
        values = values * block_levels(rng, shape, shards, -0.22, 0.18)
    return jnp.clip(values, -bound, bound).astype(held_as)


def heavy_noise(rng, extent, spread, bound, shards, heavy, kind=jnp.bfloat16):
    values = spread * jax.random.normal(rng, extent, jnp.float32)
    if shards:
        values = values * block_levels(rng, extent, shards, -0.22, 0.18)
    return jnp.clip(strengthened(values, jax.random.fold_in(rng, 3), *heavy), -bound, bound).astype(kind)


def setup_inputs(seed: int = 0) -> dict:
    key_list = jax.random.split(jax.random.key(seed), 12)
    return {
        "tokens": heavy_noise(key_list[0], (TOKENS, D), 1.0, 6.0, ((0, 32),), (0, 1, 32, 2.75)),
        "doc_ids": jax.vmap(lambda own: jnp.searchsorted(jnp.cumsum(ragged(own, SEG_COUNT, SEQ_LEN, DOC_MOST, 0)), jnp.arange(SEQ_LEN), side="right"))(jax.random.split(key_list[1], SEQS)).reshape((SEQS, SEQ_LEN)).astype(jnp.int32),
        "mixer_norm": jnp.clip(1.0 + 0.15 * jax.random.normal(key_list[2], (D,), jnp.float32), 0.25, 1.75).astype(jnp.bfloat16),
        "in_weight": gaussian(key_list[3], (D, 3, D), D ** -0.5, 0.1875, ((0, 8), (2, 4))),
        "conv_weight": gaussian(key_list[4], (KW, D), KW ** -0.5, 3.5, ((1, 8),)),
        "out_weight": gaussian(key_list[5], (D, D), D ** -0.5, 0.1875, ((0, 4), (1, 8))),
        "feed_norm": jnp.clip(1.0 + 0.15 * jax.random.normal(key_list[6], (D,), jnp.float32), 0.25, 1.75).astype(jnp.bfloat16),
        "gate_weight": gaussian(key_list[7], (D, FF), D ** -0.5, 0.1875, ((0, 8), (1, 4))),
        "up_weight": gaussian(key_list[8], (D, FF), D ** -0.5, 0.1875, ((0, 8), (1, 4))),
        "down_weight": gaussian(key_list[9], (FF, D), FF ** -0.5, 0.09375, ((0, 4), (1, 8))),
        "out_grad": heavy_noise(key_list[10], (TOKENS, D), 1.0, 6.0, ((0, 32),), (0, 1, 32, 2.75)),
    }


epsilon = 1e-05

@jax.custom_vjp
def low(v):
    return lax.optimization_barrier(v.astype(jnp.bfloat16)).astype(jnp.float32)

@jax.custom_vjp
def low_back(v):
    return v

def low_keep(v):
    return (low(v), None)

def low_pass(kept, grad):
    return (grad,)

def back_keep(v):
    return (v, None)

def back_low(kept, grad):
    return (low(grad),)
low.defvjp(low_keep, low_pass)
low_back.defvjp(back_keep, back_low)

def rms_scale(values, gain):
    inverse = lax.rsqrt(lax.optimization_barrier(jnp.mean(values * values, axis=-1, keepdims=True)) + epsilon)
    return values * inverse * gain

def shift_down(values, offset):
    if offset == 0:
        return values
    padding = jnp.zeros((offset,) + values.shape[1:], values.dtype)
    return jnp.concatenate([padding, values[:-offset]], axis=0)

def tap_masks(doc_rows):
    total_rows = doc_rows.shape[0] * doc_rows.shape[1]
    tap_keep = [jnp.ones((total_rows,), jnp.float32)]
    for offset in range(1, KW):
        matching = doc_rows[:, offset:] == doc_rows[:, :-offset]
        leading = jnp.zeros((doc_rows.shape[0], offset), dtype=bool)
        matching = jnp.concatenate([leading, matching], axis=1)
        tap_keep.append(jnp.where(matching, 1.0, 0.0).astype(jnp.float32).reshape(total_rows))
    return jnp.stack(tap_keep)

def forward(inputs, gain_one, in_proj, conv_taps, out_proj, gain_two, gate_proj, up_proj, down_proj, tap_keep):
    highest = lax.Precision.HIGHEST
    normed = low(rms_scale(inputs, gain_one))
    projected = low_back(jnp.einsum('td,dkc->tkc', normed, in_proj, precision=highest))
    input_gate = projected[:, 0]
    output_gate = projected[:, 1]
    values = projected[:, 2]
    mixed_input = input_gate * values
    convolved = sum((tap_keep[offset][:, None] * conv_taps[offset][None, :] * shift_down(mixed_input, offset) for offset in range(KW)))
    mixer_in = low(output_gate * convolved)
    mixer_out = low_back(jnp.dot(mixer_in, out_proj, precision=highest))
    hidden = inputs + mixer_out
    normed_two = low(rms_scale(hidden, gain_two))
    gate_pre = low_back(jnp.dot(normed_two, gate_proj, precision=highest))
    upward = low_back(jnp.dot(normed_two, up_proj, precision=highest))
    activated = low(jax.nn.silu(gate_pre) * upward)
    return hidden + jnp.dot(activated, down_proj, precision=highest)

def reference(tokens, doc_ids, mixer_norm, in_weight, conv_weight, out_weight, feed_norm, gate_weight, up_weight, down_weight, out_grad):
    weights = tuple((member.astype(jnp.float32) for member in (mixer_norm, in_weight, conv_weight, out_weight, feed_norm, gate_weight, up_weight, down_weight)))
    group_tokens = SEQ_GROUP * SEQ_LEN
    inputs = tokens.astype(jnp.float32).reshape(N_DP, group_tokens, D)
    cotangent = out_grad.astype(jnp.float32).reshape(N_DP, group_tokens, D)
    documents = doc_ids.reshape(N_DP, SEQ_GROUP, SEQ_LEN)

    def one_group(totals, member):
        group_rows, back_rows, doc_rows = member
        tap_keep = tap_masks(doc_rows)

        def apply_block(rows_in, *params):
            return forward(rows_in, *params, tap_keep)
        result, pullback = jax.vjp(apply_block, group_rows, *weights)
        gradients = pullback(back_rows)
        totals = tuple((total + gradient for total, gradient in zip(totals, gradients[1:])))
        return (totals, (result.astype(jnp.bfloat16), gradients[0].astype(jnp.bfloat16)))
    initial = tuple((jnp.zeros_like(member) for member in weights))
    totals, (results, input_grads) = lax.scan(one_group, initial, (inputs, cotangent, documents))
    all_tokens = N_DP * group_tokens
    return (results.reshape(all_tokens, D), input_grads.reshape(all_tokens, D), totals[0], totals[1], totals[2], totals[3], totals[4], totals[5], totals[6], totals[7])
```

```python
import functools

import jax
import jax.numpy as jnp
from jax import lax
from jax.experimental import pallas as pl
from jax.experimental.pallas import tpu as pltpu
from jax.sharding import PartitionSpec as P

KW = 3
MESH = pl.DeviceIdType.MESH
BF = jnp.bfloat16
F32 = jnp.float32

epsilon = 1e-05

NZ = 4
CONV = 4
FEED = 3
Y_LAST = (True, False, True, False)


def nn(a, b):
    return lax.dot_general(a, b, (((1,), (0,)), ((), ())), preferred_element_type=F32)


def nt(a, b):
    return lax.dot_general(a, b, (((1,), (1,)), ((), ())), preferred_element_type=F32)


def tn(a, b):
    return lax.dot_general(a, b, (((0,), (0,)), ((), ())), preferred_element_type=F32)


class Place:
    def __init__(self):
        self.dp = lax.axis_index("dp")
        self.t = lax.axis_index("tensor")
        self.z, self.x = lax.div(self.dp, 2), lax.rem(self.dp, 2)
        self.y, self.c = lax.div(self.t, 2), lax.rem(self.t, 2)
        self.over_x = (self.z * 2 + 1 - self.x, self.t)
        self.over_y = (self.dp, (1 - self.y) * 2 + self.c)
        self.over_c = (self.dp, self.y * 2 + 1 - self.c)
        self.t_y = (1 - self.y) * 2 + self.c
        self.t_c = self.y * 2 + 1 - self.c
        self.t_yc = (1 - self.y) * 2 + 1 - self.c

    def zs(self, k):
        return lax.rem(self.z + k, NZ)

    def over_z(self, k):
        return (self.zs(k) * 2 + self.x, self.t)


def greet(place, n_dp):
    barrier = pltpu.get_barrier_semaphore()
    for k in range(1, n_dp):
        peer = (lax.rem(place.dp + k, n_dp), place.t)
        pl.semaphore_signal(barrier, inc=1, device_id=peer, device_id_type=MESH)
    for peer in (place.over_c, place.over_y):
        pl.semaphore_signal(barrier, inc=1, device_id=peer, device_id_type=MESH)
    pl.semaphore_wait(barrier, n_dp + 1)


def remote(src, dst, send_sem, recv_sem, peer):
    return pltpu.make_async_remote_copy(
        src_ref=src, dst_ref=dst, send_sem=send_sem, recv_sem=recv_sem, device_id=peer, device_id_type=MESH
    )


def send(*what):
    copy = remote(*what)
    copy.start()
    return copy


def arrived(ref, sem, peer):
    pltpu.make_async_remote_copy(
        src_ref=ref, dst_ref=ref, send_sem=sem, recv_sem=sem, device_id=peer, device_id_type=MESH
    ).wait_recv()


def rows(start, size):
    return pl.ds(pl.multiple_of(start, size), size)


def forward_kernel(
    n_dp,
    tokens, cotangent, keep, small, in_own, out_own, gate_own, up_own, down_own,
    conv_out, feed_out, normed_out, small_out, cot_out, proj_out, mixer_out, hidden_out, two_out, acts_out, down_out, down_y_out,
    conv_w, feed_w, normed, small_all, mixed_pad, c_keep, proj, mixer_in, part_send, part_recv,
    hidden, two, acts, down_send, down_recv,
    own_sem, z_send, z_recv, x_send, x_recv, y_send, y_recv, fz_send, fz_recv, fx_send, fx_recv,
    s_send, s_recv, a_send, a_recv, out_sem,
):
    place = Place()
    z, x, y, c, t = place.z, place.x, place.y, place.c, place.t
    depth = gate_own.shape[0]
    local = tokens.shape[0]
    chip = 2 * local
    width = tokens.shape[1]
    half = in_own.shape[2]
    sends = []
    copies = []
    owned = {}

    def conv_part(j, dp, n, side):
        col = slice(None) if side is None else rows(side * half, half)
        return conv_w.at[j, rows(dp * depth, n * depth), col]

    def feed_part(w, dp):
        return feed_w.at[w, rows(dp * depth, depth), :]

    conv_own = [in_own.at[0], in_own.at[1], in_own.at[2], out_own]
    feed_own = [gate_own, up_own, down_own]

    greet(place, n_dp)

    small_all[place.dp] = small[...]
    for k in range(1, n_dp):
        sends.append(send(small, small_all.at[place.dp], s_send.at[k], s_recv.at[place.dp],
                          (lax.rem(place.dp + k, n_dp), t)))
    own_copies = []
    for j in range(CONV):
        mine = conv_part(j, place.dp, 1, y)
        for k in range(1, NZ):
            sends.append(send(conv_own[j], mine, z_send.at[j, k], z_recv.at[j, z], place.over_z(k)))
        if Y_LAST[j]:
            sends.append(send(conv_own[j], mine, x_send.at[j, z], x_recv.at[j, z], place.over_x))
        else:
            sends.append(send(conv_own[j], mine, y_send.at[j, z], y_recv.at[j, z], place.over_y))
        own = pltpu.make_async_copy(conv_own[j], mine, own_sem.at[j])
        own.start()
        own_copies.append(own)

    def feed_start(w):
        mine = feed_part(w, place.dp)
        for k in range(1, NZ):
            sends.append(send(feed_own[w], mine, fz_send.at[w, k], fz_recv.at[w, z], place.over_z(k)))
        sends.append(send(feed_own[w], mine, fx_send.at[w, z], fx_recv.at[w, z], place.over_x))
        owned[w] = pltpu.make_async_copy(feed_own[w], mine, own_sem.at[CONV + w])
        owned[w].start()

    def feed_forward_on(w, k):
        zk = place.zs(k)
        part = feed_part(w, zk * 2 + x)
        arrived(part, fz_recv.at[w, zk], place.over_z(k))
        sends.append(send(part, part, fx_send.at[w, zk], fx_recv.at[w, zk], place.over_x))

    def feed_wait(w):
        for k in range(NZ):
            zk = place.zs(k)
            arrived(feed_part(w, zk * 2 + 1 - x), fx_recv.at[w, zk], place.over_x)
        owned[w].wait()
        out(feed_w.at[w], feed_out.at[w], 7 + w)

    def out(src, dst, index):
        copy = pltpu.make_async_copy(src, dst, out_sem.at[index])
        copy.start()
        copies.append(copy)

    feed_start(0)

    cot_mine = cot_out.at[rows(t * local, local), :]
    sends.append(send(cotangent, cot_mine, a_send.at[0], a_recv.at[0], place.over_c))
    own_cot = pltpu.make_async_copy(cotangent, cot_mine, own_sem.at[CONV + FEED])
    own_cot.start()

    for k in range(1, n_dp):
        peer = lax.rem(place.dp + k, n_dp)
        arrived(small_all.at[peer], s_recv.at[peer], (peer, t))
    gains = [jnp.concatenate([small_all[d, r : r + 1, :] for d in range(n_dp)], axis=1) for r in range(2)]
    inputs = tokens[...].astype(F32)
    inverse = lax.rsqrt(jnp.mean(inputs * inputs, axis=-1, keepdims=True) + epsilon)
    normed[rows(c * local, local), :] = (inputs * inverse * gains[0]).astype(BF)
    normed_mine = normed.at[rows(c * local, local), :]
    sends.append(send(normed_mine, normed_mine, a_send.at[1], a_recv.at[1], place.over_c))

    for k in range(1, NZ):
        zk = place.zs(k)
        for j in range(CONV):
            part = conv_part(j, zk * 2 + x, 1, y)
            arrived(part, z_recv.at[j, zk], place.over_z(k))
            if Y_LAST[j]:
                sends.append(send(part, part, x_send.at[j, zk], x_recv.at[j, zk], place.over_x))
            else:
                sends.append(send(part, part, y_send.at[j, zk], y_recv.at[j, zk], place.over_y))
    for own in own_copies:
        own.wait()
    feed_start(1)
    for k in range(NZ):
        zk = place.zs(k)
        for j in range(CONV):
            if Y_LAST[j]:
                arrived(conv_part(j, zk * 2 + 1 - x, 1, y), x_recv.at[j, zk], place.over_x)
                pair = conv_part(j, zk * 2, 2, y)
                sends.append(send(pair, pair, y_send.at[j, zk], y_recv.at[j, zk], place.over_y))
            else:
                arrived(conv_part(j, zk * 2 + x, 1, 1 - y), y_recv.at[j, zk], place.over_y)
                pair = conv_part(j, zk * 2 + x, 1, None)
                sends.append(send(pair, pair, x_send.at[j, zk], x_recv.at[j, zk], place.over_x))
    sends.append(send(cotangent, cot_mine, a_send.at[2], a_recv.at[2], place.over_y))
    for k in range(1, NZ):
        feed_forward_on(0, k)
    feed_start(2)
    arrived(normed.at[rows((1 - c) * local, local), :], a_recv.at[1], place.over_c)
    for j in range(CONV):
        for k in range(NZ):
            zk = place.zs(k)
            if Y_LAST[j]:
                arrived(conv_part(j, zk * 2, 2, 1 - y), y_recv.at[j, zk], place.over_y)
            else:
                arrived(conv_part(j, zk * 2 + 1 - x, 1, None), x_recv.at[j, zk], place.over_x)
    out(conv_w, conv_out, 0)
    out(normed, normed_out, 1)

    tile = 256
    pad = 8
    mixed_pad[0:pad, :] = jnp.zeros((pad, 2 * half), F32)

    def project(i, carry):
        at = rows(i * tile, tile)
        lhs = normed[at, :]
        b = nn(lhs, conv_w[0])
        proj[0, at, :] = b.astype(BF)
        v = nn(lhs, conv_w[2])
        proj[2, at, :] = v.astype(BF)
        mixed_pad[pl.ds(pl.multiple_of(i * tile + pad, 8), tile), :] = b * v
        g = nn(lhs, conv_w[1])
        proj[1, at, :] = g.astype(BF)
        c_keep[at, :] = g
        return carry

    lax.fori_loop(0, chip // tile, project, 0)

    taps = []
    for r in range(2, 2 + KW):
        taps.append(jnp.concatenate(
            [small_all[side * 4 + 2 * c + i, r : r + 1, :] for side in range(2) for i in range(2)], axis=1))

    def convolve(i, carry):
        at = rows(i * tile, tile)
        window = mixed_pad[pl.ds(pl.multiple_of(i * tile, 8), tile + pad), :]
        total = taps[0] * window[pad:, :]
        for k in range(1, KW):
            mask = jnp.concatenate([keep[k - 1, at, :]] * (2 * half // 128), axis=1)
            total = total + mask * taps[k] * window[pad - k : pad - k + tile, :]
        proj[3, at, :] = total.astype(BF)
        mixer_in[at, :] = (c_keep[at, :] * total).astype(BF)
        return carry

    lax.fori_loop(0, chip // tile, convolve, 0)
    out(proj, proj_out, 2)
    out(mixer_in, mixer_out, 3)

    part_send[...] = nt(mixer_in[rows((1 - c) * local, local), :], conv_w[3]).astype(BF)
    sends.append(send(part_send, part_recv, a_send.at[3], a_recv.at[3], place.over_c))
    hidden[...] = tokens[...].astype(F32) + nt(mixer_in[rows(c * local, local), :], conv_w[3])
    arrived(part_recv, a_recv.at[3], place.over_c)
    total = hidden[...] + part_recv[...].astype(F32)
    hidden[...] = total
    inverse = lax.rsqrt(jnp.mean(total * total, axis=-1, keepdims=True) + epsilon)
    two[rows(t * local, local), :] = (total * inverse * gains[1]).astype(BF)
    two_mine = two.at[rows(t * local, local), :]
    sends.append(send(two_mine, two_mine, a_send.at[4], a_recv.at[4], place.over_c))
    sends.append(send(two_mine, two_mine, a_send.at[5], a_recv.at[5], place.over_y))
    hidden_copy = len(copies)
    out(hidden, hidden_out, 4)

    for k in range(1, NZ):
        feed_forward_on(1, k)
    there = cot_out.at[rows(place.t_y * local, local), :]
    arrived(there, a_recv.at[2], place.over_y)
    sends.append(send(there, there, a_send.at[6], a_recv.at[6], place.over_c))
    feed_wait(0)
    feed_wait(1)

    def feed(block):
        def step(i, carry):
            at = rows(block * local + i * tile, tile)
            lhs = two[at, :]
            gate = nn(lhs, feed_w[0])
            upward = nn(lhs, feed_w[1])
            s = jax.nn.sigmoid(gate)
            silu = gate * s
            acts[0, at, :] = (silu * upward).astype(BF)
            acts[1, at, :] = (upward * (s + silu * (1.0 - s))).astype(BF)
            acts[2, at, :] = silu.astype(BF)
            return carry

        lax.fori_loop(0, local // tile, step, 0)

    feed(t)
    feed_forward_on(2, 1)
    arrived(two.at[rows(place.t_c * local, local), :], a_recv.at[4], place.over_c)
    there = two.at[rows(place.t_y * local, local), :]
    arrived(there, a_recv.at[5], place.over_y)
    sends.append(send(there, there, a_send.at[7], a_recv.at[7], place.over_c))
    feed(place.t_c)
    feed_forward_on(2, 2)
    feed(place.t_y)
    feed_forward_on(2, 3)
    arrived(two.at[rows(place.t_yc * local, local), :], a_recv.at[7], place.over_c)
    feed(place.t_yc)
    out(acts, acts_out, 5)
    out(two, two_out, 6)
    small_out[...] = small_all[...]
    feed_wait(2)
    arrived(cot_out.at[rows(place.t_c * local, local), :], a_recv.at[0], place.over_c)
    arrived(cot_out.at[rows(place.t_yc * local, local), :], a_recv.at[6], place.over_c)
    own_cot.wait()

    for i, block in enumerate((place.t_yc, place.t_c)):
        down_send[i] = nt(acts[0, rows(block * local, local), :], feed_w[2]).astype(BF)
        sends.append(send(down_send.at[i], down_recv.at[i], a_send.at[8 + i], a_recv.at[8 + i], place.over_c))
    far = nt(acts[0, rows(place.t_y * local, local), :], feed_w[2])
    arrived(down_recv.at[0], a_recv.at[8], place.over_c)
    down_recv[0] = (far + down_recv[0].astype(F32)).astype(BF)
    out(down_recv.at[0], down_y_out, 10)
    copies[hidden_copy].wait()
    hidden[...] = hidden[...] + nt(acts[0, rows(t * local, local), :], feed_w[2])
    arrived(down_recv.at[1], a_recv.at[9], place.over_c)
    hidden[...] = hidden[...] + down_recv[1].astype(F32)
    out(hidden, down_out, 11)
    for copy in sends:
        copy.wait_send()
    for i, copy in enumerate(copies):
        if i != hidden_copy:
            copy.wait()


def forward_call(n_dp, *operands):
    tokens, _, _, _, in_own, _, gate_own, _, _ = operands
    local, width = tokens.shape
    half, units = in_own.shape[2], gate_own.shape[1]
    chip, group, mine = 2 * local, 4 * local, 2 * half

    def shaped(dims, kind=BF):
        return jax.ShapeDtypeStruct(dims, kind)

    dma = pltpu.SemaphoreType.DMA
    vmem, any_space = pl.BlockSpec(memory_space=pltpu.VMEM), pl.BlockSpec(memory_space=pl.ANY)
    return pl.pallas_call(
        functools.partial(forward_kernel, n_dp),
        name="gather_forward",
        out_shape=(
            shaped((CONV, width, mine)), shaped((FEED, width, units)), shaped((chip, width)), shaped((n_dp, 8, 128), F32),
            shaped((group, width)), shaped((4, chip, mine)), shaped((chip, mine)), shaped((local, width), F32),
            shaped((group, width)), shaped((3, group, units)), shaped((local, width), F32), shaped((local, width)),
        ),
        in_specs=[vmem] * 4 + [any_space] * 5,
        out_specs=tuple(vmem if i == 3 else any_space for i in range(12)),
        scratch_shapes=[
            pltpu.VMEM((CONV, width, mine), BF), pltpu.VMEM((FEED, width, units), BF), pltpu.VMEM((chip, width), BF),
            pltpu.VMEM((n_dp, 8, 128), F32), pltpu.VMEM((chip + 8, mine), F32),
            pltpu.VMEM((chip, mine), F32), pltpu.VMEM((4, chip, mine), BF), pltpu.VMEM((chip, mine), BF),
            pltpu.VMEM((local, width), BF), pltpu.VMEM((local, width), BF), pltpu.VMEM((local, width), F32),
            pltpu.VMEM((group, width), BF), pltpu.VMEM((3, group, units), BF),
            pltpu.VMEM((2, local, width), BF), pltpu.VMEM((2, local, width), BF),
            dma((8,)), dma((CONV, NZ)), dma((CONV, NZ)), dma((CONV, NZ)), dma((CONV, NZ)), dma((CONV, NZ)), dma((CONV, NZ)),
            dma((FEED, NZ)), dma((FEED, NZ)), dma((FEED, NZ)), dma((FEED, NZ)),
            dma((n_dp,)), dma((n_dp,)), dma((10,)), dma((10,)), dma((12,)),
        ],
        compiler_params=pltpu.CompilerParams(collective_id=0, has_side_effects=True, vmem_limit_bytes=62 << 20),
    )(*operands)


def backward_kernel(
    n_dp,
    tokens, cotangent, keep, small_all, conv_in, feed_in, normed_in, cot_in, proj_in, mixer_in_hbm, hidden_in, two_in, acts_in, down_in, down_y_in,
    output, input_grad, in_grad, out_grad, gate_grad, up_grad, down_grad, small_grad,
    act, g_down, x_got, z_got, g_conv, c_got_y, c_got_x, c_two, c_z, two_send, two_recv, two_y, own_two,
    down_got, hidden, grad_mix, small_sum, small_got, small_z,
    load_sem, fx_send, fx_recv, fz_send, fz_recv, c1_send, c1_recv, c2_send, c2_recv, c3_send, c3_recv,
    s_send, s_recv, a_send, a_recv,
):
    place = Place()
    z, x, y, c, t = place.z, place.x, place.y, place.c, place.t
    depth = gate_grad.shape[0]
    local, width = tokens.shape
    chip = 2 * local
    units = act.shape[1]
    mine = g_conv.shape[2]
    half = mine // 2
    tile = 256
    order = (1, 2, 3, 0)
    sends = []

    def post(make):
        make().start()
        sends.append(make)
        return make

    def load(src, dst, index):
        copy = pltpu.make_async_copy(src, dst, load_sem.at[index])
        copy.start()
        return copy

    greet(place, n_dp)
    post(lambda: remote(down_y_in, down_got, a_send.at[0], a_recv.at[0], place.over_y))

    def g_rows(w, start, size):
        if w == 2:
            return g_down.at[rows(start, size), :]
        return act.at[rows(w * width + start, size), :]

    def feed_x(w, k):
        def make():
            zk = place.zs(k)
            return remote(g_rows(w, (zk * 2 + 1 - x) * depth, depth), x_got.at[w, zk], fx_send.at[w, zk], fx_recv.at[w, zk], place.over_x)

        post(make)

    def feed_z(w, k):
        zk = place.zs(k)
        got = x_got.at[w, zk]
        arrived(got, fx_recv.at[w, zk], place.over_x)
        if k:
            got[...] = (g_rows(w, (zk * 2 + x) * depth, depth)[...].astype(F32) + got[...].astype(F32)).astype(BF)
            post(lambda: remote(x_got.at[w, place.zs(k)], z_got.at[w, NZ - k - 1], fz_send.at[w, k], fz_recv.at[w, NZ - k], place.over_z(k)))

    def feed_end(w):
        total = g_rows(w, (z * 2 + x) * depth, depth)[...].astype(F32) + x_got[w, z].astype(F32)
        for k in range(1, NZ):
            arrived(z_got.at[w, k - 1], fz_recv.at[w, k], place.over_z(k))
            total = total + z_got[w, k - 1].astype(F32)
        return total

    def first_slot():
        return remote(two_send.at[0], two_recv.at[0], a_send.at[1], a_recv.at[1], place.over_c)

    def feed_phase(feed_w, cot, acts):
        loads = [load(acts_in.at[0], act, 0), load(cot_in, cot, 1), load(feed_in, feed_w, 2),
                 load(acts_in.at[1], acts.at[0], 3), load(acts_in.at[2], acts.at[1], 4), load(hidden_in, hidden, 5)]
        loads[0].wait()
        loads[1].wait()
        for k in order:
            at = rows(place.zs(k) * 2 * depth, 2 * depth)
            g_down[at, :] = tn(cot[:, at], act[...]).astype(BF)
            feed_x(2, k)
        for index in (2, 3, 4):
            loads[index].wait()

        def back(block, store):
            def step(i, carry):
                at = rows(block * local + i * tile, tile)
                grad_act = nn(cot[at, :], feed_w[2])
                grad_gate = (grad_act * acts[0, at, :].astype(F32)).astype(BF)
                acts[0, at, :] = grad_gate
                grad_up = (grad_act * acts[1, at, :].astype(F32)).astype(BF)
                acts[1, at, :] = grad_up
                store(rows(i * tile, tile), nt(grad_gate, feed_w[0]) + nt(grad_up, feed_w[1]))
                return carry

            lax.fori_loop(0, local // tile, step, 0)

        def to_slot(slot):
            def store(at, value):
                two_send[slot, at, :] = value.astype(BF)

            return store

        def to_own(at, value):
            own_two[at, :] = value

        back(place.t_yc, to_slot(0))
        post(first_slot)
        feed_z(2, 1)
        back(place.t_y, to_own)
        arrived(two_recv.at[0], a_recv.at[1], place.over_c)
        two_recv[0] = (own_two[...] + two_recv[0].astype(F32)).astype(BF)
        post(lambda: remote(two_recv.at[0], two_y, a_send.at[2], a_recv.at[2], place.over_y))
        feed_z(2, 2)
        back(place.t_c, to_slot(1))
        post(lambda: remote(two_send.at[1], two_recv.at[1], a_send.at[3], a_recv.at[3], place.over_c))
        feed_z(2, 3)
        feed_z(2, 0)
        back(t, to_own)
        two = load(two_in, cot, 6)
        two.wait()
        for w in (0, 1):
            for k in order:
                at = rows(place.zs(k) * 2 * depth, 2 * depth)
                act[rows(w * width + place.zs(k) * 2 * depth, 2 * depth), :] = tn(cot[:, at], acts[w]).astype(BF)
                feed_x(w, k)
                if w == 1:
                    feed_z(0, k)
        loads[5].wait()

    pl.run_scoped(
        feed_phase,
        pltpu.VMEM((FEED, width, units), BF), pltpu.VMEM((4 * local, width), BF), pltpu.VMEM((2, 4 * local, units), BF),
    )

    gains = [jnp.concatenate([small_all[d, r : r + 1, :] for d in range(n_dp)], axis=1) for r in range(2)]

    def norm_back(grad, unit, inverse, gain):
        scaled = grad * gain
        return inverse * (scaled - unit * jnp.mean(scaled * unit, axis=-1, keepdims=True))

    def rms(values):
        return lax.rsqrt(jnp.mean(values * values, axis=-1, keepdims=True) + epsilon)

    def c1_slot(j, zk):
        return c_got_y.at[j // 2, zk] if Y_LAST[j] else c_got_x.at[j // 2, zk]

    def conv_first(j, k):
        def make():
            zk = place.zs(k)
            if Y_LAST[j]:
                src, peer = g_conv.at[j, rows(zk * 2 * depth, 2 * depth), rows((1 - y) * half, half)], place.over_y
            else:
                src, peer = g_conv.at[j, rows((zk * 2 + 1 - x) * depth, depth), :], place.over_x
            return remote(src, c1_slot(j, zk), c1_send.at[j, zk], c1_recv.at[j, zk], peer)

        post(make)

    def conv_second(j, k):
        zk = place.zs(k)
        got = c1_slot(j, zk)
        if Y_LAST[j]:
            arrived(got, c1_recv.at[j, zk], place.over_y)
            held = g_conv[j, rows(zk * 2 * depth, 2 * depth), rows(y * half, half)]
        else:
            arrived(got, c1_recv.at[j, zk], place.over_x)
            held = g_conv[j, rows((zk * 2 + x) * depth, depth), :]
        got[...] = (held.astype(F32) + got[...].astype(F32)).astype(BF)

        def make():
            zk = place.zs(k)
            if Y_LAST[j]:
                src, peer = c1_slot(j, zk).at[rows((1 - x) * depth, depth), :], place.over_x
            else:
                src, peer = c1_slot(j, zk).at[:, rows((1 - y) * half, half)], place.over_y
            return remote(src, c_two.at[j, zk], c2_send.at[j, zk], c2_recv.at[j, zk], peer)

        post(make)

    def conv_third(j, k):
        zk = place.zs(k)
        if Y_LAST[j]:
            arrived(c_two.at[j, zk], c2_recv.at[j, zk], place.over_x)
            held = c_got_y[j // 2, zk, rows(x * depth, depth), :]
        else:
            arrived(c_two.at[j, zk], c2_recv.at[j, zk], place.over_y)
            held = c_got_x[j // 2, zk, :, rows(y * half, half)]
        if k:
            c_two[j, zk] = (held.astype(F32) + c_two[j, zk].astype(F32)).astype(BF)
            post(lambda: remote(c_two.at[j, place.zs(k)], c_z.at[j, NZ - k - 1], c3_send.at[j, k], c3_recv.at[j, NZ - k], place.over_z(k)))

    def conv_end(j):
        if Y_LAST[j]:
            held = c_got_y[j // 2, z, rows(x * depth, depth), :]
        else:
            held = c_got_x[j // 2, z, :, rows(y * half, half)]
        total = held.astype(F32) + c_two[j, z].astype(F32)
        for k in range(1, NZ):
            arrived(c_z.at[j, k - 1], c3_recv.at[j, k], place.over_z(k))
            total = total + c_z[j, k - 1].astype(F32)
        return total

    def conv_phase(conv_w, proj, normed, mixer_in, grad_proj, pad_grad, tap_sum):
        loads = [load(conv_in, conv_w, 0), load(mixer_in_hbm, mixer_in, 1), load(proj_in, proj, 2), load(normed_in, normed, 3)]

        arrived(two_y, a_recv.at[2], place.over_y)
        arrived(two_recv.at[1], a_recv.at[3], place.over_c)

        def second_norm(i, carry):
            at = rows(i * 128, 128)
            grad_two = own_two[at, :] + two_recv[1, at, :].astype(F32) + two_y[at, :].astype(F32)
            values = hidden[at, :]
            inverse = rms(values)
            unit = values * inverse
            grad_hidden = cotangent[at, :].astype(F32) + norm_back(grad_two, unit, inverse, gains[1])
            hidden[at, :] = grad_hidden
            grad_mix[rows(c * local + i * 128, 128), :] = grad_hidden.astype(BF)
            return carry + jnp.sum(grad_two * unit, axis=0, keepdims=True)

        feed_gain = lax.fori_loop(0, local // 128, second_norm, jnp.zeros((1, width), F32))

        def send_mix():
            mix_mine = grad_mix.at[rows(c * local, local), :]
            return remote(mix_mine, mix_mine, a_send.at[4], a_recv.at[4], place.over_c)

        post(send_mix)
        for k in order:
            feed_z(1, k)
        for copy in loads:
            copy.wait()
        arrived(grad_mix.at[rows((1 - c) * local, local), :], a_recv.at[4], place.over_c)

        taps = []
        for r in range(2, 2 + KW):
            taps.append(jnp.concatenate(
                [small_all[side * 4 + 2 * c + i, r : r + 1, :] for side in range(2) for i in range(2)], axis=1))
        pad_grad[pl.ds(chip, 8), :] = jnp.zeros((8, mine), F32)

        def first_half(i, carry):
            at = rows(i * tile, tile)
            grad_in = nn(grad_mix[at, :], conv_w[3])
            grad_proj[1, at, :] = (grad_in * proj[3, at, :].astype(F32)).astype(BF)
            pad_grad[at, :] = grad_in * proj[1, at, :].astype(F32)
            return carry

        lax.fori_loop(0, chip // tile, first_half, 0)

        def weight_grad(j, lhs, rhs):
            g_conv[j] = tn(lhs, rhs).astype(BF)
            for k in order:
                conv_first(j, k)

        weight_grad(3, grad_mix[...], mixer_in[...])
        weight_grad(1, normed[...], grad_proj[1])
        tap_sum[...] = jnp.zeros_like(tap_sum)
        small_tile = 128

        def second_half(i, carry):
            at = rows(i * small_tile, small_tile)
            wide = pl.ds(pl.multiple_of(i * small_tile, 8), small_tile + 8)
            window = pad_grad[wide, :]
            b, v = proj[0, at, :].astype(F32), proj[2, at, :].astype(F32)
            mixed = b * v
            now = window[:small_tile, :]
            total = taps[0] * now
            tap_sum[0:1, :] += jnp.sum(now * mixed, axis=0, keepdims=True)
            for k in range(1, KW):
                mask = jnp.concatenate([keep[k - 1, wide, :]] * (mine // 128), axis=1)
                ahead = (mask * window)[k : k + small_tile, :]
                total = total + taps[k] * ahead
                tap_sum[k : k + 1, :] += jnp.sum(ahead * mixed, axis=0, keepdims=True)
            grad_proj[0, at, :] = (total * v).astype(BF)
            grad_proj[2, at, :] = (total * b).astype(BF)
            return carry

        lax.fori_loop(0, chip // small_tile, second_half, 0)
        weight_grad(0, normed[...], grad_proj[0])
        weight_grad(2, normed[...], grad_proj[2])

        def first_grad(block):
            at = rows(block * local, local)
            return nt(grad_proj[0, at, :], conv_w[0]) + nt(grad_proj[1, at, :], conv_w[1]) + nt(grad_proj[2, at, :], conv_w[2])

        first_slot().wait_send()
        sends.remove(first_slot)
        two_send[0] = first_grad(1 - c).astype(BF)
        post(lambda: remote(two_send.at[0], two_recv.at[1], a_send.at[5], a_recv.at[5], place.over_c))
        own_two[...] = first_grad(c)
        for k in order:
            for j in (3, 1):
                conv_second(j, k)
        arrived(two_recv.at[1], a_recv.at[5], place.over_c)

        def first_norm(i, carry):
            at = rows(i * 128, 128)
            grad_one = own_two[at, :] + two_recv[1, at, :].astype(F32)
            values = tokens[at, :].astype(F32)
            inverse = rms(values)
            unit = values * inverse
            two_recv[1, at, :] = (hidden[at, :] + norm_back(grad_one, unit, inverse, gains[0])).astype(BF)
            return carry + jnp.sum(grad_one * unit, axis=0, keepdims=True)

        mixer_gain = lax.fori_loop(0, local // 128, first_norm, jnp.zeros((1, width), F32))
        zero = jnp.zeros((1, 128), F32)
        for d in range(n_dp):
            cols = slice(d * 128, d * 128 + 128)
            here = (c == (d % 4) // 2).astype(F32)
            own = (d // 4) * half + (d % 2) * 128
            small_sum[d] = jnp.concatenate(
                [mixer_gain[:, cols], feed_gain[:, cols]]
                + [here * tap_sum[k : k + 1, own : own + 128] for k in range(KW)] + [zero] * 3, axis=0)

    pl.run_scoped(
        conv_phase,
        pltpu.VMEM((CONV, width, mine), BF), pltpu.VMEM((4, chip, mine), BF), pltpu.VMEM((chip, width), BF),
        pltpu.VMEM((chip, mine), BF), pltpu.VMEM((3, chip, mine), BF), pltpu.VMEM((chip + 8, mine), F32), pltpu.VMEM((8, mine), F32),
    )

    input_copy = load(two_recv.at[1], input_grad, 5)
    post(lambda: remote(small_sum, small_got.at[0], s_send.at[0], s_recv.at[0], place.over_c))
    for k in order:
        for j in (0, 2):
            conv_second(j, k)
    arrived(small_got.at[0], s_recv.at[0], place.over_c)
    small_got[0] = small_sum[...] + small_got[0]
    post(lambda: remote(small_got.at[0], small_got.at[1], s_send.at[1], s_recv.at[1], place.over_y))
    for k in order:
        for j in (3, 1):
            conv_third(j, k)
    final = load(down_in, own_two, 4)
    for w, ref in ((2, None), (0, gate_grad), (1, up_grad)):
        total = feed_end(w)
        if ref is None:
            down_grad[...] = jnp.transpose(total)
        else:
            ref[...] = total
    arrived(small_got.at[1], s_recv.at[1], place.over_y)
    small_got[1] = small_got[0] + small_got[1]
    for k in range(NZ):
        zk = place.zs(k)
        post(lambda zk=zk, k=k: remote(small_got.at[1, zk * 2 + 1 - x], small_z.at[zk], s_send.at[2 + k], s_recv.at[2 + zk], place.over_x))
    for k in order:
        for j in (0, 2):
            conv_third(j, k)
    arrived(down_got, a_recv.at[0], place.over_y)
    final.wait()
    down_got[...] = (own_two[...] + down_got[...].astype(F32)).astype(BF)
    output_copy = load(down_got, output, 6)
    for k in order:
        zk = place.zs(k)
        arrived(small_z.at[zk], s_recv.at[2 + zk], place.over_x)
        small_z[zk] = small_z[zk] + small_got[1, zk * 2 + x]
        if k:
            post(lambda zk=zk, k=k: remote(
                small_z.at[zk], small_z.at[NZ + NZ - k], s_send.at[6 + k], s_recv.at[6 + NZ - k], place.over_z(k)))
    out_grad[...] = jnp.transpose(conv_end(3))
    in_grad[1] = conv_end(1)
    in_grad[0] = conv_end(0)
    in_grad[2] = conv_end(2)
    total = small_z[z]
    for k in range(1, NZ):
        arrived(small_z.at[NZ + k], s_recv.at[6 + k], place.over_z(k))
        total = total + small_z[NZ + k]
    small_grad[...] = total
    for make in sends:
        make().wait_send()
    input_copy.wait()
    output_copy.wait()


def backward_call(n_dp, tokens, cotangent, keep, small_all, conv_w, feed_w, *rest):
    local, width = tokens.shape
    units, mine = feed_w.shape[2], conv_w.shape[2]
    chip, half, depth = 2 * local, mine // 2, width // n_dp

    def shaped(dims, kind=BF):
        return jax.ShapeDtypeStruct(dims, kind)

    dma = pltpu.SemaphoreType.DMA
    vmem, any_space = pl.BlockSpec(memory_space=pltpu.VMEM), pl.BlockSpec(memory_space=pl.ANY)
    return pl.pallas_call(
        functools.partial(backward_kernel, n_dp),
        name="backward_scatter",
        out_shape=(
            shaped((local, width)), shaped((local, width)), shaped((3, depth, half), F32), shaped((half, depth), F32),
            shaped((depth, units), F32), shaped((depth, units), F32), shaped((units, depth), F32), shaped((8, 128), F32),
        ),
        in_specs=[vmem] * 4 + [any_space] * (2 + len(rest)),
        out_specs=(any_space,) * 2 + (vmem,) * 6,
        scratch_shapes=[
            pltpu.VMEM((4 * local, units), BF), pltpu.VMEM((width, units), BF), pltpu.VMEM((FEED, NZ, depth, units), BF),
            pltpu.VMEM((FEED, NZ - 1, depth, units), BF), pltpu.VMEM((CONV, width, mine), BF),
            pltpu.VMEM((2, NZ, 2 * depth, half), BF), pltpu.VMEM((2, NZ, depth, mine), BF), pltpu.VMEM((CONV, NZ, depth, half), BF),
            pltpu.VMEM((CONV, NZ - 1, depth, half), BF), pltpu.VMEM((2, local, width), BF), pltpu.VMEM((2, local, width), BF),
            pltpu.VMEM((local, width), BF), pltpu.VMEM((local, width), F32), pltpu.VMEM((local, width), BF),
            pltpu.VMEM((local, width), F32), pltpu.VMEM((chip, width), BF), pltpu.VMEM((n_dp, 8, 128), F32),
            pltpu.VMEM((2, n_dp, 8, 128), F32), pltpu.VMEM((2 * NZ, 8, 128), F32),
            dma((7,)), dma((FEED, NZ)), dma((FEED, NZ)), dma((FEED, NZ)), dma((FEED, NZ)), dma((CONV, NZ)), dma((CONV, NZ)),
            dma((CONV, NZ)), dma((CONV, NZ)), dma((CONV, NZ)), dma((CONV, NZ)), dma((10,)), dma((10,)), dma((6,)), dma((6,)),
        ],
        compiler_params=pltpu.CompilerParams(collective_id=1, has_side_effects=True, vmem_limit_bytes=63 << 20),
    )(tokens, cotangent, keep, small_all, conv_w, feed_w, *rest)


def block(n_dp, tokens, doc_ids, mixer_norm, in_weight, conv_weight, out_weight, feed_norm, gate_weight, up_weight, down_weight, out_grad):
    chip = 2 * tokens.shape[0]
    documents = lax.dynamic_index_in_dim(doc_ids, lax.div(lax.axis_index("tensor"), 2), 0, keepdims=False)
    keep = []
    for offset in range(1, KW):
        same = jnp.concatenate([jnp.zeros((offset,), bool), documents[offset:] == documents[:-offset], jnp.zeros((8,), bool)])
        keep.append(jnp.broadcast_to(same.astype(F32)[:, None], (chip + 8, 128)))
    keep = jnp.stack(keep)
    small = jnp.concatenate(
        [mixer_norm[None], feed_norm[None], conv_weight, jnp.zeros((6 - KW, mixer_norm.shape[0]), BF)], axis=0).astype(F32)
    conv_w, feed_w, normed, small_all, cot, proj, mixer_in, hidden, two, acts, down, down_y = forward_call(
        n_dp, tokens, out_grad, keep, small, in_weight.transpose(1, 0, 2), out_weight.T, gate_weight, up_weight, down_weight.T)
    output, input_grad, in_g, out_g, gate_g, up_g, down_g, small_g = backward_call(
        n_dp, tokens, out_grad, keep, small_all, conv_w, feed_w, normed, cot, proj, mixer_in, hidden, two, acts, down, down_y)
    return (output, input_grad, small_g[0], in_g.transpose(1, 0, 2), small_g[2 : 2 + KW], out_g, small_g[1], gate_g, up_g, down_g)


def shift_down(values, offset):
    if offset == 0:
        return values
    padding = jnp.zeros((offset,) + values.shape[1:], values.dtype)
    return jnp.concatenate([padding, values[:-offset]], axis=0)


def shift_up(values, offset):
    if offset == 0:
        return values
    padding = jnp.zeros((offset,) + values.shape[1:], values.dtype)
    return jnp.concatenate([values[offset:], padding], axis=0)


def tap_masks(doc_rows):
    total_rows = doc_rows.shape[0] * doc_rows.shape[1]
    tap_keep = [jnp.ones((total_rows,), jnp.float32)]
    for offset in range(1, KW):
        matching = doc_rows[:, offset:] == doc_rows[:, :-offset]
        leading = jnp.zeros((doc_rows.shape[0], offset), dtype=bool)
        matching = jnp.concatenate([leading, matching], axis=1)
        tap_keep.append(jnp.where(matching, 1.0, 0.0).astype(jnp.float32).reshape(total_rows))
    return jnp.stack(tap_keep)


def norm_back(grad_out, unit_rows, inverse, gain):
    scaled = grad_out * gain
    return inverse * (scaled - unit_rows * jnp.mean(scaled * unit_rows, axis=-1, keepdims=True))


def body(
    tokens,
    doc_ids,
    mixer_norm,
    in_weight,
    conv_weight,
    out_weight,
    feed_norm,
    gate_weight,
    up_weight,
    down_weight,
    out_grad,
):
    model_width = tokens.shape[1]
    gathered = (
        lax.all_gather(mixer_norm, "dp", axis=0, tiled=True),
        lax.all_gather(in_weight, "dp", axis=0, tiled=True),
        lax.all_gather(conv_weight, "dp", axis=1, tiled=True),
        lax.all_gather(out_weight, "dp", axis=1, tiled=True),
        lax.all_gather(feed_norm, "dp", axis=0, tiled=True),
        lax.all_gather(gate_weight, "dp", axis=0, tiled=True),
        lax.all_gather(up_weight, "dp", axis=0, tiled=True),
        lax.all_gather(down_weight, "dp", axis=1, tiled=True),
    )
    norm_one, in_full, conv_full, out_full, norm_two, gate_full, up_full, down_full = gathered
    channels = in_full.shape[2]
    channel_start = lax.axis_index("tensor") * channels
    tap_keep = tap_masks(doc_ids)
    conv_taps = lax.dynamic_slice_in_dim(conv_full, channel_start, channels, 1).astype(jnp.float32)
    inputs = tokens.astype(jnp.float32)
    inverse_one = lax.rsqrt(jnp.mean(inputs * inputs, axis=-1, keepdims=True) + epsilon)
    unit_one = inputs * inverse_one
    normed_local = (unit_one * norm_one.astype(jnp.float32)).astype(jnp.bfloat16)
    normed = lax.all_gather(normed_local, "tensor", axis=0, tiled=True)
    projected = jnp.einsum("td,dkc->tkc", normed, in_full, preferred_element_type=jnp.float32)
    input_gate = projected[:, 0]
    output_gate = projected[:, 1]
    values = projected[:, 2]
    mixed_input = input_gate * values
    convolved = sum(
        (
            tap_keep[offset][:, None] * conv_taps[offset][None, :] * shift_down(mixed_input, offset)
            for offset in range(KW)
        )
    )
    mixer_in = (output_gate * convolved).astype(jnp.bfloat16)
    mixer_out = lax.psum_scatter(
        jnp.dot(mixer_in, out_full, preferred_element_type=jnp.float32),
        "tensor",
        scatter_dimension=0,
        tiled=True,
    )
    hidden = inputs + mixer_out
    inverse_two = lax.rsqrt(jnp.mean(hidden * hidden, axis=-1, keepdims=True) + epsilon)
    unit_two = hidden * inverse_two
    normed_two_local = (unit_two * norm_two.astype(jnp.float32)).astype(jnp.bfloat16)
    normed_two = lax.all_gather(normed_two_local, "tensor", axis=0, tiled=True)
    gate_pre = jnp.dot(normed_two, gate_full, preferred_element_type=jnp.float32)
    upward = jnp.dot(normed_two, up_full, preferred_element_type=jnp.float32)
    activated = (jax.nn.silu(gate_pre) * upward).astype(jnp.bfloat16)
    feed_out = lax.psum_scatter(
        jnp.dot(activated, down_full, preferred_element_type=jnp.float32).astype(jnp.bfloat16),
        "tensor",
        scatter_dimension=0,
        tiled=True,
    ).astype(jnp.float32)
    output = (hidden + feed_out).astype(jnp.bfloat16)
    regathered = (
        lax.all_gather(mixer_norm, "dp", axis=0, tiled=True),
        lax.all_gather(in_weight, "dp", axis=0, tiled=True),
        lax.all_gather(conv_weight, "dp", axis=1, tiled=True),
        lax.all_gather(out_weight, "dp", axis=1, tiled=True),
        lax.all_gather(feed_norm, "dp", axis=0, tiled=True),
        lax.all_gather(gate_weight, "dp", axis=0, tiled=True),
        lax.all_gather(up_weight, "dp", axis=0, tiled=True),
        lax.all_gather(down_weight, "dp", axis=1, tiled=True),
    )
    norm_one_b, in_again, conv_again, out_again, norm_two_b, gate_again, up_again, down_again = (
        regathered
    )
    gain_one = norm_one_b.astype(jnp.float32)
    gain_two = norm_two_b.astype(jnp.float32)
    taps_again = lax.dynamic_slice_in_dim(conv_again, channel_start, channels, 1).astype(
        jnp.float32
    )
    sigmoid = jax.nn.sigmoid(gate_pre)
    cotangent = lax.all_gather(out_grad, "tensor", axis=0, tiled=True)
    down_grad = jnp.einsum("tf,td->fd", activated, cotangent, preferred_element_type=jnp.float32)
    grad_act = jnp.einsum("td,fd->tf", cotangent, down_again, preferred_element_type=jnp.float32)
    grad_gate = (grad_act * upward * sigmoid * (1.0 + gate_pre * (1.0 - sigmoid))).astype(
        jnp.bfloat16
    )
    grad_up = (grad_act * gate_pre * sigmoid).astype(jnp.bfloat16)
    gate_grad = jnp.einsum("td,tf->df", normed_two, grad_gate, preferred_element_type=jnp.float32)
    up_grad = jnp.einsum("td,tf->df", normed_two, grad_up, preferred_element_type=jnp.float32)
    grad_two = lax.psum_scatter(
        (
            jnp.einsum("tf,df->td", grad_gate, gate_again, preferred_element_type=jnp.float32)
            + jnp.einsum("tf,df->td", grad_up, up_again, preferred_element_type=jnp.float32)
        ).astype(jnp.bfloat16),
        "tensor",
        scatter_dimension=0,
        tiled=True,
    ).astype(jnp.float32)
    feed_gain_part = jnp.sum(grad_two * unit_two, axis=0)
    grad_hidden = out_grad.astype(jnp.float32) + norm_back(
        grad_two, unit_two, inverse_two, gain_two
    )
    grad_mix_local = grad_hidden.astype(jnp.bfloat16)
    grad_mix = lax.all_gather(grad_mix_local, "tensor", axis=0, tiled=True)
    out_grad_part = jnp.einsum("tc,td->cd", mixer_in, grad_mix, preferred_element_type=jnp.float32)
    grad_in = jnp.einsum("td,cd->tc", grad_mix, out_again, preferred_element_type=jnp.float32)
    grad_c = grad_in * convolved
    grad_conv = grad_in * output_gate
    grad_mixed = sum(
        (
            taps_again[offset][None, :] * shift_up(tap_keep[offset][:, None] * grad_conv, offset)
            for offset in range(KW)
        )
    )
    tap_grad = jnp.stack(
        [
            jnp.sum(tap_keep[offset][:, None] * grad_conv * shift_down(mixed_input, offset), axis=0)
            for offset in range(KW)
        ]
    )
    grad_projected = jnp.stack(
        [grad_mixed * values, grad_c, grad_mixed * input_gate], axis=1
    ).astype(jnp.bfloat16)
    in_grad_part = jnp.einsum(
        "td,tkc->dkc", normed, grad_projected, preferred_element_type=jnp.float32
    )
    grad_one = lax.psum_scatter(
        jnp.einsum(
            "tkc,dkc->td", grad_projected, in_again, preferred_element_type=jnp.float32
        ).astype(jnp.bfloat16),
        "tensor",
        scatter_dimension=0,
        tiled=True,
    ).astype(jnp.float32)
    mixer_gain_part = jnp.sum(grad_one * unit_one, axis=0)
    input_grad = (grad_hidden + norm_back(grad_one, unit_one, inverse_one, gain_one)).astype(
        jnp.bfloat16
    )
    conv_part = lax.dynamic_update_slice_in_dim(
        jnp.zeros((KW, model_width), jnp.float32), tap_grad, channel_start, 1
    )
    summed = (
        lax.psum_scatter(mixer_gain_part, "dp", scatter_dimension=0, tiled=True),
        lax.psum_scatter(in_grad_part, "dp", scatter_dimension=0, tiled=True),
        lax.psum_scatter(conv_part, "dp", scatter_dimension=1, tiled=True),
        lax.psum_scatter(out_grad_part, "dp", scatter_dimension=1, tiled=True),
        lax.psum_scatter(feed_gain_part, "dp", scatter_dimension=0, tiled=True),
        lax.psum_scatter(gate_grad, "dp", scatter_dimension=0, tiled=True),
        lax.psum_scatter(up_grad, "dp", scatter_dimension=0, tiled=True),
        lax.psum_scatter(down_grad, "dp", scatter_dimension=1, tiled=True),
    )
    (
        mixer_gain_sum,
        in_weight_grad,
        conv_sum,
        out_weight_grad,
        feed_gain_sum,
        gate_weight_grad,
        up_weight_grad,
        down_weight_grad,
    ) = summed
    mixer_norm_grad, conv_weight_grad, feed_norm_grad = lax.psum(
        (mixer_gain_sum, conv_sum, feed_gain_sum), "tensor"
    )
    return (
        output,
        input_grad,
        mixer_norm_grad,
        in_weight_grad,
        conv_weight_grad,
        out_weight_grad,
        feed_norm_grad,
        gate_weight_grad,
        up_weight_grad,
        down_weight_grad,
    )


def solution(mesh):
    in_specs = (
        P(("dp", "tensor"), None),
        P("dp", None),
        P("dp"),
        P("dp", None, "tensor"),
        P(None, "dp"),
        P("tensor", "dp"),
        P("dp"),
        P("dp", "tensor"),
        P("dp", "tensor"),
        P("tensor", "dp"),
        P(("dp", "tensor"), None),
    )
    out_specs = (
        P(("dp", "tensor"), None),
        P(("dp", "tensor"), None),
        P("dp"),
        P("dp", None, "tensor"),
        P(None, "dp"),
        P("tensor", "dp"),
        P("dp"),
        P("dp", "tensor"),
        P("dp", "tensor"),
        P("tensor", "dp"),
    )
    n_dp = mesh.shape["dp"]
    fits = n_dp == 2 * NZ and mesh.shape["tensor"] == 4
    step = functools.partial(block, n_dp) if fits else body
    return jax.shard_map(step, mesh=mesh, in_specs=in_specs, out_specs=out_specs, check_vma=False)
```

```python
import functools

import jax
import jax.numpy as jnp
from jax import lax
from jax.experimental import pallas as pl
from jax.experimental.pallas import tpu as pltpu
from jax.sharding import PartitionSpec as P

KW = 3
MESH = pl.DeviceIdType.MESH
BF = jnp.bfloat16
F32 = jnp.float32

epsilon = 1e-05

NZ = 4
CONV = 4
FEED = 3
Y_LAST = (True, False, True, False)
X_FIRST = (False, True, False)
Y_FIRST = (True, True, True, True)


def nn(a, b):
    return lax.dot_general(a, b, (((1,), (0,)), ((), ())), preferred_element_type=F32)


def nt(a, b):
    return lax.dot_general(a, b, (((1,), (1,)), ((), ())), preferred_element_type=F32)


def tn(a, b):
    return lax.dot_general(a, b, (((0,), (0,)), ((), ())), preferred_element_type=F32)


class Place:
    def __init__(self):
        self.dp = lax.axis_index("dp")
        self.t = lax.axis_index("tensor")
        self.z, self.x = lax.div(self.dp, 2), lax.rem(self.dp, 2)
        self.y, self.c = lax.div(self.t, 2), lax.rem(self.t, 2)
        self.over_x = (self.z * 2 + 1 - self.x, self.t)
        self.over_y = (self.dp, (1 - self.y) * 2 + self.c)
        self.over_c = (self.dp, self.y * 2 + 1 - self.c)
        self.t_y = (1 - self.y) * 2 + self.c
        self.t_c = self.y * 2 + 1 - self.c
        self.t_yc = (1 - self.y) * 2 + 1 - self.c
        self.middle = lax.rem(lax.div(self.z + 1, 2), 2) == 1

    def zs(self, k):
        if k == 0:
            return self.z
        if k == 1:
            return self.z + 1 - 2 * lax.rem(self.z, 2)
        if k == 2:
            return lax.rem(self.z + 2, NZ)
        return NZ - 1 - self.z

    def over_z(self, k):
        return (self.zs(k) * 2 + self.x, self.t)


def greet(place, n_dp):
    barrier = pltpu.get_barrier_semaphore()
    for k in range(1, n_dp):
        peer = (lax.rem(place.dp + k, n_dp), place.t)
        pl.semaphore_signal(barrier, inc=1, device_id=peer, device_id_type=MESH)
    for peer in (place.over_c, place.over_y):
        pl.semaphore_signal(barrier, inc=1, device_id=peer, device_id_type=MESH)
    pl.semaphore_wait(barrier, n_dp + 1)


def remote(src, dst, send_sem, recv_sem, peer):
    return pltpu.make_async_remote_copy(
        src_ref=src, dst_ref=dst, send_sem=send_sem, recv_sem=recv_sem, device_id=peer, device_id_type=MESH
    )


def send(*what):
    copy = remote(*what)
    copy.start()
    return copy


def arrived(ref, sem, peer):
    pltpu.make_async_remote_copy(
        src_ref=ref, dst_ref=ref, send_sem=sem, recv_sem=sem, device_id=peer, device_id_type=MESH
    ).wait_recv()


def rows(start, size):
    return pl.ds(pl.multiple_of(start, size), size)


def forward_kernel(
    n_dp,
    tokens, cotangent, keep, small, in_own, out_own, gate_own, up_own, down_own,
    conv_out, feed_out, normed_out, small_out, cot_out, proj_out, mixer_out, hidden_out, two_out, acts_out,
    conv_w, feed_w, normed, small_all, mixed_pad, c_keep, proj, mixer_in, part_send, part_recv,
    hidden, two, acts, out_turned, down_turned,
    own_sem, z_send, z_recv, x_send, x_recv, y_send, y_recv, fz_send, fz_recv, fx_send, fx_recv,
    s_send, s_recv, a_send, a_recv, out_sem,
):
    place = Place()
    z, x, y, c, t = place.z, place.x, place.y, place.c, place.t
    depth = gate_own.shape[0]
    local, width = tokens.shape
    chip = 2 * local
    half = in_own.shape[2]
    mine = 2 * half
    tile, pad = 256, 8
    blocks = (t, place.t_c, place.t_y, place.t_yc)
    sends = []
    copies = []
    owned = {}

    def post(make, when=None):
        if when is None:
            make().start()
        else:
            pl.when(when)(lambda: make().start())
        sends.append((make, when))

    def keep_own(src, dst, index):
        owned[index] = pltpu.make_async_copy(src, dst, own_sem.at[index])
        owned[index].start()

    def out(src, dst):
        copy = pltpu.make_async_copy(src, dst, out_sem.at[len(copies)])
        copy.start()
        copies.append(copy)

    def conv_part(j, dp, n, side):
        col = slice(None) if side is None else rows(side * half, half)
        return conv_w.at[j, rows(dp * depth, n * depth), col]

    def feed_part(w, dp, n=1):
        return feed_w.at[w, rows(dp * depth, n * depth), :]

    conv_own = [in_own.at[0], in_own.at[1], in_own.at[2], out_turned]
    feed_own = [gate_own, up_own, down_turned]

    def along_z(src, part, send_sems, recv_sems, index):
        for k in (2, 3, 1):
            post(lambda k=k: remote(src, part(z), send_sems.at[index, k], recv_sems.at[index, z], place.over_z(k)),
                 place.middle if k == 3 else None)

    def from_z(part, send_sems, recv_sems, index, k):
        zk = place.zs(k)
        arrived(part(zk), recv_sems.at[index, zk], place.over_z(k))
        if k == 2:
            post(lambda: remote(part(zk), part(zk), send_sems.at[index, 0], recv_sems.at[index, zk], place.over_z(1)), place.middle)

    def conv_z(j):
        return lambda zk: conv_part(j, zk * 2 + x, 1, y)

    def feed_z(w):
        if X_FIRST[w]:
            return lambda zk: feed_part(w, zk * 2, 2)
        return lambda zk: feed_part(w, zk * 2 + x)

    def conv_second(j, k, src=None):
        zk = place.zs(k)
        part = conv_part(j, zk * 2 + x, 1, y)
        src = part if src is None else src
        if Y_LAST[j]:
            post(lambda: remote(src, part, x_send.at[j, zk], x_recv.at[j, zk], place.over_x))
        else:
            post(lambda: remote(src, part, y_send.at[j, zk], y_recv.at[j, zk], place.over_y))

    def feed_x(w, k, src=None):
        zk = place.zs(k)
        part = feed_part(w, zk * 2 + x)
        src = part if src is None else src
        post(lambda: remote(src, part, fx_send.at[w, zk], fx_recv.at[w, zk], place.over_x))

    def cown(j):
        along_z(conv_own[j], conv_z(j), z_send, z_recv, j)
        conv_second(j, 0, conv_own[j])

    def cz(j, k):
        from_z(conv_z(j), z_send, z_recv, j, k)
        conv_second(j, k)

    def ct(j, k):
        zk = place.zs(k)
        if k == 0:
            owned[j].wait()
        if Y_LAST[j]:
            arrived(conv_part(j, zk * 2 + 1 - x, 1, y), x_recv.at[j, zk], place.over_x)
            pair = conv_part(j, zk * 2, 2, y)
            post(lambda: remote(pair, pair, y_send.at[j, zk], y_recv.at[j, zk], place.over_y))
        else:
            arrived(conv_part(j, zk * 2 + x, 1, 1 - y), y_recv.at[j, zk], place.over_y)
            pair = conv_part(j, zk * 2 + x, 1, None)
            post(lambda: remote(pair, pair, x_send.at[j, zk], x_recv.at[j, zk], place.over_x))

    def fx(w):
        feed_x(w, 0, feed_own[w])

    def fz(w):
        if X_FIRST[w]:
            arrived(feed_part(w, z * 2 + 1 - x), fx_recv.at[w, z], place.over_x)
            owned[CONV + w].wait()
            along_z(feed_part(w, z * 2, 2), feed_z(w), fz_send, fz_recv, w)
        else:
            along_z(feed_own[w], feed_z(w), fz_send, fz_recv, w)

    def fp(w, k):
        from_z(feed_z(w), fz_send, fz_recv, w, k)
        if not X_FIRST[w]:
            feed_x(w, k)

    def feed_ready(w):
        if not X_FIRST[w]:
            for k in range(NZ):
                zk = place.zs(k)
                arrived(feed_part(w, zk * 2 + 1 - x), fx_recv.at[w, zk], place.over_x)
            owned[CONV + w].wait()
        out(feed_w.at[w], feed_out.at[w])

    def cot_block(block):
        return cot_out.at[rows(block * local, local), :]

    def cotc():
        post(lambda: remote(cotangent, cot_block(t), a_send.at[0], a_recv.at[0], place.over_c))

    def coty():
        post(lambda: remote(cotangent, cot_block(t), a_send.at[2], a_recv.at[2], place.over_y))

    def cotf():
        there = cot_block(place.t_y)
        arrived(there, a_recv.at[2], place.over_y)
        post(lambda: remote(there, there, a_send.at[6], a_recv.at[6], place.over_c))

    def turn():
        down_turned[...] = jnp.transpose(down_own[...])
        for w in range(FEED):
            keep_own(feed_own[w], feed_part(w, place.dp), CONV + w)

    def gain(r):
        return jnp.concatenate([small_all[d, r : r + 1, :] for d in range(n_dp)], axis=1)

    def norm():
        for k in range(1, n_dp):
            peer = lax.rem(place.dp + k, n_dp)
            arrived(small_all.at[peer], s_recv.at[peer], (peer, t))
        inputs = tokens[...].astype(F32)
        inverse = lax.rsqrt(jnp.mean(inputs * inputs, axis=-1, keepdims=True) + epsilon)
        normed[rows(c * local, local), :] = (inputs * inverse * gain(0)).astype(BF)
        own = normed.at[rows(c * local, local), :]
        post(lambda: remote(own, own, a_send.at[1], a_recv.at[1], place.over_c))

    def p1():
        arrived(normed.at[rows((1 - c) * local, local), :], a_recv.at[1], place.over_c)
        for j in range(CONV):
            for k in range(NZ):
                zk = place.zs(k)
                if Y_LAST[j]:
                    arrived(conv_part(j, zk * 2, 2, 1 - y), y_recv.at[j, zk], place.over_y)
                else:
                    arrived(conv_part(j, zk * 2 + 1 - x, 1, None), x_recv.at[j, zk], place.over_x)
        out(conv_w, conv_out)
        out(normed, normed_out)
        mixed_pad[0:pad, :] = jnp.zeros((pad, mine), F32)

        def project(i, carry):
            at = rows(i * tile, tile)
            lhs = normed[at, :]
            b = nn(lhs, conv_w[0])
            proj[0, at, :] = b.astype(BF)
            v = nn(lhs, conv_w[2])
            proj[2, at, :] = v.astype(BF)
            mixed_pad[pl.ds(pl.multiple_of(i * tile + pad, 8), tile), :] = b * v
            g = nn(lhs, conv_w[1])
            proj[1, at, :] = g.astype(BF)
            c_keep[at, :] = g
            return carry

        lax.fori_loop(0, chip // tile, project, 0)

    def p2():
        taps = []
        for r in range(2, 2 + KW):
            taps.append(jnp.concatenate(
                [small_all[side * 4 + 2 * c + i, r : r + 1, :] for side in range(2) for i in range(2)], axis=1))

        def convolve(i, carry):
            at = rows(i * tile, tile)
            window = mixed_pad[pl.ds(pl.multiple_of(i * tile, 8), tile + pad), :]
            total = taps[0] * window[pad:, :]
            for k in range(1, KW):
                mask = jnp.concatenate([keep[k - 1, at, :]] * (mine // 128), axis=1)
                total = total + mask * taps[k] * window[pad - k : pad - k + tile, :]
            proj[3, at, :] = total.astype(BF)
            mixer_in[at, :] = (c_keep[at, :] * total).astype(BF)
            return carry

        lax.fori_loop(0, chip // tile, convolve, 0)
        out(proj, proj_out)
        out(mixer_in, mixer_out)
        part_send[...] = nt(mixer_in[rows((1 - c) * local, local), :], conv_w[3]).astype(BF)
        post(lambda: remote(part_send, part_recv, a_send.at[3], a_recv.at[3], place.over_c))
        hidden[...] = tokens[...].astype(F32) + nt(mixer_in[rows(c * local, local), :], conv_w[3])

    def p3():
        arrived(part_recv, a_recv.at[3], place.over_c)
        total = hidden[...] + part_recv[...].astype(F32)
        hidden[...] = total
        inverse = lax.rsqrt(jnp.mean(total * total, axis=-1, keepdims=True) + epsilon)
        two[rows(t * local, local), :] = (total * inverse * gain(1)).astype(BF)
        own = two.at[rows(t * local, local), :]
        post(lambda: remote(own, own, a_send.at[5], a_recv.at[5], place.over_y))
        post(lambda: remote(own, own, a_send.at[4], a_recv.at[4], place.over_c))
        out(hidden, hidden_out)

    def t2():
        there = two.at[rows(place.t_y * local, local), :]
        arrived(there, a_recv.at[5], place.over_y)
        post(lambda: remote(there, there, a_send.at[7], a_recv.at[7], place.over_c))

    def g(b):
        if b == 0:
            feed_ready(0)
        if b == 1:
            arrived(two.at[rows(place.t_c * local, local), :], a_recv.at[4], place.over_c)
        if b == 3:
            arrived(two.at[rows(place.t_yc * local, local), :], a_recv.at[7], place.over_c)

        def step(i, carry):
            at = rows(blocks[b] * local + i * tile, tile)
            gate = nn(two[at, :], feed_w[0])
            s = jax.nn.sigmoid(gate)
            silu = gate * s
            acts[1, at, :] = (s + silu * (1.0 - s)).astype(BF)
            acts[2, at, :] = silu.astype(BF)
            return carry

        lax.fori_loop(0, local // tile, step, 0)

    def u(b):
        if b == 0:
            feed_ready(1)

        def step(i, carry):
            at = rows(blocks[b] * local + i * tile, tile)
            upward = nn(two[at, :], feed_w[1])
            acts[0, at, :] = (acts[2, at, :].astype(F32) * upward).astype(BF)
            acts[1, at, :] = (acts[1, at, :].astype(F32) * upward).astype(BF)
            return carry

        lax.fori_loop(0, local // tile, step, 0)
        at = rows(blocks[b] * local, local)
        out(acts.at[:, at, :], acts_out.at[:, at, :])
        out(two.at[at, :], two_out.at[at, :])

    small_all[place.dp] = small[...]
    out_turned[...] = jnp.transpose(out_own[...])
    greet(place, n_dp)
    for k in range(1, n_dp):
        post(lambda k=k: remote(small, small_all.at[place.dp], s_send.at[k], s_recv.at[place.dp], (lax.rem(place.dp + k, n_dp), t)))
    for j in range(CONV):
        keep_own(conv_own[j], conv_part(j, place.dp, 1, y), j)
    keep_own(cotangent, cot_block(t), CONV + FEED)
    cown(2)
    cotc()
    cown(0)
    ct(2, 0)
    cown(3)
    ct(0, 0)
    cz(2, 2)
    cz(0, 2)
    cown(1)
    ct(3, 0)
    turn()
    cz(3, 2)
    cz(0, 3)
    fx(1)
    cz(3, 1)
    cz(2, 1)
    cz(0, 1)
    ct(0, 2)
    norm()
    fz(0)
    cz(1, 2)
    fz(2)
    ct(0, 3)
    cz(1, 1)
    fz(1)
    ct(1, 2)
    cz(3, 3)
    ct(3, 2)
    ct(2, 1)
    ct(2, 2)
    cz(2, 3)
    ct(3, 3)
    cz(1, 3)
    ct(3, 1)
    ct(1, 0)
    ct(1, 3)
    ct(1, 1)
    fp(0, 2)
    ct(2, 3)
    ct(0, 1)
    coty()
    p1()
    fx(2)
    fx(0)
    fp(2, 2)
    fp(0, 1)
    p2()
    p3()
    fp(0, 3)
    fp(1, 2)
    fp(2, 1)
    g(0)
    t2()
    g(2)
    g(1)
    fp(2, 3)
    cotf()
    g(3)
    fp(1, 1)
    fp(1, 3)
    u(0)
    u(1)
    u(2)
    u(3)
    feed_ready(2)
    small_out[...] = small_all[...]
    arrived(cot_block(place.t_c), a_recv.at[0], place.over_c)
    arrived(cot_block(place.t_yc), a_recv.at[6], place.over_c)
    owned[CONV + FEED].wait()
    for make, when in sends:
        if when is None:
            make().wait_send()
        else:
            pl.when(when)(lambda make=make: make().wait_send())
    for copy in copies:
        copy.wait()


def forward_call(n_dp, *operands):
    tokens, _, _, _, in_own, _, gate_own, _, _ = operands
    local, width = tokens.shape
    half, units = in_own.shape[2], gate_own.shape[1]
    chip, group, mine = 2 * local, 4 * local, 2 * half

    def shaped(dims, kind=BF):
        return jax.ShapeDtypeStruct(dims, kind)

    dma = pltpu.SemaphoreType.DMA
    vmem, any_space = pl.BlockSpec(memory_space=pltpu.VMEM), pl.BlockSpec(memory_space=pl.ANY)
    return pl.pallas_call(
        functools.partial(forward_kernel, n_dp),
        name="gather_forward",
        out_shape=(
            shaped((CONV, width, mine)), shaped((FEED, width, units)), shaped((chip, width)), shaped((n_dp, 8, 128), F32),
            shaped((group, width)), shaped((4, chip, mine)), shaped((chip, mine)), shaped((local, width), F32),
            shaped((group, width)), shaped((3, group, units)),
        ),
        in_specs=[vmem] * 4 + [any_space, vmem, any_space, any_space, vmem],
        out_specs=tuple(vmem if i == 3 else any_space for i in range(10)),
        scratch_shapes=[
            pltpu.VMEM((CONV, width, mine), BF), pltpu.VMEM((FEED, width, units), BF), pltpu.VMEM((chip, width), BF),
            pltpu.VMEM((n_dp, 8, 128), F32), pltpu.VMEM((chip + 8, mine), F32),
            pltpu.VMEM((chip, mine), F32), pltpu.VMEM((4, chip, mine), BF), pltpu.VMEM((chip, mine), BF),
            pltpu.VMEM((local, width), BF), pltpu.VMEM((local, width), BF), pltpu.VMEM((local, width), F32),
            pltpu.VMEM((group, width), BF), pltpu.VMEM((3, group, units), BF),
            pltpu.VMEM((width // n_dp, half), BF), pltpu.VMEM((width // n_dp, units), BF),
            dma((8,)), dma((CONV, NZ)), dma((CONV, NZ)), dma((CONV, NZ)), dma((CONV, NZ)), dma((CONV, NZ)), dma((CONV, NZ)),
            dma((FEED, NZ)), dma((FEED, NZ)), dma((FEED, NZ)), dma((FEED, NZ)),
            dma((n_dp,)), dma((n_dp,)), dma((8,)), dma((8,)), dma((16,)),
        ],
        compiler_params=pltpu.CompilerParams(collective_id=0, has_side_effects=True, vmem_limit_bytes=62 << 20),
    )(*operands)


def backward_kernel(
    n_dp,
    small_all, tokens_in, cot_own_in, keep_in, conv_in, feed_in, normed_in, cot_in, proj_in, mixer_in_hbm, hidden_in, two_in, acts_in,
    output, input_grad, in_grad, out_grad, gate_grad, up_grad, down_grad, small_grad,
    act, g_down, x_got, z_got, c_got_y, c_got_x, c_two, c_z, two_send, two_recv, two_y, own_two,
    down_send, down_recv, down_y, down_own, grad_mix, feed_gain, small_sum, small_got, small_z,
    load_sem, fx_send, fx_recv, fz_send, fz_recv, c1_send, c1_recv, c2_send, c2_recv, c3_send, c3_recv,
    s_send, s_recv, a_send, a_recv,
):
    place = Place()
    z, x, y, c, t = place.z, place.x, place.y, place.c, place.t
    depth, units = gate_grad.shape
    local, width = own_two.shape
    chip = 2 * local
    half = in_grad.shape[2]
    mine = 2 * half
    tile = 256
    sends = []

    def post(make):
        make().start()
        sends.append(make)
        return make

    def load(src, dst, index):
        copy = pltpu.make_async_copy(src, dst, load_sem.at[index])
        copy.start()
        return copy

    def g_rows(w, start, size):
        if w == 2:
            return g_down.at[rows(start, size), :]
        return act.at[rows(w * width + start, size), :]

    def m(w, k):
        zk = place.zs(k)
        got = x_got.at[w, zk]
        arrived(got, fx_recv.at[w, zk], place.over_x)
        if k:
            got[...] = (g_rows(w, (zk * 2 + x) * depth, depth)[...].astype(F32) + got[...].astype(F32)).astype(BF)

            def add(more):
                held = x_got.at[w, place.zs(k)]
                held[...] = (held[...].astype(F32) + more[...].astype(F32)).astype(BF)

            if k == 2:
                @pl.when(place.middle)
                def _():
                    arrived(z_got.at[w, 0], fz_recv.at[w, 0], place.over_z(1))
                    add(z_got.at[w, 0])

            post(lambda: z_remote(x_got.at[w, place.zs(k)], z_got.at[w], fz_send.at[w], fz_recv.at[w], k))

    def z_remote(held, got, sends_at, recvs_at, k):
        if k == 3:
            slot = jnp.where(place.middle, 3, 0)
            peer = (jnp.where(place.middle, place.zs(3), place.zs(1)) * 2 + x, t)
            return remote(held, got.at[slot], sends_at.at[k], recvs_at.at[slot], peer)
        return remote(held, got.at[k], sends_at.at[k], recvs_at.at[k], place.over_z(k))

    def z_sum(total, got, recvs_at):
        for k in (1, 2):
            arrived(got.at[k], recvs_at.at[k], place.over_z(k))
            total = total + got[k].astype(F32)
        return total

    def z_last(ref, got, recvs_at):
        @pl.when(place.middle)
        def _():
            arrived(got.at[3], recvs_at.at[3], place.over_z(3))
            ref[...] = ref[...] + got[3].astype(F32)

    def gain(r):
        return jnp.concatenate([small_all[d, r : r + 1, :] for d in range(n_dp)], axis=1)

    def norm_back(grad, unit, inverse, scale):
        scaled = grad * scale
        return inverse * (scaled - unit * jnp.mean(scaled * unit, axis=-1, keepdims=True))

    def rms(values):
        return lax.rsqrt(jnp.mean(values * values, axis=-1, keepdims=True) + epsilon)

    def send_slot(i):
        return lambda: remote(two_send.at[i], two_recv.at[i], a_send.at[1 + i], a_recv.at[1 + i], place.over_c)

    first_slot = send_slot(0)

    def feed_phase(feed_w, cot, acts):
        loads = [load(acts_in.at[0], act, 0), load(cot_in, cot, 1), load(feed_in, feed_w, 2),
                 load(acts_in.at[1], acts.at[0], 3), load(acts_in.at[2], acts.at[1], 4)]
        greet(place, n_dp)
        waited = set()

        def loaded(*which):
            for i in which:
                if i not in waited:
                    waited.add(i)
                    loads[i].wait()

        def g(w, k):
            at = rows(place.zs(k) * 2 * depth, 2 * depth)
            if w == 2:
                loaded(0, 1)
                g_down[at, :] = tn(cot[:, at], act[...]).astype(BF)
            else:
                if 5 not in waited:
                    loads.append(load(two_in, cot, 5))
                    loaded(5)
                act[rows(w * width + place.zs(k) * 2 * depth, 2 * depth), :] = tn(cot[:, at], acts[w]).astype(BF)

            def make():
                zk = place.zs(k)
                return remote(g_rows(w, (zk * 2 + 1 - x) * depth, depth), x_got.at[w, zk], fx_send.at[w, zk], fx_recv.at[w, zk], place.over_x)

            post(make)

        def back(block, store):
            loaded(1, 2, 3, 4)

            def step(i, carry):
                at = rows(block * local + i * tile, tile)
                grad_act = nn(cot[at, :], feed_w[2])
                grad_gate = (grad_act * acts[0, at, :].astype(F32)).astype(BF)
                acts[0, at, :] = grad_gate
                grad_up = (grad_act * acts[1, at, :].astype(F32)).astype(BF)
                acts[1, at, :] = grad_up
                store(rows(i * tile, tile), nt(grad_gate, feed_w[0]) + nt(grad_up, feed_w[1]))
                return carry

            lax.fori_loop(0, local // tile, step, 0)

        def to_slot(i):
            def store(at, value):
                two_send[i, at, :] = value.astype(BF)

            return store

        def to_own(at, value):
            own_two[at, :] = value

        def a_yc():
            back(place.t_yc, to_slot(0))
            post(first_slot)

        def a_c():
            back(place.t_c, to_slot(1))
            post(send_slot(1))

        def a_y():
            back(place.t_y, to_own)

        def ay():
            arrived(two_recv.at[0], a_recv.at[1], place.over_c)
            two_recv[0] = (own_two[...] + two_recv[0].astype(F32)).astype(BF)
            post(lambda: remote(two_recv.at[0], two_y, a_send.at[3], a_recv.at[3], place.over_y))

        def a_o():
            back(t, to_own)

        def down(block):
            loaded(0, 2)
            return nt(act[rows(block * local, local), :], feed_w[2]).astype(BF)

        def d_yc():
            down_send[0] = down(place.t_yc)
            post(lambda: remote(down_send.at[0], down_recv.at[0], a_send.at[6], a_recv.at[6], place.over_c))

        def d_c():
            down_send[1] = down(place.t_c)
            post(lambda: remote(down_send.at[1], down_recv.at[1], a_send.at[7], a_recv.at[7], place.over_c))

        def d_y():
            down_own[...] = down(place.t_y)

        def dy():
            arrived(down_recv.at[0], a_recv.at[6], place.over_c)
            down_recv[0] = (down_own[...].astype(F32) + down_recv[0].astype(F32)).astype(BF)
            post(lambda: remote(down_recv.at[0], down_y, a_send.at[8], a_recv.at[8], place.over_y))

        def d_o():
            down_own[...] = down(t)

        g(2, 0)
        g(2, 3)
        a_yc()
        a_y()
        ay()
        d_yc()
        m(2, 0)
        d_y()
        g(2, 1)
        m(2, 3)
        d_c()
        g(2, 2)
        a_o()
        a_c()
        m(2, 1)
        dy()
        d_o()
        g(0, 3)
        m(2, 2)
        g(1, 3)
        g(0, 1)
        g(0, 2)
        g(1, 2)
        g(1, 0)
        g(1, 1)
        g(0, 0)

    pl.run_scoped(
        feed_phase,
        pltpu.VMEM((FEED, width, units), BF), pltpu.VMEM((4 * local, width), BF), pltpu.VMEM((2, 4 * local, units), BF),
    )

    def conv_phase(conv_w, proj, normed, mixer_in, grad_proj, pad_grad, tap_sum, g_conv, token_rows, keep, hidden, stage):
        loads = [load(hidden_in, hidden, 0), load(cot_own_in, token_rows, 1), load(conv_in.at[3], conv_w.at[3], 2), load(mixer_in_hbm, mixer_in, 3),
                 load(proj_in, proj, 4), load(normed_in, normed, 5), load(conv_in.at[pl.ds(0, 3)], conv_w.at[pl.ds(0, 3)], 6),
                 load(keep_in, keep, 7)]
        waited = set()

        def loaded(*which):
            for i in which:
                if i not in waited:
                    waited.add(i)
                    loads[i].wait()

        def n2():
            loaded(0, 1)
            arrived(two_y, a_recv.at[3], place.over_y)
            arrived(two_recv.at[1], a_recv.at[2], place.over_c)
            scale = gain(1)

            def step(i, carry):
                at = rows(i * 128, 128)
                grad_two = own_two[at, :] + two_recv[1, at, :].astype(F32) + two_y[at, :].astype(F32)
                values = hidden[at, :]
                inverse = rms(values)
                unit = values * inverse
                grad_hidden = token_rows[at, :].astype(F32) + norm_back(grad_two, unit, inverse, scale)
                hidden[at, :] = grad_hidden
                grad_mix[rows(c * local + i * 128, 128), :] = grad_hidden.astype(BF)
                return carry + jnp.sum(grad_two * unit, axis=0, keepdims=True)

            feed_gain[0:1, :] = lax.fori_loop(0, local // 128, step, jnp.zeros((1, width), F32))
            loads.append(load(tokens_in, token_rows, 8))

            def make():
                own = grad_mix.at[rows(c * local, local), :]
                return remote(own, own, a_send.at[4], a_recv.at[4], place.over_c)

            post(make)

        def taps():
            return [jnp.concatenate([small_all[side * 4 + 2 * c + i, r : r + 1, :] for side in range(2) for i in range(2)], axis=1)
                    for r in range(2, 2 + KW)]

        def gm():
            loaded(2, 4)
            arrived(grad_mix.at[rows((1 - c) * local, local), :], a_recv.at[4], place.over_c)
            pad_grad[pl.ds(chip, 8), :] = jnp.zeros((8, mine), F32)

            def step(i, carry):
                at = rows(i * tile, tile)
                grad_in = nn(grad_mix[at, :], conv_w[3])
                grad_proj[1, at, :] = (grad_in * proj[3, at, :].astype(F32)).astype(BF)
                pad_grad[at, :] = grad_in * proj[1, at, :].astype(F32)
                return carry

            lax.fori_loop(0, chip // tile, step, 0)

        def c1_slot(j, zk):
            if Y_FIRST[j]:
                return c_got_y.at[sum(Y_FIRST[:j]), zk]
            return c_got_x.at[j - sum(Y_FIRST[:j]), zk]

        def w(j):
            if j == 3:
                loaded(3)
                g_conv[j] = tn(grad_mix[...], mixer_in[...]).astype(BF)
            else:
                loaded(5)
                g_conv[j] = tn(normed[...], grad_proj[j]).astype(BF)
            for k in (2, 1, 3, 0):
                zk = place.zs(k)
                if Y_FIRST[j]:
                    src, peer = g_conv.at[j, rows(zk * 2 * depth, 2 * depth), rows((1 - y) * half, half)], place.over_y
                else:
                    src, peer = g_conv.at[j, rows((zk * 2 + 1 - x) * depth, depth), :], place.over_x
                post(lambda src=src, peer=peer, zk=zk: remote(src, c1_slot(j, zk), c1_send.at[j, zk], c1_recv.at[j, zk], peer))

        def h2():
            loaded(4, 7)
            tap = taps()
            tap_sum[...] = jnp.zeros_like(tap_sum)
            size = 128

            def step(i, carry):
                at = rows(i * size, size)
                wide = pl.ds(pl.multiple_of(i * size, 8), size + 8)
                window = pad_grad[wide, :]
                b, v = proj[0, at, :].astype(F32), proj[2, at, :].astype(F32)
                mixed = b * v
                now = window[:size, :]
                total = tap[0] * now
                tap_sum[0:1, :] += jnp.sum(now * mixed, axis=0, keepdims=True)
                for k in range(1, KW):
                    mask = jnp.concatenate([keep[k - 1, wide, :]] * (mine // 128), axis=1)
                    ahead = (mask * window)[k : k + size, :]
                    total = total + tap[k] * ahead
                    tap_sum[k : k + 1, :] += jnp.sum(ahead * mixed, axis=0, keepdims=True)
                grad_proj[0, at, :] = (total * v).astype(BF)
                grad_proj[2, at, :] = (total * b).astype(BF)
                return carry

            lax.fori_loop(0, chip // size, step, 0)

        def first_grad(block):
            at = rows(block * local, local)
            return nt(grad_proj[0, at, :], conv_w[0]) + nt(grad_proj[1, at, :], conv_w[1]) + nt(grad_proj[2, at, :], conv_w[2])

        def f1():
            loaded(6)
            first_slot().wait_send()
            sends.remove(first_slot)
            two_send[0] = first_grad(1 - c).astype(BF)
            post(lambda: remote(two_send.at[0], two_recv.at[1], a_send.at[5], a_recv.at[5], place.over_c))
            own_two[...] = first_grad(c)

        def n1():
            loaded(8)
            arrived(two_recv.at[1], a_recv.at[5], place.over_c)
            scale = gain(0)

            def step(i, carry):
                at = rows(i * 128, 128)
                grad_one = own_two[at, :] + two_recv[1, at, :].astype(F32)
                values = token_rows[at, :].astype(F32)
                inverse = rms(values)
                unit = values * inverse
                two_recv[1, at, :] = (hidden[at, :] + norm_back(grad_one, unit, inverse, scale)).astype(BF)
                return carry + jnp.sum(grad_one * unit, axis=0, keepdims=True)

            mixer_gain = lax.fori_loop(0, local // 128, step, jnp.zeros((1, width), F32))
            loads.append(load(two_recv.at[1], input_grad, 1))
            loads.append(load(hidden_in, own_two, 0))
            zero = jnp.zeros((1, 128), F32)
            for d in range(n_dp):
                cols = slice(d * 128, d * 128 + 128)
                here = (c == (d % 4) // 2).astype(F32)
                own = (d // 4) * half + (d % 2) * 128
                small_sum[d] = jnp.concatenate(
                    [mixer_gain[:, cols], feed_gain[0:1, cols]]
                    + [here * tap_sum[k : k + 1, own : own + 128] for k in range(KW)] + [zero] * 3, axis=0)

        def c2(j, k):
            zk = place.zs(k)
            got = c1_slot(j, zk)
            if Y_FIRST[j]:
                arrived(got, c1_recv.at[j, zk], place.over_y)
                held = g_conv[j, rows(zk * 2 * depth, 2 * depth), rows(y * half, half)]
                src, peer = got.at[rows((1 - x) * depth, depth), :], place.over_x
            else:
                arrived(got, c1_recv.at[j, zk], place.over_x)
                held = g_conv[j, rows((zk * 2 + x) * depth, depth), :]
                src, peer = got.at[:, rows((1 - y) * half, half)], place.over_y
            got[...] = (held.astype(F32) + got[...].astype(F32)).astype(BF)
            post(lambda: remote(src, c_two.at[j, zk], c2_send.at[j, zk], c2_recv.at[j, zk], peer))

        def held_half(j, zk):
            if Y_FIRST[j]:
                return c1_slot(j, zk)[rows(x * depth, depth), :].astype(F32)
            return c1_slot(j, zk)[:, rows(y * half, half)].astype(F32)

        def c3(j, k):
            zk = place.zs(k)
            got = c_two.at[j, zk]
            arrived(got, c2_recv.at[j, zk], place.over_x if Y_FIRST[j] else place.over_y)
            if k:
                got[...] = (held_half(j, zk) + got[...].astype(F32)).astype(BF)
                if k == 2:
                    @pl.when(place.middle)
                    def _():
                        arrived(c_z.at[j, 0], c3_recv.at[j, 0], place.over_z(1))
                        got[...] = (got[...].astype(F32) + c_z[j, 0].astype(F32)).astype(BF)

                post(lambda: z_remote(got, c_z.at[j], c3_send.at[j], c3_recv.at[j], k))

        def cf(j):
            total = z_sum(held_half(j, z) + c_two[j, z].astype(F32), c_z.at[j], c3_recv.at[j])
            if j == 3:
                stage[0:depth, 0:half] = total
                ref = stage.at[0:depth, 0:half]
                z_last(ref, c_z.at[j], c3_recv.at[j])
                out_grad[...] = jnp.transpose(ref[...])
            else:
                in_grad[j] = total
                z_last(in_grad.at[j], c_z.at[j], c3_recv.at[j])

        def ff(w):
            total = g_rows(w, (z * 2 + x) * depth, depth)[...].astype(F32) + x_got[w, z].astype(F32)
            total = z_sum(total, z_got.at[w], fz_recv.at[w])
            ref = (gate_grad, up_grad, stage)[w]
            ref[...] = total
            z_last(ref, z_got.at[w], fz_recv.at[w])
            if w == 2:
                down_grad[...] = jnp.transpose(stage[...])

        def do():
            loads[-1].wait()
            arrived(down_recv.at[1], a_recv.at[7], place.over_c)
            arrived(down_y, a_recv.at[8], place.over_y)
            total = own_two[...] + down_own[...].astype(F32) + down_recv[1].astype(F32) + down_y[...].astype(F32)
            down_own[...] = total.astype(BF)
            loads.append(load(down_own, output, 2))

        def s0():
            post(lambda: remote(small_sum, small_got.at[0], s_send.at[0], s_recv.at[0], place.over_c))

        def s1():
            arrived(small_got.at[0], s_recv.at[0], place.over_c)
            small_got[0] = small_sum[...] + small_got[0]
            post(lambda: remote(small_got.at[0], small_got.at[1], s_send.at[1], s_recv.at[1], place.over_y))

        def s2():
            arrived(small_got.at[1], s_recv.at[1], place.over_y)
            small_got[1] = small_got[0] + small_got[1]
            for k in range(NZ):
                zk = place.zs(k)
                post(lambda zk=zk, k=k: remote(
                    small_got.at[1, zk * 2 + 1 - x], small_z.at[zk], s_send.at[2 + k], s_recv.at[2 + zk], place.over_x))

        def s3():
            for k in range(NZ):
                zk = place.zs(k)
                arrived(small_z.at[zk], s_recv.at[2 + zk], place.over_x)
                small_z[zk] = small_z[zk] + small_got[1, zk * 2 + x]
                if k:
                    post(lambda zk=zk, k=k: remote(small_z.at[zk], small_z.at[NZ + k], s_send.at[6 + k], s_recv.at[6 + k], place.over_z(k)))

        def s4():
            total = small_z[z]
            for k in range(1, NZ):
                arrived(small_z.at[NZ + k], s_recv.at[6 + k], place.over_z(k))
                total = total + small_z[NZ + k]
            small_grad[...] = total

        n2()
        m(0, 3)
        m(1, 3)
        gm()
        w(1)
        m(0, 2)
        m(0, 1)
        h2()
        c2(1, 2)
        w(3)
        m(1, 2)
        w(2)
        f1()
        c2(3, 3)
        n1()
        m(1, 0)
        s0()
        c2(1, 3)
        c2(1, 1)
        m(1, 1)
        s1()
        c2(1, 0)
        c2(2, 1)
        c3(1, 3)
        c2(3, 2)
        w(0)
        c2(2, 2)
        c2(2, 0)
        c2(3, 1)
        c3(1, 2)
        s2()
        c2(2, 3)
        c3(3, 3)
        c3(1, 1)
        c3(3, 2)
        c2(0, 1)
        c3(3, 1)
        c3(2, 3)
        c2(0, 3)
        c2(3, 0)
        m(0, 0)
        do()
        s3()
        c3(2, 0)
        c3(0, 1)
        c2(0, 2)
        c3(0, 3)
        c3(2, 2)
        ff(0)
        c3(1, 0)
        c3(3, 0)
        cf(3)
        c2(0, 0)
        c3(2, 1)
        c3(0, 2)
        c3(0, 0)
        ff(1)
        cf(2)
        ff(2)
        cf(1)
        s4()
        cf(0)
        for make in sends:
            make().wait_send()
        loads[-3].wait()
        loads[-1].wait()

    pl.run_scoped(
        conv_phase,
        pltpu.VMEM((CONV, width, mine), BF), pltpu.VMEM((4, chip, mine), BF), pltpu.VMEM((chip, width), BF),
        pltpu.VMEM((chip, mine), BF), pltpu.VMEM((3, chip, mine), BF), pltpu.VMEM((chip + 8, mine), F32), pltpu.VMEM((8, mine), F32),
        pltpu.VMEM((CONV, width, mine), BF), pltpu.VMEM((local, width), BF),
        pltpu.VMEM((KW - 1, chip + 8, 128), F32), pltpu.VMEM((local, width), F32), pltpu.VMEM((depth, units), F32),
    )


def backward_call(n_dp, small_all, tokens, cotangent, keep, conv_w, feed_w, *rest):
    local, width = tokens.shape
    units, mine = feed_w.shape[2], conv_w.shape[2]
    chip, half, depth = 2 * local, mine // 2, width // n_dp
    over_y = sum(Y_FIRST)

    def shaped(dims, kind=BF):
        return jax.ShapeDtypeStruct(dims, kind)

    def slots(n, *dims):
        return pltpu.VMEM((max(n, 1), *(dims if n else (NZ, 16, 128))), BF)

    dma = pltpu.SemaphoreType.DMA
    vmem, any_space = pl.BlockSpec(memory_space=pltpu.VMEM), pl.BlockSpec(memory_space=pl.ANY)
    return pl.pallas_call(
        functools.partial(backward_kernel, n_dp),
        name="backward_scatter",
        out_shape=(
            shaped((local, width)), shaped((local, width)), shaped((3, depth, half), F32), shaped((half, depth), F32),
            shaped((depth, units), F32), shaped((depth, units), F32), shaped((units, depth), F32), shaped((8, 128), F32),
        ),
        in_specs=[vmem] + [any_space] * (5 + len(rest)),
        out_specs=(any_space,) * 2 + (vmem,) * 6,
        scratch_shapes=[
            pltpu.VMEM((4 * local, units), BF), pltpu.VMEM((width, units), BF), pltpu.VMEM((FEED, NZ, depth, units), BF),
            pltpu.VMEM((FEED, NZ, depth, units), BF),
            slots(over_y, NZ, 2 * depth, half), slots(CONV - over_y, NZ, depth, mine), pltpu.VMEM((CONV, NZ, depth, half), BF),
            pltpu.VMEM((CONV, NZ, depth, half), BF), pltpu.VMEM((2, local, width), BF), pltpu.VMEM((2, local, width), BF),
            pltpu.VMEM((local, width), BF), pltpu.VMEM((local, width), F32),
            pltpu.VMEM((2, local, width), BF), pltpu.VMEM((2, local, width), BF), pltpu.VMEM((local, width), BF),
            pltpu.VMEM((local, width), BF), pltpu.VMEM((chip, width), BF), pltpu.VMEM((8, width), F32), pltpu.VMEM((n_dp, 8, 128), F32),
            pltpu.VMEM((2, n_dp, 8, 128), F32), pltpu.VMEM((2 * NZ, 8, 128), F32),
            dma((9,)), dma((FEED, NZ)), dma((FEED, NZ)), dma((FEED, NZ)), dma((FEED, NZ)), dma((CONV, NZ)), dma((CONV, NZ)),
            dma((CONV, NZ)), dma((CONV, NZ)), dma((CONV, NZ)), dma((CONV, NZ)), dma((10,)), dma((10,)), dma((9,)), dma((9,)),
        ],
        compiler_params=pltpu.CompilerParams(collective_id=1, has_side_effects=True, vmem_limit_bytes=63 << 20),
    )(small_all, tokens, cotangent, keep, conv_w, feed_w, *rest)


def block(n_dp, tokens, doc_ids, mixer_norm, in_weight, conv_weight, out_weight, feed_norm, gate_weight, up_weight, down_weight, out_grad):
    chip = 2 * tokens.shape[0]
    documents = lax.dynamic_index_in_dim(doc_ids, lax.div(lax.axis_index("tensor"), 2), 0, keepdims=False)
    keep = []
    for offset in range(1, KW):
        same = jnp.concatenate([jnp.zeros((offset,), bool), documents[offset:] == documents[:-offset], jnp.zeros((8,), bool)])
        keep.append(jnp.broadcast_to(same.astype(F32)[:, None], (chip + 8, 128)))
    keep = jnp.stack(keep)
    small = jnp.concatenate(
        [mixer_norm[None], feed_norm[None], conv_weight, jnp.zeros((6 - KW, mixer_norm.shape[0]), BF)], axis=0).astype(F32)
    conv_w, feed_w, normed, small_all, cot, proj, mixer_in, hidden, two, acts = forward_call(
        n_dp, tokens, out_grad, keep, small, in_weight.transpose(1, 0, 2), out_weight, gate_weight, up_weight, down_weight)
    output, input_grad, in_g, out_g, gate_g, up_g, down_g, small_g = backward_call(
        n_dp, small_all, tokens, out_grad, keep, conv_w, feed_w, normed, cot, proj, mixer_in, hidden, two, acts)
    return (output, input_grad, small_g[0], in_g.transpose(1, 0, 2), small_g[2 : 2 + KW], out_g, small_g[1], gate_g, up_g, down_g)


def shift_down(values, offset):
    if offset == 0:
        return values
    padding = jnp.zeros((offset,) + values.shape[1:], values.dtype)
    return jnp.concatenate([padding, values[:-offset]], axis=0)


def shift_up(values, offset):
    if offset == 0:
        return values
    padding = jnp.zeros((offset,) + values.shape[1:], values.dtype)
    return jnp.concatenate([values[offset:], padding], axis=0)


def tap_masks(doc_rows):
    total_rows = doc_rows.shape[0] * doc_rows.shape[1]
    tap_keep = [jnp.ones((total_rows,), jnp.float32)]
    for offset in range(1, KW):
        matching = doc_rows[:, offset:] == doc_rows[:, :-offset]
        leading = jnp.zeros((doc_rows.shape[0], offset), dtype=bool)
        matching = jnp.concatenate([leading, matching], axis=1)
        tap_keep.append(jnp.where(matching, 1.0, 0.0).astype(jnp.float32).reshape(total_rows))
    return jnp.stack(tap_keep)


def norm_back(grad_out, unit_rows, inverse, gain):
    scaled = grad_out * gain
    return inverse * (scaled - unit_rows * jnp.mean(scaled * unit_rows, axis=-1, keepdims=True))


def body(
    tokens,
    doc_ids,
    mixer_norm,
    in_weight,
    conv_weight,
    out_weight,
    feed_norm,
    gate_weight,
    up_weight,
    down_weight,
    out_grad,
):
    model_width = tokens.shape[1]
    gathered = (
        lax.all_gather(mixer_norm, "dp", axis=0, tiled=True),
        lax.all_gather(in_weight, "dp", axis=0, tiled=True),
        lax.all_gather(conv_weight, "dp", axis=1, tiled=True),
        lax.all_gather(out_weight, "dp", axis=1, tiled=True),
        lax.all_gather(feed_norm, "dp", axis=0, tiled=True),
        lax.all_gather(gate_weight, "dp", axis=0, tiled=True),
        lax.all_gather(up_weight, "dp", axis=0, tiled=True),
        lax.all_gather(down_weight, "dp", axis=1, tiled=True),
    )
    norm_one, in_full, conv_full, out_full, norm_two, gate_full, up_full, down_full = gathered
    channels = in_full.shape[2]
    channel_start = lax.axis_index("tensor") * channels
    tap_keep = tap_masks(doc_ids)
    conv_taps = lax.dynamic_slice_in_dim(conv_full, channel_start, channels, 1).astype(jnp.float32)
    inputs = tokens.astype(jnp.float32)
    inverse_one = lax.rsqrt(jnp.mean(inputs * inputs, axis=-1, keepdims=True) + epsilon)
    unit_one = inputs * inverse_one
    normed_local = (unit_one * norm_one.astype(jnp.float32)).astype(jnp.bfloat16)
    normed = lax.all_gather(normed_local, "tensor", axis=0, tiled=True)
    projected = jnp.einsum("td,dkc->tkc", normed, in_full, preferred_element_type=jnp.float32)
    input_gate = projected[:, 0]
    output_gate = projected[:, 1]
    values = projected[:, 2]
    mixed_input = input_gate * values
    convolved = sum(
        (
            tap_keep[offset][:, None] * conv_taps[offset][None, :] * shift_down(mixed_input, offset)
            for offset in range(KW)
        )
    )
    mixer_in = (output_gate * convolved).astype(jnp.bfloat16)
    mixer_out = lax.psum_scatter(
        jnp.dot(mixer_in, out_full, preferred_element_type=jnp.float32),
        "tensor",
        scatter_dimension=0,
        tiled=True,
    )
    hidden = inputs + mixer_out
    inverse_two = lax.rsqrt(jnp.mean(hidden * hidden, axis=-1, keepdims=True) + epsilon)
    unit_two = hidden * inverse_two
    normed_two_local = (unit_two * norm_two.astype(jnp.float32)).astype(jnp.bfloat16)
    normed_two = lax.all_gather(normed_two_local, "tensor", axis=0, tiled=True)
    gate_pre = jnp.dot(normed_two, gate_full, preferred_element_type=jnp.float32)
    upward = jnp.dot(normed_two, up_full, preferred_element_type=jnp.float32)
    activated = (jax.nn.silu(gate_pre) * upward).astype(jnp.bfloat16)
    feed_out = lax.psum_scatter(
        jnp.dot(activated, down_full, preferred_element_type=jnp.float32).astype(jnp.bfloat16),
        "tensor",
        scatter_dimension=0,
        tiled=True,
    ).astype(jnp.float32)
    output = (hidden + feed_out).astype(jnp.bfloat16)
    regathered = (
        lax.all_gather(mixer_norm, "dp", axis=0, tiled=True),
        lax.all_gather(in_weight, "dp", axis=0, tiled=True),
        lax.all_gather(conv_weight, "dp", axis=1, tiled=True),
        lax.all_gather(out_weight, "dp", axis=1, tiled=True),
        lax.all_gather(feed_norm, "dp", axis=0, tiled=True),
        lax.all_gather(gate_weight, "dp", axis=0, tiled=True),
        lax.all_gather(up_weight, "dp", axis=0, tiled=True),
        lax.all_gather(down_weight, "dp", axis=1, tiled=True),
    )
    norm_one_b, in_again, conv_again, out_again, norm_two_b, gate_again, up_again, down_again = (
        regathered
    )
    gain_one = norm_one_b.astype(jnp.float32)
    gain_two = norm_two_b.astype(jnp.float32)
    taps_again = lax.dynamic_slice_in_dim(conv_again, channel_start, channels, 1).astype(
        jnp.float32
    )
    sigmoid = jax.nn.sigmoid(gate_pre)
    cotangent = lax.all_gather(out_grad, "tensor", axis=0, tiled=True)
    down_grad = jnp.einsum("tf,td->fd", activated, cotangent, preferred_element_type=jnp.float32)
    grad_act = jnp.einsum("td,fd->tf", cotangent, down_again, preferred_element_type=jnp.float32)
    grad_gate = (grad_act * upward * sigmoid * (1.0 + gate_pre * (1.0 - sigmoid))).astype(
        jnp.bfloat16
    )
    grad_up = (grad_act * gate_pre * sigmoid).astype(jnp.bfloat16)
    gate_grad = jnp.einsum("td,tf->df", normed_two, grad_gate, preferred_element_type=jnp.float32)
    up_grad = jnp.einsum("td,tf->df", normed_two, grad_up, preferred_element_type=jnp.float32)
    grad_two = lax.psum_scatter(
        (
            jnp.einsum("tf,df->td", grad_gate, gate_again, preferred_element_type=jnp.float32)
            + jnp.einsum("tf,df->td", grad_up, up_again, preferred_element_type=jnp.float32)
        ).astype(jnp.bfloat16),
        "tensor",
        scatter_dimension=0,
        tiled=True,
    ).astype(jnp.float32)
    feed_gain_part = jnp.sum(grad_two * unit_two, axis=0)
    grad_hidden = out_grad.astype(jnp.float32) + norm_back(
        grad_two, unit_two, inverse_two, gain_two
    )
    grad_mix_local = grad_hidden.astype(jnp.bfloat16)
    grad_mix = lax.all_gather(grad_mix_local, "tensor", axis=0, tiled=True)
    out_grad_part = jnp.einsum("tc,td->cd", mixer_in, grad_mix, preferred_element_type=jnp.float32)
    grad_in = jnp.einsum("td,cd->tc", grad_mix, out_again, preferred_element_type=jnp.float32)
    grad_c = grad_in * convolved
    grad_conv = grad_in * output_gate
    grad_mixed = sum(
        (
            taps_again[offset][None, :] * shift_up(tap_keep[offset][:, None] * grad_conv, offset)
            for offset in range(KW)
        )
    )
    tap_grad = jnp.stack(
        [
            jnp.sum(tap_keep[offset][:, None] * grad_conv * shift_down(mixed_input, offset), axis=0)
            for offset in range(KW)
        ]
    )
    grad_projected = jnp.stack(
        [grad_mixed * values, grad_c, grad_mixed * input_gate], axis=1
    ).astype(jnp.bfloat16)
    in_grad_part = jnp.einsum(
        "td,tkc->dkc", normed, grad_projected, preferred_element_type=jnp.float32
    )
    grad_one = lax.psum_scatter(
        jnp.einsum(
            "tkc,dkc->td", grad_projected, in_again, preferred_element_type=jnp.float32
        ).astype(jnp.bfloat16),
        "tensor",
        scatter_dimension=0,
        tiled=True,
    ).astype(jnp.float32)
    mixer_gain_part = jnp.sum(grad_one * unit_one, axis=0)
    input_grad = (grad_hidden + norm_back(grad_one, unit_one, inverse_one, gain_one)).astype(
        jnp.bfloat16
    )
    conv_part = lax.dynamic_update_slice_in_dim(
        jnp.zeros((KW, model_width), jnp.float32), tap_grad, channel_start, 1
    )
    summed = (
        lax.psum_scatter(mixer_gain_part, "dp", scatter_dimension=0, tiled=True),
        lax.psum_scatter(in_grad_part, "dp", scatter_dimension=0, tiled=True),
        lax.psum_scatter(conv_part, "dp", scatter_dimension=1, tiled=True),
        lax.psum_scatter(out_grad_part, "dp", scatter_dimension=1, tiled=True),
        lax.psum_scatter(feed_gain_part, "dp", scatter_dimension=0, tiled=True),
        lax.psum_scatter(gate_grad, "dp", scatter_dimension=0, tiled=True),
        lax.psum_scatter(up_grad, "dp", scatter_dimension=0, tiled=True),
        lax.psum_scatter(down_grad, "dp", scatter_dimension=1, tiled=True),
    )
    (
        mixer_gain_sum,
        in_weight_grad,
        conv_sum,
        out_weight_grad,
        feed_gain_sum,
        gate_weight_grad,
        up_weight_grad,
        down_weight_grad,
    ) = summed
    mixer_norm_grad, conv_weight_grad, feed_norm_grad = lax.psum(
        (mixer_gain_sum, conv_sum, feed_gain_sum), "tensor"
    )
    return (
        output,
        input_grad,
        mixer_norm_grad,
        in_weight_grad,
        conv_weight_grad,
        out_weight_grad,
        feed_norm_grad,
        gate_weight_grad,
        up_weight_grad,
        down_weight_grad,
    )


def solution(mesh):
    in_specs = (
        P(("dp", "tensor"), None),
        P("dp", None),
        P("dp"),
        P("dp", None, "tensor"),
        P(None, "dp"),
        P("tensor", "dp"),
        P("dp"),
        P("dp", "tensor"),
        P("dp", "tensor"),
        P("tensor", "dp"),
        P(("dp", "tensor"), None),
    )
    out_specs = (
        P(("dp", "tensor"), None),
        P(("dp", "tensor"), None),
        P("dp"),
        P("dp", None, "tensor"),
        P(None, "dp"),
        P("tensor", "dp"),
        P("dp"),
        P("dp", "tensor"),
        P("dp", "tensor"),
        P("tensor", "dp"),
    )
    n_dp = mesh.shape["dp"]
    fits = n_dp == 2 * NZ and mesh.shape["tensor"] == 4
    step = functools.partial(block, n_dp) if fits else body
    return jax.shard_map(step, mesh=mesh, in_specs=in_specs, out_specs=out_specs, check_vma=False)
```

```python
import functools

import jax
import jax.numpy as jnp
from jax import lax
from jax.experimental import pallas as pl
from jax.experimental.pallas import tpu as pltpu
from jax.sharding import PartitionSpec as P

KW = 3
MESH = pl.DeviceIdType.MESH
BF = jnp.bfloat16
F32 = jnp.float32

epsilon = 1e-05

NZ = 4
CONV = 4
FEED = 3
Y_LAST = (True, False, True, False)
X_FIRST = (False, True, False)
Y_FIRST = (True, True, True, True)


def nn(a, b):
    return lax.dot_general(a, b, (((1,), (0,)), ((), ())), preferred_element_type=F32)


def nt(a, b):
    return lax.dot_general(a, b, (((1,), (1,)), ((), ())), preferred_element_type=F32)


def tn(a, b):
    return lax.dot_general(a, b, (((0,), (0,)), ((), ())), preferred_element_type=F32)


class Place:
    def __init__(self):
        self.dp = lax.axis_index("dp")
        self.t = lax.axis_index("tensor")
        self.z, self.x = lax.div(self.dp, 2), lax.rem(self.dp, 2)
        self.y, self.c = lax.div(self.t, 2), lax.rem(self.t, 2)
        self.over_x = (self.z * 2 + 1 - self.x, self.t)
        self.over_y = (self.dp, (1 - self.y) * 2 + self.c)
        self.over_c = (self.dp, self.y * 2 + 1 - self.c)
        self.t_y = (1 - self.y) * 2 + self.c
        self.t_c = self.y * 2 + 1 - self.c
        self.t_yc = (1 - self.y) * 2 + 1 - self.c
        self.middle = lax.rem(lax.div(self.z + 1, 2), 2) == 1

    def zs(self, k):
        if k == 0:
            return self.z
        if k == 1:
            return self.z + 1 - 2 * lax.rem(self.z, 2)
        if k == 2:
            return lax.rem(self.z + 2, NZ)
        return NZ - 1 - self.z

    def over_z(self, k):
        return (self.zs(k) * 2 + self.x, self.t)


def greet(place, n_dp):
    barrier = pltpu.get_barrier_semaphore()
    for k in range(1, n_dp):
        peer = (lax.rem(place.dp + k, n_dp), place.t)
        pl.semaphore_signal(barrier, inc=1, device_id=peer, device_id_type=MESH)
    for peer in (place.over_c, place.over_y):
        pl.semaphore_signal(barrier, inc=1, device_id=peer, device_id_type=MESH)
    pl.semaphore_wait(barrier, n_dp + 1)


def remote(src, dst, send_sem, recv_sem, peer):
    return pltpu.make_async_remote_copy(
        src_ref=src, dst_ref=dst, send_sem=send_sem, recv_sem=recv_sem, device_id=peer, device_id_type=MESH
    )


def send(*what):
    copy = remote(*what)
    copy.start()
    return copy


def arrived(ref, sem, peer):
    pltpu.make_async_remote_copy(
        src_ref=ref, dst_ref=ref, send_sem=sem, recv_sem=sem, device_id=peer, device_id_type=MESH
    ).wait_recv()


def rows(start, size):
    return pl.ds(pl.multiple_of(start, size), size)


def forward_kernel(
    n_dp,
    tokens, cotangent, doc_rows, small, in_own, out_own, gate_own, up_own, down_own,
    conv_out, feed_out, normed_out, small_out, cot_out, proj_out, mixer_out, hidden_out, two_out, acts_out, keep_out,
    conv_w, feed_w, normed, small_all, mixed_pad, c_keep, proj, mixer_in, part_send, part_recv,
    hidden, two, acts, out_turned, down_turned, keep,
    own_sem, z_send, z_recv, x_send, x_recv, y_send, y_recv, fz_send, fz_recv, fx_send, fx_recv,
    s_send, s_recv, a_send, a_recv, out_sem,
):
    place = Place()
    z, x, y, c, t = place.z, place.x, place.y, place.c, place.t
    depth = gate_own.shape[0]
    local, width = tokens.shape
    chip = 2 * local
    half = in_own.shape[2]
    mine = 2 * half
    tile, pad = 256, 8
    blocks = (t, place.t_c, place.t_y, place.t_yc)
    sends = []
    copies = []
    owned = {}

    def post(make, when=None):
        if when is None:
            make().start()
        else:
            pl.when(when)(lambda: make().start())
        sends.append((make, when))

    def keep_own(src, dst, index):
        owned[index] = pltpu.make_async_copy(src, dst, own_sem.at[index])
        owned[index].start()

    def out(src, dst):
        copy = pltpu.make_async_copy(src, dst, out_sem.at[len(copies)])
        copy.start()
        copies.append(copy)

    def conv_part(j, dp, n, side):
        col = slice(None) if side is None else rows(side * half, half)
        return conv_w.at[j, rows(dp * depth, n * depth), col]

    def feed_part(w, dp, n=1):
        return feed_w.at[w, rows(dp * depth, n * depth), :]

    conv_own = [in_own.at[0], in_own.at[1], in_own.at[2], out_turned]
    feed_own = [gate_own, up_own, down_turned]

    def along_z(src, part, send_sems, recv_sems, index):
        for k in (2, 3, 1):
            post(lambda k=k: remote(src, part(z), send_sems.at[index, k], recv_sems.at[index, z], place.over_z(k)),
                 place.middle if k == 3 else None)

    def from_z(part, send_sems, recv_sems, index, k):
        zk = place.zs(k)
        arrived(part(zk), recv_sems.at[index, zk], place.over_z(k))
        if k == 2:
            post(lambda: remote(part(zk), part(zk), send_sems.at[index, 0], recv_sems.at[index, zk], place.over_z(1)), place.middle)

    def conv_z(j):
        return lambda zk: conv_part(j, zk * 2 + x, 1, y)

    def feed_z(w):
        if X_FIRST[w]:
            return lambda zk: feed_part(w, zk * 2, 2)
        return lambda zk: feed_part(w, zk * 2 + x)

    def conv_second(j, k, src=None):
        zk = place.zs(k)
        part = conv_part(j, zk * 2 + x, 1, y)
        src = part if src is None else src
        if Y_LAST[j]:
            post(lambda: remote(src, part, x_send.at[j, zk], x_recv.at[j, zk], place.over_x))
        else:
            post(lambda: remote(src, part, y_send.at[j, zk], y_recv.at[j, zk], place.over_y))

    def feed_x(w, k, src=None):
        zk = place.zs(k)
        part = feed_part(w, zk * 2 + x)
        src = part if src is None else src
        post(lambda: remote(src, part, fx_send.at[w, zk], fx_recv.at[w, zk], place.over_x))

    def cown(j):
        along_z(conv_own[j], conv_z(j), z_send, z_recv, j)
        conv_second(j, 0, conv_own[j])

    def cz(j, k):
        from_z(conv_z(j), z_send, z_recv, j, k)
        conv_second(j, k)

    def ct(j, k):
        zk = place.zs(k)
        if k == 0:
            owned[j].wait()
        if Y_LAST[j]:
            arrived(conv_part(j, zk * 2 + 1 - x, 1, y), x_recv.at[j, zk], place.over_x)
            pair = conv_part(j, zk * 2, 2, y)
            post(lambda: remote(pair, pair, y_send.at[j, zk], y_recv.at[j, zk], place.over_y))
        else:
            arrived(conv_part(j, zk * 2 + x, 1, 1 - y), y_recv.at[j, zk], place.over_y)
            pair = conv_part(j, zk * 2 + x, 1, None)
            post(lambda: remote(pair, pair, x_send.at[j, zk], x_recv.at[j, zk], place.over_x))

    def fx(w):
        feed_x(w, 0, feed_own[w])

    def fz(w):
        if X_FIRST[w]:
            arrived(feed_part(w, z * 2 + 1 - x), fx_recv.at[w, z], place.over_x)
            owned[CONV + w].wait()
            along_z(feed_part(w, z * 2, 2), feed_z(w), fz_send, fz_recv, w)
        else:
            along_z(feed_own[w], feed_z(w), fz_send, fz_recv, w)

    def fp(w, k):
        from_z(feed_z(w), fz_send, fz_recv, w, k)
        if not X_FIRST[w]:
            feed_x(w, k)

    def feed_ready(w):
        if not X_FIRST[w]:
            for k in range(NZ):
                zk = place.zs(k)
                arrived(feed_part(w, zk * 2 + 1 - x), fx_recv.at[w, zk], place.over_x)
            owned[CONV + w].wait()
        out(feed_w.at[w], feed_out.at[w])

    def cot_block(block):
        return cot_out.at[rows(block * local, local), :]

    def cotc():
        post(lambda: remote(cotangent, cot_block(t), a_send.at[0], a_recv.at[0], place.over_c))

    def coty():
        post(lambda: remote(cotangent, cot_block(t), a_send.at[2], a_recv.at[2], place.over_y))

    def cotf():
        there = cot_block(place.t_y)
        arrived(there, a_recv.at[2], place.over_y)
        post(lambda: remote(there, there, a_send.at[6], a_recv.at[6], place.over_c))

    def turn():
        down_turned[...] = jnp.transpose(down_own[...])
        for w in range(FEED):
            keep_own(feed_own[w], feed_part(w, place.dp), CONV + w)
        own = doc_rows[pl.ds(y, 1), :].astype(F32)
        position = lax.broadcasted_iota(jnp.int32, (1, chip), 1)
        for k in range(1, KW):
            same = jnp.where((own == pltpu.roll(own, k, 1)) & (position >= k), 1.0, 0.0)
            keep[k - 1, 0:chip, :] = jnp.transpose(jnp.broadcast_to(same, (128, chip)))
            keep[k - 1, chip : chip + pad, :] = jnp.zeros((pad, 128), F32)
        out(keep, keep_out)

    def gain(r):
        return jnp.concatenate([small_all[d, r : r + 1, :] for d in range(n_dp)], axis=1)

    def norm():
        for k in range(1, n_dp):
            peer = lax.rem(place.dp + k, n_dp)
            arrived(small_all.at[peer], s_recv.at[peer], (peer, t))
        inputs = tokens[...].astype(F32)
        inverse = lax.rsqrt(jnp.mean(inputs * inputs, axis=-1, keepdims=True) + epsilon)
        normed[rows(c * local, local), :] = (inputs * inverse * gain(0)).astype(BF)
        own = normed.at[rows(c * local, local), :]
        post(lambda: remote(own, own, a_send.at[1], a_recv.at[1], place.over_c))

    def p1():
        arrived(normed.at[rows((1 - c) * local, local), :], a_recv.at[1], place.over_c)
        for j in range(CONV):
            for k in range(NZ):
                zk = place.zs(k)
                if Y_LAST[j]:
                    arrived(conv_part(j, zk * 2, 2, 1 - y), y_recv.at[j, zk], place.over_y)
                else:
                    arrived(conv_part(j, zk * 2 + 1 - x, 1, None), x_recv.at[j, zk], place.over_x)
        out(conv_w, conv_out)
        out(normed, normed_out)
        mixed_pad[0:pad, :] = jnp.zeros((pad, mine), F32)

        def project(i, carry):
            at = rows(i * tile, tile)
            lhs = normed[at, :]
            b = nn(lhs, conv_w[0])
            proj[0, at, :] = b.astype(BF)
            v = nn(lhs, conv_w[2])
            proj[2, at, :] = v.astype(BF)
            mixed_pad[pl.ds(pl.multiple_of(i * tile + pad, 8), tile), :] = b * v
            g = nn(lhs, conv_w[1])
            proj[1, at, :] = g.astype(BF)
            c_keep[at, :] = g
            return carry

        lax.fori_loop(0, chip // tile, project, 0)

    def p2():
        taps = []
        for r in range(2, 2 + KW):
            taps.append(jnp.concatenate(
                [small_all[side * 4 + 2 * c + i, r : r + 1, :] for side in range(2) for i in range(2)], axis=1))

        def convolve(i, carry):
            at = rows(i * tile, tile)
            window = mixed_pad[pl.ds(pl.multiple_of(i * tile, 8), tile + pad), :]
            total = taps[0] * window[pad:, :]
            for k in range(1, KW):
                mask = jnp.concatenate([keep[k - 1, at, :]] * (mine // 128), axis=1)
                total = total + mask * taps[k] * window[pad - k : pad - k + tile, :]
            proj[3, at, :] = total.astype(BF)
            mixer_in[at, :] = (c_keep[at, :] * total).astype(BF)
            return carry

        lax.fori_loop(0, chip // tile, convolve, 0)
        out(proj, proj_out)
        out(mixer_in, mixer_out)
        part_send[...] = nt(mixer_in[rows((1 - c) * local, local), :], conv_w[3]).astype(BF)
        post(lambda: remote(part_send, part_recv, a_send.at[3], a_recv.at[3], place.over_c))
        hidden[...] = tokens[...].astype(F32) + nt(mixer_in[rows(c * local, local), :], conv_w[3])

    def p3():
        arrived(part_recv, a_recv.at[3], place.over_c)
        total = hidden[...] + part_recv[...].astype(F32)
        hidden[...] = total
        inverse = lax.rsqrt(jnp.mean(total * total, axis=-1, keepdims=True) + epsilon)
        two[rows(t * local, local), :] = (total * inverse * gain(1)).astype(BF)
        own = two.at[rows(t * local, local), :]
        post(lambda: remote(own, own, a_send.at[5], a_recv.at[5], place.over_y))
        post(lambda: remote(own, own, a_send.at[4], a_recv.at[4], place.over_c))
        out(hidden, hidden_out)

    def t2():
        there = two.at[rows(place.t_y * local, local), :]
        arrived(there, a_recv.at[5], place.over_y)
        post(lambda: remote(there, there, a_send.at[7], a_recv.at[7], place.over_c))

    def g(b):
        if b == 0:
            feed_ready(0)
        if b == 1:
            arrived(two.at[rows(place.t_c * local, local), :], a_recv.at[4], place.over_c)
        if b == 3:
            arrived(two.at[rows(place.t_yc * local, local), :], a_recv.at[7], place.over_c)

        def step(i, carry):
            at = rows(blocks[b] * local + i * tile, tile)
            gate = nn(two[at, :], feed_w[0])
            s = jax.nn.sigmoid(gate)
            silu = gate * s
            acts[1, at, :] = (s + silu * (1.0 - s)).astype(BF)
            acts[2, at, :] = silu.astype(BF)
            return carry

        lax.fori_loop(0, local // tile, step, 0)

    def u(b):
        if b == 0:
            feed_ready(1)

        def step(i, carry):
            at = rows(blocks[b] * local + i * tile, tile)
            upward = nn(two[at, :], feed_w[1])
            acts[0, at, :] = (acts[2, at, :].astype(F32) * upward).astype(BF)
            acts[1, at, :] = (acts[1, at, :].astype(F32) * upward).astype(BF)
            return carry

        lax.fori_loop(0, local // tile, step, 0)
        at = rows(blocks[b] * local, local)
        out(acts.at[:, at, :], acts_out.at[:, at, :])
        out(two.at[at, :], two_out.at[at, :])

    small_all[place.dp] = small[...]
    out_turned[...] = jnp.transpose(out_own[...])
    greet(place, n_dp)
    for k in range(1, n_dp):
        post(lambda k=k: remote(small, small_all.at[place.dp], s_send.at[k], s_recv.at[place.dp], (lax.rem(place.dp + k, n_dp), t)))
    for j in range(CONV):
        keep_own(conv_own[j], conv_part(j, place.dp, 1, y), j)
    keep_own(cotangent, cot_block(t), CONV + FEED)
    cown(2)
    cotc()
    cown(0)
    ct(2, 0)
    cown(3)
    ct(0, 0)
    cz(2, 2)
    cz(0, 2)
    cown(1)
    ct(3, 0)
    turn()
    cz(3, 2)
    cz(0, 3)
    fx(1)
    cz(3, 1)
    cz(2, 1)
    cz(0, 1)
    ct(0, 2)
    norm()
    fz(0)
    cz(1, 2)
    fz(2)
    ct(0, 3)
    cz(1, 1)
    fz(1)
    ct(1, 2)
    cz(3, 3)
    ct(3, 2)
    ct(2, 1)
    ct(2, 2)
    cz(2, 3)
    ct(3, 3)
    cz(1, 3)
    ct(3, 1)
    ct(1, 0)
    ct(1, 3)
    ct(1, 1)
    fp(0, 2)
    ct(2, 3)
    ct(0, 1)
    coty()
    p1()
    fx(2)
    fx(0)
    fp(2, 2)
    fp(0, 1)
    p2()
    p3()
    fp(0, 3)
    fp(1, 2)
    fp(2, 1)
    g(0)
    t2()
    g(2)
    g(1)
    fp(2, 3)
    cotf()
    g(3)
    fp(1, 1)
    fp(1, 3)
    u(0)
    u(1)
    u(2)
    u(3)
    feed_ready(2)
    small_out[...] = small_all[...]
    arrived(cot_block(place.t_c), a_recv.at[0], place.over_c)
    arrived(cot_block(place.t_yc), a_recv.at[6], place.over_c)
    owned[CONV + FEED].wait()
    for make, when in sends:
        if when is None:
            make().wait_send()
        else:
            pl.when(when)(lambda make=make: make().wait_send())
    for copy in copies:
        copy.wait()


def forward_call(n_dp, *operands):
    tokens, _, _, _, in_own, _, gate_own, _, _ = operands
    local, width = tokens.shape
    half, units = in_own.shape[2], gate_own.shape[1]
    chip, group, mine = 2 * local, 4 * local, 2 * half

    def shaped(dims, kind=BF):
        return jax.ShapeDtypeStruct(dims, kind)

    dma = pltpu.SemaphoreType.DMA
    vmem, any_space = pl.BlockSpec(memory_space=pltpu.VMEM), pl.BlockSpec(memory_space=pl.ANY)
    return pl.pallas_call(
        functools.partial(forward_kernel, n_dp),
        name="gather_forward",
        out_shape=(
            shaped((CONV, width, mine)), shaped((FEED, width, units)), shaped((chip, width)), shaped((n_dp, 8, 128), F32),
            shaped((group, width)), shaped((4, chip, mine)), shaped((chip, mine)), shaped((local, width), F32),
            shaped((group, width)), shaped((3, group, units)), shaped((KW - 1, chip + 8, 128), F32),
        ),
        in_specs=[vmem] * 4 + [any_space, vmem, any_space, any_space, vmem],
        out_specs=tuple(vmem if i == 3 else any_space for i in range(11)),
        scratch_shapes=[
            pltpu.VMEM((CONV, width, mine), BF), pltpu.VMEM((FEED, width, units), BF), pltpu.VMEM((chip, width), BF),
            pltpu.VMEM((n_dp, 8, 128), F32), pltpu.VMEM((chip + 8, mine), F32),
            pltpu.VMEM((chip, mine), F32), pltpu.VMEM((4, chip, mine), BF), pltpu.VMEM((chip, mine), BF),
            pltpu.VMEM((local, width), BF), pltpu.VMEM((local, width), BF), pltpu.VMEM((local, width), F32),
            pltpu.VMEM((group, width), BF), pltpu.VMEM((3, group, units), BF),
            pltpu.VMEM((width // n_dp, half), BF), pltpu.VMEM((width // n_dp, units), BF), pltpu.VMEM((KW - 1, chip + 8, 128), F32),
            dma((8,)), dma((CONV, NZ)), dma((CONV, NZ)), dma((CONV, NZ)), dma((CONV, NZ)), dma((CONV, NZ)), dma((CONV, NZ)),
            dma((FEED, NZ)), dma((FEED, NZ)), dma((FEED, NZ)), dma((FEED, NZ)),
            dma((n_dp,)), dma((n_dp,)), dma((8,)), dma((8,)), dma((20,)),
        ],
        compiler_params=pltpu.CompilerParams(collective_id=0, has_side_effects=True, vmem_limit_bytes=62 << 20),
    )(*operands)


def backward_kernel(
    n_dp,
    small_all, tokens_in, cot_own_in, keep_in, conv_in, feed_in, normed_in, cot_in, proj_in, mixer_in_hbm, hidden_in, two_in, acts_in,
    output, input_grad, in_grad, out_grad, gate_grad, up_grad, down_grad, small_grad,
    act, g_down, x_got, z_got, c_got_y, c_got_x, c_two, c_z, two_send, two_recv, two_y, own_two,
    down_send, down_recv, down_y, down_own, grad_mix, feed_gain, small_sum, small_got, small_z,
    load_sem, fx_send, fx_recv, fz_send, fz_recv, c1_send, c1_recv, c2_send, c2_recv, c3_send, c3_recv,
    s_send, s_recv, a_send, a_recv,
):
    place = Place()
    z, x, y, c, t = place.z, place.x, place.y, place.c, place.t
    depth, units = gate_grad.shape
    local, width = own_two.shape
    chip = 2 * local
    half = in_grad.shape[2]
    mine = 2 * half
    tile = 256
    sends = []

    def post(make):
        make().start()
        sends.append(make)
        return make

    def load(src, dst, index):
        copy = pltpu.make_async_copy(src, dst, load_sem.at[index])
        copy.start()
        return copy

    def g_rows(w, start, size):
        if w == 2:
            return g_down.at[rows(start, size), :]
        return act.at[rows(w * width + start, size), :]

    def m(w, k):
        zk = place.zs(k)
        got = x_got.at[w, zk]
        arrived(got, fx_recv.at[w, zk], place.over_x)
        if k:
            got[...] = (g_rows(w, (zk * 2 + x) * depth, depth)[...].astype(F32) + got[...].astype(F32)).astype(BF)

            def add(more):
                held = x_got.at[w, place.zs(k)]
                held[...] = (held[...].astype(F32) + more[...].astype(F32)).astype(BF)

            if k == 2:
                @pl.when(place.middle)
                def _():
                    arrived(z_got.at[w, 0], fz_recv.at[w, 0], place.over_z(1))
                    add(z_got.at[w, 0])

            post(lambda: z_remote(x_got.at[w, place.zs(k)], z_got.at[w], fz_send.at[w], fz_recv.at[w], k))

    def z_remote(held, got, sends_at, recvs_at, k):
        if k == 3:
            slot = jnp.where(place.middle, 3, 0)
            peer = (jnp.where(place.middle, place.zs(3), place.zs(1)) * 2 + x, t)
            return remote(held, got.at[slot], sends_at.at[k], recvs_at.at[slot], peer)
        return remote(held, got.at[k], sends_at.at[k], recvs_at.at[k], place.over_z(k))

    def z_sum(total, got, recvs_at):
        for k in (1, 2):
            arrived(got.at[k], recvs_at.at[k], place.over_z(k))
            total = total + got[k].astype(F32)
        return total

    def z_last(ref, got, recvs_at):
        @pl.when(place.middle)
        def _():
            arrived(got.at[3], recvs_at.at[3], place.over_z(3))
            ref[...] = ref[...] + got[3].astype(F32)

    def gain(r):
        return jnp.concatenate([small_all[d, r : r + 1, :] for d in range(n_dp)], axis=1)

    def norm_back(grad, unit, inverse, scale):
        scaled = grad * scale
        return inverse * (scaled - unit * jnp.mean(scaled * unit, axis=-1, keepdims=True))

    def rms(values):
        return lax.rsqrt(jnp.mean(values * values, axis=-1, keepdims=True) + epsilon)

    def send_slot(i):
        return lambda: remote(two_send.at[i], two_recv.at[i], a_send.at[1 + i], a_recv.at[1 + i], place.over_c)

    first_slot = send_slot(0)

    def feed_phase(feed_w, cot, acts):
        loads = [load(acts_in.at[0], act, 0), load(cot_in, cot, 1), load(feed_in, feed_w, 2),
                 load(acts_in.at[1], acts.at[0], 3), load(acts_in.at[2], acts.at[1], 4)]
        greet(place, n_dp)
        waited = set()

        def loaded(*which):
            for i in which:
                if i not in waited:
                    waited.add(i)
                    loads[i].wait()

        def g(w, k):
            at = rows(place.zs(k) * 2 * depth, 2 * depth)
            if w == 2:
                loaded(0, 1)
                g_down[at, :] = tn(cot[:, at], act[...]).astype(BF)
            else:
                if 5 not in waited:
                    loads.append(load(two_in, cot, 5))
                    loaded(5)
                act[rows(w * width + place.zs(k) * 2 * depth, 2 * depth), :] = tn(cot[:, at], acts[w]).astype(BF)

            def make():
                zk = place.zs(k)
                return remote(g_rows(w, (zk * 2 + 1 - x) * depth, depth), x_got.at[w, zk], fx_send.at[w, zk], fx_recv.at[w, zk], place.over_x)

            post(make)

        def back(block, store):
            loaded(1, 2, 3, 4)

            def step(i, carry):
                at = rows(block * local + i * tile, tile)
                grad_act = nn(cot[at, :], feed_w[2])
                grad_gate = (grad_act * acts[0, at, :].astype(F32)).astype(BF)
                acts[0, at, :] = grad_gate
                grad_up = (grad_act * acts[1, at, :].astype(F32)).astype(BF)
                acts[1, at, :] = grad_up
                store(rows(i * tile, tile), nt(grad_gate, feed_w[0]) + nt(grad_up, feed_w[1]))
                return carry

            lax.fori_loop(0, local // tile, step, 0)

        def to_slot(i):
            def store(at, value):
                two_send[i, at, :] = value.astype(BF)

            return store

        def to_own(at, value):
            own_two[at, :] = value

        def a_yc():
            back(place.t_yc, to_slot(0))
            post(first_slot)

        def a_c():
            back(place.t_c, to_slot(1))
            post(send_slot(1))

        def a_y():
            back(place.t_y, to_own)

        def ay():
            arrived(two_recv.at[0], a_recv.at[1], place.over_c)
            two_recv[0] = (own_two[...] + two_recv[0].astype(F32)).astype(BF)
            post(lambda: remote(two_recv.at[0], two_y, a_send.at[3], a_recv.at[3], place.over_y))

        def a_o():
            back(t, to_own)

        def down(block):
            loaded(0, 2)
            return nt(act[rows(block * local, local), :], feed_w[2]).astype(BF)

        def d_yc():
            down_send[0] = down(place.t_yc)
            post(lambda: remote(down_send.at[0], down_recv.at[0], a_send.at[6], a_recv.at[6], place.over_c))

        def d_c():
            down_send[1] = down(place.t_c)
            post(lambda: remote(down_send.at[1], down_recv.at[1], a_send.at[7], a_recv.at[7], place.over_c))

        def d_y():
            down_own[...] = down(place.t_y)

        def dy():
            arrived(down_recv.at[0], a_recv.at[6], place.over_c)
            down_recv[0] = (down_own[...].astype(F32) + down_recv[0].astype(F32)).astype(BF)
            post(lambda: remote(down_recv.at[0], down_y, a_send.at[8], a_recv.at[8], place.over_y))

        def d_o():
            down_own[...] = down(t)

        g(2, 0)
        g(2, 3)
        a_yc()
        a_y()
        ay()
        d_yc()
        m(2, 0)
        d_y()
        g(2, 1)
        m(2, 3)
        d_c()
        g(2, 2)
        a_o()
        a_c()
        m(2, 1)
        dy()
        d_o()
        g(0, 3)
        m(2, 2)
        g(1, 3)
        g(0, 1)
        g(0, 2)
        g(1, 2)
        g(1, 0)
        g(1, 1)
        g(0, 0)

    pl.run_scoped(
        feed_phase,
        pltpu.VMEM((FEED, width, units), BF), pltpu.VMEM((4 * local, width), BF), pltpu.VMEM((2, 4 * local, units), BF),
    )

    def conv_phase(conv_w, proj, normed, mixer_in, grad_proj, pad_grad, tap_sum, g_conv, token_rows, keep, hidden, stage):
        loads = [load(hidden_in, hidden, 0), load(cot_own_in, token_rows, 1), load(conv_in.at[3], conv_w.at[3], 2), load(mixer_in_hbm, mixer_in, 3),
                 load(proj_in, proj, 4), load(normed_in, normed, 5), load(conv_in.at[pl.ds(0, 3)], conv_w.at[pl.ds(0, 3)], 6),
                 load(keep_in, keep, 7)]
        waited = set()

        def loaded(*which):
            for i in which:
                if i not in waited:
                    waited.add(i)
                    loads[i].wait()

        def n2():
            loaded(0, 1)
            arrived(two_y, a_recv.at[3], place.over_y)
            arrived(two_recv.at[1], a_recv.at[2], place.over_c)
            scale = gain(1)

            def step(i, carry):
                at = rows(i * 128, 128)
                grad_two = own_two[at, :] + two_recv[1, at, :].astype(F32) + two_y[at, :].astype(F32)
                values = hidden[at, :]
                inverse = rms(values)
                unit = values * inverse
                grad_hidden = token_rows[at, :].astype(F32) + norm_back(grad_two, unit, inverse, scale)
                hidden[at, :] = grad_hidden
                grad_mix[rows(c * local + i * 128, 128), :] = grad_hidden.astype(BF)
                return carry + jnp.sum(grad_two * unit, axis=0, keepdims=True)

            feed_gain[0:1, :] = lax.fori_loop(0, local // 128, step, jnp.zeros((1, width), F32))
            loads.append(load(tokens_in, token_rows, 8))

            def make():
                own = grad_mix.at[rows(c * local, local), :]
                return remote(own, own, a_send.at[4], a_recv.at[4], place.over_c)

            post(make)

        def taps():
            return [jnp.concatenate([small_all[side * 4 + 2 * c + i, r : r + 1, :] for side in range(2) for i in range(2)], axis=1)
                    for r in range(2, 2 + KW)]

        def gm():
            loaded(2, 4)
            arrived(grad_mix.at[rows((1 - c) * local, local), :], a_recv.at[4], place.over_c)
            pad_grad[pl.ds(chip, 8), :] = jnp.zeros((8, mine), F32)

            def step(i, carry):
                at = rows(i * tile, tile)
                grad_in = nn(grad_mix[at, :], conv_w[3])
                grad_proj[1, at, :] = (grad_in * proj[3, at, :].astype(F32)).astype(BF)
                pad_grad[at, :] = grad_in * proj[1, at, :].astype(F32)
                return carry

            lax.fori_loop(0, chip // tile, step, 0)

        def c1_slot(j, zk):
            if Y_FIRST[j]:
                return c_got_y.at[sum(Y_FIRST[:j]), zk]
            return c_got_x.at[j - sum(Y_FIRST[:j]), zk]

        def w(j):
            if j == 3:
                loaded(3)
                g_conv[j] = tn(grad_mix[...], mixer_in[...]).astype(BF)
            else:
                loaded(5)
                g_conv[j] = tn(normed[...], grad_proj[j]).astype(BF)
            for k in (2, 1, 3, 0):
                zk = place.zs(k)
                if Y_FIRST[j]:
                    src, peer = g_conv.at[j, rows(zk * 2 * depth, 2 * depth), rows((1 - y) * half, half)], place.over_y
                else:
                    src, peer = g_conv.at[j, rows((zk * 2 + 1 - x) * depth, depth), :], place.over_x
                post(lambda src=src, peer=peer, zk=zk: remote(src, c1_slot(j, zk), c1_send.at[j, zk], c1_recv.at[j, zk], peer))

        def h2():
            loaded(4, 7)
            tap = taps()
            tap_sum[...] = jnp.zeros_like(tap_sum)
            size = 128

            def step(i, carry):
                at = rows(i * size, size)
                wide = pl.ds(pl.multiple_of(i * size, 8), size + 8)
                window = pad_grad[wide, :]
                b, v = proj[0, at, :].astype(F32), proj[2, at, :].astype(F32)
                mixed = b * v
                now = window[:size, :]
                total = tap[0] * now
                tap_sum[0:1, :] += jnp.sum(now * mixed, axis=0, keepdims=True)
                for k in range(1, KW):
                    mask = jnp.concatenate([keep[k - 1, wide, :]] * (mine // 128), axis=1)
                    ahead = (mask * window)[k : k + size, :]
                    total = total + tap[k] * ahead
                    tap_sum[k : k + 1, :] += jnp.sum(ahead * mixed, axis=0, keepdims=True)
                grad_proj[0, at, :] = (total * v).astype(BF)
                grad_proj[2, at, :] = (total * b).astype(BF)
                return carry

            lax.fori_loop(0, chip // size, step, 0)

        def first_grad(block):
            at = rows(block * local, local)
            return nt(grad_proj[0, at, :], conv_w[0]) + nt(grad_proj[1, at, :], conv_w[1]) + nt(grad_proj[2, at, :], conv_w[2])

        def f1():
            loaded(6)
            first_slot().wait_send()
            sends.remove(first_slot)
            two_send[0] = first_grad(1 - c).astype(BF)
            post(lambda: remote(two_send.at[0], two_recv.at[1], a_send.at[5], a_recv.at[5], place.over_c))
            own_two[...] = first_grad(c)

        def n1():
            loaded(8)
            arrived(two_recv.at[1], a_recv.at[5], place.over_c)
            scale = gain(0)

            def step(i, carry):
                at = rows(i * 128, 128)
                grad_one = own_two[at, :] + two_recv[1, at, :].astype(F32)
                values = token_rows[at, :].astype(F32)
                inverse = rms(values)
                unit = values * inverse
                two_recv[1, at, :] = (hidden[at, :] + norm_back(grad_one, unit, inverse, scale)).astype(BF)
                return carry + jnp.sum(grad_one * unit, axis=0, keepdims=True)

            mixer_gain = lax.fori_loop(0, local // 128, step, jnp.zeros((1, width), F32))
            loads.append(load(two_recv.at[1], input_grad, 1))
            loads.append(load(hidden_in, own_two, 0))
            zero = jnp.zeros((1, 128), F32)
            for d in range(n_dp):
                cols = slice(d * 128, d * 128 + 128)
                here = (c == (d % 4) // 2).astype(F32)
                own = (d // 4) * half + (d % 2) * 128
                small_sum[d] = jnp.concatenate(
                    [mixer_gain[:, cols], feed_gain[0:1, cols]]
                    + [here * tap_sum[k : k + 1, own : own + 128] for k in range(KW)] + [zero] * 3, axis=0)

        def c2(j, k):
            zk = place.zs(k)
            got = c1_slot(j, zk)
            if Y_FIRST[j]:
                arrived(got, c1_recv.at[j, zk], place.over_y)
                held = g_conv[j, rows(zk * 2 * depth, 2 * depth), rows(y * half, half)]
                src, peer = got.at[rows((1 - x) * depth, depth), :], place.over_x
            else:
                arrived(got, c1_recv.at[j, zk], place.over_x)
                held = g_conv[j, rows((zk * 2 + x) * depth, depth), :]
                src, peer = got.at[:, rows((1 - y) * half, half)], place.over_y
            got[...] = (held.astype(F32) + got[...].astype(F32)).astype(BF)
            post(lambda: remote(src, c_two.at[j, zk], c2_send.at[j, zk], c2_recv.at[j, zk], peer))

        def held_half(j, zk):
            if Y_FIRST[j]:
                return c1_slot(j, zk)[rows(x * depth, depth), :].astype(F32)
            return c1_slot(j, zk)[:, rows(y * half, half)].astype(F32)

        def c3(j, k):
            zk = place.zs(k)
            got = c_two.at[j, zk]
            arrived(got, c2_recv.at[j, zk], place.over_x if Y_FIRST[j] else place.over_y)
            if k:
                got[...] = (held_half(j, zk) + got[...].astype(F32)).astype(BF)
                if k == 2:
                    @pl.when(place.middle)
                    def _():
                        arrived(c_z.at[j, 0], c3_recv.at[j, 0], place.over_z(1))
                        got[...] = (got[...].astype(F32) + c_z[j, 0].astype(F32)).astype(BF)

                post(lambda: z_remote(got, c_z.at[j], c3_send.at[j], c3_recv.at[j], k))

        def cf(j):
            total = z_sum(held_half(j, z) + c_two[j, z].astype(F32), c_z.at[j], c3_recv.at[j])
            if j == 3:
                stage[0:depth, 0:half] = total
                ref = stage.at[0:depth, 0:half]
                z_last(ref, c_z.at[j], c3_recv.at[j])
                out_grad[...] = jnp.transpose(ref[...])
            else:
                in_grad[j] = total
                z_last(in_grad.at[j], c_z.at[j], c3_recv.at[j])

        def ff(w):
            total = g_rows(w, (z * 2 + x) * depth, depth)[...].astype(F32) + x_got[w, z].astype(F32)
            total = z_sum(total, z_got.at[w], fz_recv.at[w])
            ref = (gate_grad, up_grad, stage)[w]
            ref[...] = total
            z_last(ref, z_got.at[w], fz_recv.at[w])
            if w == 2:
                down_grad[...] = jnp.transpose(stage[...])

        def do():
            loads[-1].wait()
            arrived(down_recv.at[1], a_recv.at[7], place.over_c)
            arrived(down_y, a_recv.at[8], place.over_y)
            total = own_two[...] + down_own[...].astype(F32) + down_recv[1].astype(F32) + down_y[...].astype(F32)
            down_own[...] = total.astype(BF)
            loads.append(load(down_own, output, 2))

        def s0():
            post(lambda: remote(small_sum, small_got.at[0], s_send.at[0], s_recv.at[0], place.over_c))

        def s1():
            arrived(small_got.at[0], s_recv.at[0], place.over_c)
            small_got[0] = small_sum[...] + small_got[0]
            post(lambda: remote(small_got.at[0], small_got.at[1], s_send.at[1], s_recv.at[1], place.over_y))

        def s2():
            arrived(small_got.at[1], s_recv.at[1], place.over_y)
            small_got[1] = small_got[0] + small_got[1]
            for k in range(NZ):
                zk = place.zs(k)
                post(lambda zk=zk, k=k: remote(
                    small_got.at[1, zk * 2 + 1 - x], small_z.at[zk], s_send.at[2 + k], s_recv.at[2 + zk], place.over_x))

        def s3():
            for k in range(NZ):
                zk = place.zs(k)
                arrived(small_z.at[zk], s_recv.at[2 + zk], place.over_x)
                small_z[zk] = small_z[zk] + small_got[1, zk * 2 + x]
                if k:
                    post(lambda zk=zk, k=k: remote(small_z.at[zk], small_z.at[NZ + k], s_send.at[6 + k], s_recv.at[6 + k], place.over_z(k)))

        def s4():
            total = small_z[z]
            for k in range(1, NZ):
                arrived(small_z.at[NZ + k], s_recv.at[6 + k], place.over_z(k))
                total = total + small_z[NZ + k]
            small_grad[...] = total

        n2()
        m(0, 3)
        m(1, 3)
        gm()
        w(1)
        m(0, 2)
        m(0, 1)
        h2()
        c2(1, 2)
        w(3)
        m(1, 2)
        w(2)
        f1()
        c2(3, 3)
        n1()
        m(1, 0)
        s0()
        c2(1, 3)
        c2(1, 1)
        m(1, 1)
        s1()
        c2(1, 0)
        c2(2, 1)
        c3(1, 3)
        c2(3, 2)
        w(0)
        c2(2, 2)
        c2(2, 0)
        c2(3, 1)
        c3(1, 2)
        s2()
        c2(2, 3)
        c3(3, 3)
        c3(1, 1)
        c3(3, 2)
        c2(0, 1)
        c3(3, 1)
        c3(2, 3)
        c2(0, 3)
        c2(3, 0)
        m(0, 0)
        do()
        s3()
        c3(2, 0)
        c3(0, 1)
        c2(0, 2)
        c3(0, 3)
        c3(2, 2)
        ff(0)
        c3(1, 0)
        c3(3, 0)
        cf(3)
        c2(0, 0)
        c3(2, 1)
        c3(0, 2)
        c3(0, 0)
        ff(1)
        cf(2)
        ff(2)
        cf(1)
        s4()
        cf(0)
        for make in sends:
            make().wait_send()
        loads[-3].wait()
        loads[-1].wait()

    pl.run_scoped(
        conv_phase,
        pltpu.VMEM((CONV, width, mine), BF), pltpu.VMEM((4, chip, mine), BF), pltpu.VMEM((chip, width), BF),
        pltpu.VMEM((chip, mine), BF), pltpu.VMEM((3, chip, mine), BF), pltpu.VMEM((chip + 8, mine), F32), pltpu.VMEM((8, mine), F32),
        pltpu.VMEM((CONV, width, mine), BF), pltpu.VMEM((local, width), BF),
        pltpu.VMEM((KW - 1, chip + 8, 128), F32), pltpu.VMEM((local, width), F32), pltpu.VMEM((depth, units), F32),
    )


def backward_call(n_dp, small_all, tokens, cotangent, keep, conv_w, feed_w, *rest):
    local, width = tokens.shape
    units, mine = feed_w.shape[2], conv_w.shape[2]
    chip, half, depth = 2 * local, mine // 2, width // n_dp
    over_y = sum(Y_FIRST)

    def shaped(dims, kind=BF):
        return jax.ShapeDtypeStruct(dims, kind)

    def slots(n, *dims):
        return pltpu.VMEM((max(n, 1), *(dims if n else (NZ, 16, 128))), BF)

    dma = pltpu.SemaphoreType.DMA
    vmem, any_space = pl.BlockSpec(memory_space=pltpu.VMEM), pl.BlockSpec(memory_space=pl.ANY)
    return pl.pallas_call(
        functools.partial(backward_kernel, n_dp),
        name="backward_scatter",
        out_shape=(
            shaped((local, width)), shaped((local, width)), shaped((3, depth, half), F32), shaped((half, depth), F32),
            shaped((depth, units), F32), shaped((depth, units), F32), shaped((units, depth), F32), shaped((8, 128), F32),
        ),
        in_specs=[vmem] + [any_space] * (5 + len(rest)),
        out_specs=(any_space,) * 2 + (vmem,) * 6,
        scratch_shapes=[
            pltpu.VMEM((4 * local, units), BF), pltpu.VMEM((width, units), BF), pltpu.VMEM((FEED, NZ, depth, units), BF),
            pltpu.VMEM((FEED, NZ, depth, units), BF),
            slots(over_y, NZ, 2 * depth, half), slots(CONV - over_y, NZ, depth, mine), pltpu.VMEM((CONV, NZ, depth, half), BF),
            pltpu.VMEM((CONV, NZ, depth, half), BF), pltpu.VMEM((2, local, width), BF), pltpu.VMEM((2, local, width), BF),
            pltpu.VMEM((local, width), BF), pltpu.VMEM((local, width), F32),
            pltpu.VMEM((2, local, width), BF), pltpu.VMEM((2, local, width), BF), pltpu.VMEM((local, width), BF),
            pltpu.VMEM((local, width), BF), pltpu.VMEM((chip, width), BF), pltpu.VMEM((8, width), F32), pltpu.VMEM((n_dp, 8, 128), F32),
            pltpu.VMEM((2, n_dp, 8, 128), F32), pltpu.VMEM((2 * NZ, 8, 128), F32),
            dma((9,)), dma((FEED, NZ)), dma((FEED, NZ)), dma((FEED, NZ)), dma((FEED, NZ)), dma((CONV, NZ)), dma((CONV, NZ)),
            dma((CONV, NZ)), dma((CONV, NZ)), dma((CONV, NZ)), dma((CONV, NZ)), dma((10,)), dma((10,)), dma((9,)), dma((9,)),
        ],
        compiler_params=pltpu.CompilerParams(collective_id=1, has_side_effects=True, vmem_limit_bytes=63 << 20),
    )(small_all, tokens, cotangent, keep, conv_w, feed_w, *rest)


def finish_kernel(n, small, *refs):
    arrays, outs, held, in_sem, out_sem = refs[:n], refs[n : 2 * n + 3], refs[2 * n + 3 : 3 * n + 3], refs[-2], refs[-1]
    loads = [pltpu.make_async_copy(arrays[i], held[i], in_sem.at[i]) for i in range(n)]
    stores = [pltpu.make_async_copy(held[i], outs[i], out_sem.at[i]) for i in range(n)]
    for copy in loads:
        copy.start()
    outs[n][...] = small[0:1, :]
    outs[n + 1][...] = small[1:2, :]
    outs[n + 2][...] = small[2 : 2 + KW, :]
    for load, store in zip(loads, stores):
        load.wait()
        store.start()
    for copy in stores:
        copy.wait()


def finish_call(small, *arrays):
    vmem, any_space = pl.BlockSpec(memory_space=pltpu.VMEM), pl.BlockSpec(memory_space=pl.ANY)
    n = len(arrays)
    row = small.shape[1]
    return pl.pallas_call(
        functools.partial(finish_kernel, n),
        name="finish",
        out_shape=tuple(jax.ShapeDtypeStruct(a.shape, a.dtype) for a in arrays)
        + tuple(jax.ShapeDtypeStruct((r, row), F32) for r in (1, 1, KW)),
        in_specs=[vmem] + [any_space] * n,
        out_specs=(any_space,) * n + (vmem,) * 3,
        scratch_shapes=[pltpu.VMEM(a.shape, a.dtype) for a in arrays] + [pltpu.SemaphoreType.DMA((n,))] * 2,
        compiler_params=pltpu.CompilerParams(vmem_limit_bytes=62 << 20),
    )(small, *arrays)


def block(n_dp, tokens, doc_ids, mixer_norm, in_weight, conv_weight, out_weight, feed_norm, gate_weight, up_weight, down_weight, out_grad):
    small = jnp.concatenate(
        [mixer_norm[None], feed_norm[None], conv_weight, jnp.zeros((6 - KW, mixer_norm.shape[0]), BF)], axis=0).astype(F32)
    conv_w, feed_w, normed, small_all, cot, proj, mixer_in, hidden, two, acts, keep = forward_call(
        n_dp, tokens, out_grad, doc_ids, small, in_weight.transpose(1, 0, 2), out_weight, gate_weight, up_weight, down_weight)
    *large, small_g = backward_call(
        n_dp, small_all, tokens, out_grad, keep, conv_w, feed_w, normed, cot, proj, mixer_in, hidden, two, acts)
    output, input_grad, in_g, out_g, gate_g, up_g, down_g, mixer_g, feed_g, taps_g = finish_call(small_g, *large)
    return (output, input_grad, mixer_g[0], in_g.transpose(1, 0, 2), taps_g, out_g, feed_g[0], gate_g, up_g, down_g)


def shift_down(values, offset):
    if offset == 0:
        return values
    padding = jnp.zeros((offset,) + values.shape[1:], values.dtype)
    return jnp.concatenate([padding, values[:-offset]], axis=0)


def shift_up(values, offset):
    if offset == 0:
        return values
    padding = jnp.zeros((offset,) + values.shape[1:], values.dtype)
    return jnp.concatenate([values[offset:], padding], axis=0)


def tap_masks(doc_rows):
    total_rows = doc_rows.shape[0] * doc_rows.shape[1]
    tap_keep = [jnp.ones((total_rows,), jnp.float32)]
    for offset in range(1, KW):
        matching = doc_rows[:, offset:] == doc_rows[:, :-offset]
        leading = jnp.zeros((doc_rows.shape[0], offset), dtype=bool)
        matching = jnp.concatenate([leading, matching], axis=1)
        tap_keep.append(jnp.where(matching, 1.0, 0.0).astype(jnp.float32).reshape(total_rows))
    return jnp.stack(tap_keep)


def norm_back(grad_out, unit_rows, inverse, gain):
    scaled = grad_out * gain
    return inverse * (scaled - unit_rows * jnp.mean(scaled * unit_rows, axis=-1, keepdims=True))


def body(
    tokens,
    doc_ids,
    mixer_norm,
    in_weight,
    conv_weight,
    out_weight,
    feed_norm,
    gate_weight,
    up_weight,
    down_weight,
    out_grad,
):
    model_width = tokens.shape[1]
    gathered = (
        lax.all_gather(mixer_norm, "dp", axis=0, tiled=True),
        lax.all_gather(in_weight, "dp", axis=0, tiled=True),
        lax.all_gather(conv_weight, "dp", axis=1, tiled=True),
        lax.all_gather(out_weight, "dp", axis=1, tiled=True),
        lax.all_gather(feed_norm, "dp", axis=0, tiled=True),
        lax.all_gather(gate_weight, "dp", axis=0, tiled=True),
        lax.all_gather(up_weight, "dp", axis=0, tiled=True),
        lax.all_gather(down_weight, "dp", axis=1, tiled=True),
    )
    norm_one, in_full, conv_full, out_full, norm_two, gate_full, up_full, down_full = gathered
    channels = in_full.shape[2]
    channel_start = lax.axis_index("tensor") * channels
    tap_keep = tap_masks(doc_ids)
    conv_taps = lax.dynamic_slice_in_dim(conv_full, channel_start, channels, 1).astype(jnp.float32)
    inputs = tokens.astype(jnp.float32)
    inverse_one = lax.rsqrt(jnp.mean(inputs * inputs, axis=-1, keepdims=True) + epsilon)
    unit_one = inputs * inverse_one
    normed_local = (unit_one * norm_one.astype(jnp.float32)).astype(jnp.bfloat16)
    normed = lax.all_gather(normed_local, "tensor", axis=0, tiled=True)
    projected = jnp.einsum("td,dkc->tkc", normed, in_full, preferred_element_type=jnp.float32)
    input_gate = projected[:, 0]
    output_gate = projected[:, 1]
    values = projected[:, 2]
    mixed_input = input_gate * values
    convolved = sum(
        (
            tap_keep[offset][:, None] * conv_taps[offset][None, :] * shift_down(mixed_input, offset)
            for offset in range(KW)
        )
    )
    mixer_in = (output_gate * convolved).astype(jnp.bfloat16)
    mixer_out = lax.psum_scatter(
        jnp.dot(mixer_in, out_full, preferred_element_type=jnp.float32),
        "tensor",
        scatter_dimension=0,
        tiled=True,
    )
    hidden = inputs + mixer_out
    inverse_two = lax.rsqrt(jnp.mean(hidden * hidden, axis=-1, keepdims=True) + epsilon)
    unit_two = hidden * inverse_two
    normed_two_local = (unit_two * norm_two.astype(jnp.float32)).astype(jnp.bfloat16)
    normed_two = lax.all_gather(normed_two_local, "tensor", axis=0, tiled=True)
    gate_pre = jnp.dot(normed_two, gate_full, preferred_element_type=jnp.float32)
    upward = jnp.dot(normed_two, up_full, preferred_element_type=jnp.float32)
    activated = (jax.nn.silu(gate_pre) * upward).astype(jnp.bfloat16)
    feed_out = lax.psum_scatter(
        jnp.dot(activated, down_full, preferred_element_type=jnp.float32).astype(jnp.bfloat16),
        "tensor",
        scatter_dimension=0,
        tiled=True,
    ).astype(jnp.float32)
    output = (hidden + feed_out).astype(jnp.bfloat16)
    regathered = (
        lax.all_gather(mixer_norm, "dp", axis=0, tiled=True),
        lax.all_gather(in_weight, "dp", axis=0, tiled=True),
        lax.all_gather(conv_weight, "dp", axis=1, tiled=True),
        lax.all_gather(out_weight, "dp", axis=1, tiled=True),
        lax.all_gather(feed_norm, "dp", axis=0, tiled=True),
        lax.all_gather(gate_weight, "dp", axis=0, tiled=True),
        lax.all_gather(up_weight, "dp", axis=0, tiled=True),
        lax.all_gather(down_weight, "dp", axis=1, tiled=True),
    )
    norm_one_b, in_again, conv_again, out_again, norm_two_b, gate_again, up_again, down_again = (
        regathered
    )
    gain_one = norm_one_b.astype(jnp.float32)
    gain_two = norm_two_b.astype(jnp.float32)
    taps_again = lax.dynamic_slice_in_dim(conv_again, channel_start, channels, 1).astype(
        jnp.float32
    )
    sigmoid = jax.nn.sigmoid(gate_pre)
    cotangent = lax.all_gather(out_grad, "tensor", axis=0, tiled=True)
    down_grad = jnp.einsum("tf,td->fd", activated, cotangent, preferred_element_type=jnp.float32)
    grad_act = jnp.einsum("td,fd->tf", cotangent, down_again, preferred_element_type=jnp.float32)
    grad_gate = (grad_act * upward * sigmoid * (1.0 + gate_pre * (1.0 - sigmoid))).astype(
        jnp.bfloat16
    )
    grad_up = (grad_act * gate_pre * sigmoid).astype(jnp.bfloat16)
    gate_grad = jnp.einsum("td,tf->df", normed_two, grad_gate, preferred_element_type=jnp.float32)
    up_grad = jnp.einsum("td,tf->df", normed_two, grad_up, preferred_element_type=jnp.float32)
    grad_two = lax.psum_scatter(
        (
            jnp.einsum("tf,df->td", grad_gate, gate_again, preferred_element_type=jnp.float32)
            + jnp.einsum("tf,df->td", grad_up, up_again, preferred_element_type=jnp.float32)
        ).astype(jnp.bfloat16),
        "tensor",
        scatter_dimension=0,
        tiled=True,
    ).astype(jnp.float32)
    feed_gain_part = jnp.sum(grad_two * unit_two, axis=0)
    grad_hidden = out_grad.astype(jnp.float32) + norm_back(
        grad_two, unit_two, inverse_two, gain_two
    )
    grad_mix_local = grad_hidden.astype(jnp.bfloat16)
    grad_mix = lax.all_gather(grad_mix_local, "tensor", axis=0, tiled=True)
    out_grad_part = jnp.einsum("tc,td->cd", mixer_in, grad_mix, preferred_element_type=jnp.float32)
    grad_in = jnp.einsum("td,cd->tc", grad_mix, out_again, preferred_element_type=jnp.float32)
    grad_c = grad_in * convolved
    grad_conv = grad_in * output_gate
    grad_mixed = sum(
        (
            taps_again[offset][None, :] * shift_up(tap_keep[offset][:, None] * grad_conv, offset)
            for offset in range(KW)
        )
    )
    tap_grad = jnp.stack(
        [
            jnp.sum(tap_keep[offset][:, None] * grad_conv * shift_down(mixed_input, offset), axis=0)
            for offset in range(KW)
        ]
    )
    grad_projected = jnp.stack(
        [grad_mixed * values, grad_c, grad_mixed * input_gate], axis=1
    ).astype(jnp.bfloat16)
    in_grad_part = jnp.einsum(
        "td,tkc->dkc", normed, grad_projected, preferred_element_type=jnp.float32
    )
    grad_one = lax.psum_scatter(
        jnp.einsum(
            "tkc,dkc->td", grad_projected, in_again, preferred_element_type=jnp.float32
        ).astype(jnp.bfloat16),
        "tensor",
        scatter_dimension=0,
        tiled=True,
    ).astype(jnp.float32)
    mixer_gain_part = jnp.sum(grad_one * unit_one, axis=0)
    input_grad = (grad_hidden + norm_back(grad_one, unit_one, inverse_one, gain_one)).astype(
        jnp.bfloat16
    )
    conv_part = lax.dynamic_update_slice_in_dim(
        jnp.zeros((KW, model_width), jnp.float32), tap_grad, channel_start, 1
    )
    summed = (
        lax.psum_scatter(mixer_gain_part, "dp", scatter_dimension=0, tiled=True),
        lax.psum_scatter(in_grad_part, "dp", scatter_dimension=0, tiled=True),
        lax.psum_scatter(conv_part, "dp", scatter_dimension=1, tiled=True),
        lax.psum_scatter(out_grad_part, "dp", scatter_dimension=1, tiled=True),
        lax.psum_scatter(feed_gain_part, "dp", scatter_dimension=0, tiled=True),
        lax.psum_scatter(gate_grad, "dp", scatter_dimension=0, tiled=True),
        lax.psum_scatter(up_grad, "dp", scatter_dimension=0, tiled=True),
        lax.psum_scatter(down_grad, "dp", scatter_dimension=1, tiled=True),
    )
    (
        mixer_gain_sum,
        in_weight_grad,
        conv_sum,
        out_weight_grad,
        feed_gain_sum,
        gate_weight_grad,
        up_weight_grad,
        down_weight_grad,
    ) = summed
    mixer_norm_grad, conv_weight_grad, feed_norm_grad = lax.psum(
        (mixer_gain_sum, conv_sum, feed_gain_sum), "tensor"
    )
    return (
        output,
        input_grad,
        mixer_norm_grad,
        in_weight_grad,
        conv_weight_grad,
        out_weight_grad,
        feed_norm_grad,
        gate_weight_grad,
        up_weight_grad,
        down_weight_grad,
    )


def solution(mesh):
    in_specs = (
        P(("dp", "tensor"), None),
        P("dp", None),
        P("dp"),
        P("dp", None, "tensor"),
        P(None, "dp"),
        P("tensor", "dp"),
        P("dp"),
        P("dp", "tensor"),
        P("dp", "tensor"),
        P("tensor", "dp"),
        P(("dp", "tensor"), None),
    )
    out_specs = (
        P(("dp", "tensor"), None),
        P(("dp", "tensor"), None),
        P("dp"),
        P("dp", None, "tensor"),
        P(None, "dp"),
        P("tensor", "dp"),
        P("dp"),
        P("dp", "tensor"),
        P("dp", "tensor"),
        P("tensor", "dp"),
    )
    n_dp = mesh.shape["dp"]
    fits = n_dp == 2 * NZ and mesh.shape["tensor"] == 4
    step = functools.partial(block, n_dp) if fits else body
    return jax.shard_map(step, mesh=mesh, in_specs=in_specs, out_specs=out_specs, check_vma=False)
```

```python
import functools

import jax
import jax.numpy as jnp
from jax import lax
from jax.experimental import pallas as pl
from jax.experimental.pallas import tpu as pltpu
from jax.sharding import PartitionSpec as P

KW = 3
MESH = pl.DeviceIdType.MESH
BF = jnp.bfloat16
F32 = jnp.float32

epsilon = 1e-05

NZ = 4
CONV = 4
FEED = 3
Y_LAST = (True, True, True, False)
X_FIRST = (False, False, True)
Z_FIRST = (False, False, False)
Y_FIRST = (True, True, True, True)


def nn(a, b):
    return lax.dot_general(a, b, (((1,), (0,)), ((), ())), preferred_element_type=F32)


def nt(a, b):
    return lax.dot_general(a, b, (((1,), (1,)), ((), ())), preferred_element_type=F32)


def tn(a, b):
    return lax.dot_general(a, b, (((0,), (0,)), ((), ())), preferred_element_type=F32)


class Place:
    def __init__(self):
        self.dp = lax.axis_index("dp")
        self.t = lax.axis_index("tensor")
        self.z, self.x = lax.div(self.dp, 2), lax.rem(self.dp, 2)
        self.y, self.c = lax.div(self.t, 2), lax.rem(self.t, 2)
        self.over_x = (self.z * 2 + 1 - self.x, self.t)
        self.over_y = (self.dp, (1 - self.y) * 2 + self.c)
        self.over_c = (self.dp, self.y * 2 + 1 - self.c)
        self.t_y = (1 - self.y) * 2 + self.c
        self.t_c = self.y * 2 + 1 - self.c
        self.t_yc = (1 - self.y) * 2 + 1 - self.c
        self.middle = lax.rem(lax.div(self.z + 1, 2), 2) == 1

    def zs(self, k):
        if k == 0:
            return self.z
        if k == 1:
            return self.z + 1 - 2 * lax.rem(self.z, 2)
        if k == 2:
            return lax.rem(self.z + 2, NZ)
        return NZ - 1 - self.z

    def over_z(self, k):
        return (self.zs(k) * 2 + self.x, self.t)


def greet(place, n_dp):
    barrier = pltpu.get_barrier_semaphore()
    for k in range(1, n_dp):
        peer = (lax.rem(place.dp + k, n_dp), place.t)
        pl.semaphore_signal(barrier, inc=1, device_id=peer, device_id_type=MESH)
    for peer in (place.over_c, place.over_y):
        pl.semaphore_signal(barrier, inc=1, device_id=peer, device_id_type=MESH)
    pl.semaphore_wait(barrier, n_dp + 1)


def remote(src, dst, send_sem, recv_sem, peer):
    return pltpu.make_async_remote_copy(
        src_ref=src, dst_ref=dst, send_sem=send_sem, recv_sem=recv_sem, device_id=peer, device_id_type=MESH
    )


def send(*what):
    copy = remote(*what)
    copy.start()
    return copy


def arrived(ref, sem, peer):
    pltpu.make_async_remote_copy(
        src_ref=ref, dst_ref=ref, send_sem=sem, recv_sem=sem, device_id=peer, device_id_type=MESH
    ).wait_recv()


def rows(start, size):
    return pl.ds(pl.multiple_of(start, size), size)


def forward_kernel(
    n_dp,
    tokens, cotangent, doc_rows, small, in_own, out_own, gate_own, up_own, down_own,
    conv_out, feed_out, normed_out, small_out, cot_out, proj_out, mixer_out, hidden_out, two_out, acts_out, keep_out,
    conv_w, feed_w, normed, small_all, mixed_pad, c_keep, proj, mixer_in, part_send, part_recv,
    hidden, two, acts, out_turned, down_turned, keep,
    own_sem, z_send, z_recv, x_send, x_recv, y_send, y_recv, fz_send, fz_recv, fx_send, fx_recv,
    s_send, s_recv, a_send, a_recv, out_sem,
):
    place = Place()
    z, x, y, c, t = place.z, place.x, place.y, place.c, place.t
    depth = gate_own.shape[0]
    local, width = tokens.shape
    chip = 2 * local
    half = in_own.shape[2]
    mine = 2 * half
    tile, pad = 256, 8
    blocks = (t, place.t_c, place.t_y, place.t_yc)
    sends = []
    copies = []
    owned = {}

    def post(make, when=None):
        if when is None:
            make().start()
        else:
            pl.when(when)(lambda: make().start())
        sends.append((make, when))

    def keep_own(src, dst, index):
        owned[index] = pltpu.make_async_copy(src, dst, own_sem.at[index])
        owned[index].start()

    def out(src, dst):
        copy = pltpu.make_async_copy(src, dst, out_sem.at[len(copies)])
        copy.start()
        copies.append(copy)

    def conv_part(j, dp, n, side):
        col = slice(None) if side is None else rows(side * half, half)
        return conv_w.at[j, rows(dp * depth, n * depth), col]

    def feed_part(w, dp, n=1):
        return feed_w.at[w, rows(dp * depth, n * depth), :]

    conv_own = [in_own.at[0], in_own.at[1], in_own.at[2], out_turned]
    feed_own = [gate_own, up_own, down_turned]

    def along_z(src, part, send_sems, recv_sems, index):
        for k in (2, 3, 1):
            post(lambda k=k: remote(src, part(z), send_sems.at[index, k], recv_sems.at[index, z], place.over_z(k)),
                 place.middle if k == 3 else None)

    def from_z(part, send_sems, recv_sems, index, k):
        zk = place.zs(k)
        arrived(part(zk), recv_sems.at[index, zk], place.over_z(k))
        if k == 2:
            post(lambda: remote(part(zk), part(zk), send_sems.at[index, 0], recv_sems.at[index, zk], place.over_z(1)), place.middle)

    def conv_z(j):
        return lambda zk: conv_part(j, zk * 2 + x, 1, y)

    def feed_z(w):
        if X_FIRST[w]:
            return lambda zk: feed_part(w, zk * 2, 2)
        return lambda zk: feed_part(w, zk * 2 + x)

    def conv_second(j, k, src=None):
        zk = place.zs(k)
        part = conv_part(j, zk * 2 + x, 1, y)
        src = part if src is None else src
        if Y_LAST[j]:
            post(lambda: remote(src, part, x_send.at[j, zk], x_recv.at[j, zk], place.over_x))
        else:
            post(lambda: remote(src, part, y_send.at[j, zk], y_recv.at[j, zk], place.over_y))

    def feed_x(w, k, src=None):
        zk = place.zs(k)
        part = feed_part(w, zk * 2 + x)
        src = part if src is None else src
        post(lambda: remote(src, part, fx_send.at[w, zk], fx_recv.at[w, zk], place.over_x))

    def cown(j):
        along_z(conv_own[j], conv_z(j), z_send, z_recv, j)
        conv_second(j, 0, conv_own[j])

    def cz(j, k):
        from_z(conv_z(j), z_send, z_recv, j, k)
        conv_second(j, k)

    def ct(j, k):
        zk = place.zs(k)
        if k == 0:
            owned[j].wait()
        if Y_LAST[j]:
            arrived(conv_part(j, zk * 2 + 1 - x, 1, y), x_recv.at[j, zk], place.over_x)
            pair = conv_part(j, zk * 2, 2, y)
            post(lambda: remote(pair, pair, y_send.at[j, zk], y_recv.at[j, zk], place.over_y))
        else:
            arrived(conv_part(j, zk * 2 + x, 1, 1 - y), y_recv.at[j, zk], place.over_y)
            pair = conv_part(j, zk * 2 + x, 1, None)
            post(lambda: remote(pair, pair, x_send.at[j, zk], x_recv.at[j, zk], place.over_x))

    def fx(w):
        feed_x(w, 0, feed_own[w])

    def fz(w):
        if X_FIRST[w]:
            arrived(feed_part(w, z * 2 + 1 - x), fx_recv.at[w, z], place.over_x)
            owned[CONV + w].wait()
            along_z(feed_part(w, z * 2, 2), feed_z(w), fz_send, fz_recv, w)
        else:
            along_z(feed_own[w], feed_z(w), fz_send, fz_recv, w)

    def fp(w, k):
        from_z(feed_z(w), fz_send, fz_recv, w, k)
        if not X_FIRST[w]:
            feed_x(w, k)

    def feed_ready(w):
        if not X_FIRST[w]:
            for k in range(NZ):
                zk = place.zs(k)
                arrived(feed_part(w, zk * 2 + 1 - x), fx_recv.at[w, zk], place.over_x)
            owned[CONV + w].wait()
        out(feed_w.at[w], feed_out.at[w])

    def cot_block(block):
        return cot_out.at[rows(block * local, local), :]

    def cotc():
        post(lambda: remote(cotangent, cot_block(t), a_send.at[0], a_recv.at[0], place.over_c))

    def coty():
        post(lambda: remote(cotangent, cot_block(t), a_send.at[2], a_recv.at[2], place.over_y))

    def cotf():
        there = cot_block(place.t_y)
        arrived(there, a_recv.at[2], place.over_y)
        post(lambda: remote(there, there, a_send.at[6], a_recv.at[6], place.over_c))

    def turn():
        down_turned[...] = jnp.transpose(down_own[...])
        for w in range(FEED):
            keep_own(feed_own[w], feed_part(w, place.dp), CONV + w)
        own = doc_rows[pl.ds(y, 1), :].astype(F32)
        position = lax.broadcasted_iota(jnp.int32, (1, chip), 1)
        for k in range(1, KW):
            same = jnp.where((own == pltpu.roll(own, k, 1)) & (position >= k), 1.0, 0.0)
            keep[k - 1, 0:chip, :] = jnp.transpose(jnp.broadcast_to(same, (128, chip)))
            keep[k - 1, chip : chip + pad, :] = jnp.zeros((pad, 128), F32)
        out(keep, keep_out)

    def gain(r):
        return jnp.concatenate([small_all[d, r : r + 1, :] for d in range(n_dp)], axis=1)

    def norm():
        for k in range(1, n_dp):
            peer = lax.rem(place.dp + k, n_dp)
            arrived(small_all.at[peer], s_recv.at[peer], (peer, t))
        inputs = tokens[...].astype(F32)
        inverse = lax.rsqrt(jnp.mean(inputs * inputs, axis=-1, keepdims=True) + epsilon)
        normed[rows(c * local, local), :] = (inputs * inverse * gain(0)).astype(BF)
        own = normed.at[rows(c * local, local), :]
        post(lambda: remote(own, own, a_send.at[1], a_recv.at[1], place.over_c))

    def p1():
        arrived(normed.at[rows((1 - c) * local, local), :], a_recv.at[1], place.over_c)
        for j in range(CONV):
            for k in range(NZ):
                zk = place.zs(k)
                if Y_LAST[j]:
                    arrived(conv_part(j, zk * 2, 2, 1 - y), y_recv.at[j, zk], place.over_y)
                else:
                    arrived(conv_part(j, zk * 2 + 1 - x, 1, None), x_recv.at[j, zk], place.over_x)
        out(conv_w, conv_out)
        out(normed, normed_out)
        mixed_pad[0:pad, :] = jnp.zeros((pad, mine), F32)

        def project(i, carry):
            at = rows(i * tile, tile)
            lhs = normed[at, :]
            b = nn(lhs, conv_w[0])
            proj[0, at, :] = b.astype(BF)
            v = nn(lhs, conv_w[2])
            proj[2, at, :] = v.astype(BF)
            mixed_pad[pl.ds(pl.multiple_of(i * tile + pad, 8), tile), :] = b * v
            g = nn(lhs, conv_w[1])
            proj[1, at, :] = g.astype(BF)
            c_keep[at, :] = g
            return carry

        lax.fori_loop(0, chip // tile, project, 0)

    def p2():
        taps = []
        for r in range(2, 2 + KW):
            taps.append(jnp.concatenate(
                [small_all[side * 4 + 2 * c + i, r : r + 1, :] for side in range(2) for i in range(2)], axis=1))

        def convolve(i, carry):
            at = rows(i * tile, tile)
            window = mixed_pad[pl.ds(pl.multiple_of(i * tile, 8), tile + pad), :]
            total = taps[0] * window[pad:, :]
            for k in range(1, KW):
                mask = jnp.concatenate([keep[k - 1, at, :]] * (mine // 128), axis=1)
                total = total + mask * taps[k] * window[pad - k : pad - k + tile, :]
            proj[3, at, :] = total.astype(BF)
            mixer_in[at, :] = (c_keep[at, :] * total).astype(BF)
            return carry

        lax.fori_loop(0, chip // tile, convolve, 0)
        out(proj, proj_out)
        out(mixer_in, mixer_out)
        part_send[...] = nt(mixer_in[rows((1 - c) * local, local), :], conv_w[3]).astype(BF)
        post(lambda: remote(part_send, part_recv, a_send.at[3], a_recv.at[3], place.over_c))
        hidden[...] = tokens[...].astype(F32) + nt(mixer_in[rows(c * local, local), :], conv_w[3])

    def p3():
        arrived(part_recv, a_recv.at[3], place.over_c)
        total = hidden[...] + part_recv[...].astype(F32)
        hidden[...] = total
        inverse = lax.rsqrt(jnp.mean(total * total, axis=-1, keepdims=True) + epsilon)
        two[rows(t * local, local), :] = (total * inverse * gain(1)).astype(BF)
        own = two.at[rows(t * local, local), :]
        post(lambda: remote(own, own, a_send.at[5], a_recv.at[5], place.over_y))
        post(lambda: remote(own, own, a_send.at[4], a_recv.at[4], place.over_c))
        out(hidden, hidden_out)

    def t2():
        there = two.at[rows(place.t_y * local, local), :]
        arrived(there, a_recv.at[5], place.over_y)
        post(lambda: remote(there, there, a_send.at[7], a_recv.at[7], place.over_c))

    def g(b):
        if b == 0:
            feed_ready(0)
        if b == 1:
            arrived(two.at[rows(place.t_c * local, local), :], a_recv.at[4], place.over_c)
        if b == 3:
            arrived(two.at[rows(place.t_yc * local, local), :], a_recv.at[7], place.over_c)

        def step(i, carry):
            at = rows(blocks[b] * local + i * tile, tile)
            gate = nn(two[at, :], feed_w[0])
            s = jax.nn.sigmoid(gate)
            silu = gate * s
            acts[1, at, :] = (s + silu * (1.0 - s)).astype(BF)
            acts[2, at, :] = silu.astype(BF)
            return carry

        lax.fori_loop(0, local // tile, step, 0)

    def u(b):
        if b == 0:
            feed_ready(1)

        def step(i, carry):
            at = rows(blocks[b] * local + i * tile, tile)
            upward = nn(two[at, :], feed_w[1])
            acts[0, at, :] = (acts[2, at, :].astype(F32) * upward).astype(BF)
            acts[1, at, :] = (acts[1, at, :].astype(F32) * upward).astype(BF)
            return carry

        lax.fori_loop(0, local // tile, step, 0)
        at = rows(blocks[b] * local, local)
        out(acts.at[:, at, :], acts_out.at[:, at, :])
        out(two.at[at, :], two_out.at[at, :])

    small_all[place.dp] = small[...]
    out_turned[...] = jnp.transpose(out_own[...])
    greet(place, n_dp)
    for k in range(1, n_dp):
        post(lambda k=k: remote(small, small_all.at[place.dp], s_send.at[k], s_recv.at[place.dp], (lax.rem(place.dp + k, n_dp), t)))
    for j in range(CONV):
        keep_own(conv_own[j], conv_part(j, place.dp, 1, y), j)
    keep_own(cotangent, cot_block(t), CONV + FEED)
    cown(1)
    cown(3)
    cown(0)
    fx(0)
    ct(1, 0)
    cz(1, 2)
    ct(0, 0)
    cown(2)
    cz(3, 2)
    cz(3, 1)
    cz(1, 1)
    cz(1, 3)
    ct(1, 2)
    turn()
    cz(0, 2)
    cz(3, 3)
    cz(0, 1)
    ct(1, 3)
    cz(2, 2)
    fz(0)
    ct(2, 0)
    ct(3, 2)
    cz(2, 1)
    fx(2)
    fz(1)
    cz(2, 3)
    cz(0, 3)
    ct(0, 2)
    norm()
    ct(1, 1)
    ct(2, 1)
    ct(0, 1)
    ct(3, 0)
    ct(2, 3)
    ct(3, 1)
    ct(2, 2)
    ct(3, 3)
    ct(0, 3)
    cotc()
    fp(0, 1)
    coty()
    fp(0, 2)
    p1()
    fp(1, 2)
    fp(1, 1)
    fp(0, 3)
    fz(2)
    p2()
    p3()
    fp(1, 3)
    cotf()
    g(0)
    fx(1)
    fp(2, 2)
    g(1)
    u(0)
    u(1)
    t2()
    g(2)
    u(2)
    fp(2, 1)
    g(3)
    u(3)
    fp(2, 3)
    feed_ready(2)
    small_out[...] = small_all[...]
    arrived(cot_block(place.t_c), a_recv.at[0], place.over_c)
    arrived(cot_block(place.t_yc), a_recv.at[6], place.over_c)
    owned[CONV + FEED].wait()
    for make, when in sends:
        if when is None:
            make().wait_send()
        else:
            pl.when(when)(lambda make=make: make().wait_send())
    for copy in copies:
        copy.wait()


def forward_call(n_dp, *operands):
    tokens, _, _, _, in_own, _, gate_own, _, _ = operands
    local, width = tokens.shape
    half, units = in_own.shape[2], gate_own.shape[1]
    chip, group, mine = 2 * local, 4 * local, 2 * half

    def shaped(dims, kind=BF):
        return jax.ShapeDtypeStruct(dims, kind)

    dma = pltpu.SemaphoreType.DMA
    vmem, any_space = pl.BlockSpec(memory_space=pltpu.VMEM), pl.BlockSpec(memory_space=pl.ANY)
    return pl.pallas_call(
        functools.partial(forward_kernel, n_dp),
        name="gather_forward",
        out_shape=(
            shaped((CONV, width, mine)), shaped((FEED, width, units)), shaped((chip, width)), shaped((n_dp, 8, 128), F32),
            shaped((group, width)), shaped((4, chip, mine)), shaped((chip, mine)), shaped((local, width), F32),
            shaped((group, width)), shaped((3, group, units)), shaped((KW - 1, chip + 8, 128), F32),
        ),
        in_specs=[vmem] * 4 + [any_space, vmem, any_space, any_space, vmem],
        out_specs=tuple(vmem if i == 3 else any_space for i in range(11)),
        scratch_shapes=[
            pltpu.VMEM((CONV, width, mine), BF), pltpu.VMEM((FEED, width, units), BF), pltpu.VMEM((chip, width), BF),
            pltpu.VMEM((n_dp, 8, 128), F32), pltpu.VMEM((chip + 8, mine), F32),
            pltpu.VMEM((chip, mine), F32), pltpu.VMEM((4, chip, mine), BF), pltpu.VMEM((chip, mine), BF),
            pltpu.VMEM((local, width), BF), pltpu.VMEM((local, width), BF), pltpu.VMEM((local, width), F32),
            pltpu.VMEM((group, width), BF), pltpu.VMEM((3, group, units), BF),
            pltpu.VMEM((width // n_dp, half), BF), pltpu.VMEM((width // n_dp, units), BF), pltpu.VMEM((KW - 1, chip + 8, 128), F32),
            dma((8,)), dma((CONV, NZ)), dma((CONV, NZ)), dma((CONV, NZ)), dma((CONV, NZ)), dma((CONV, NZ)), dma((CONV, NZ)),
            dma((FEED, NZ)), dma((FEED, NZ)), dma((FEED, NZ)), dma((FEED, NZ)),
            dma((n_dp,)), dma((n_dp,)), dma((8,)), dma((8,)), dma((20,)),
        ],
        compiler_params=pltpu.CompilerParams(collective_id=0, has_side_effects=True, vmem_limit_bytes=62 << 20),
    )(*operands)


def backward_kernel(
    n_dp,
    small_all, tokens_in, cot_own_in, keep_in, conv_in, feed_in, normed_in, cot_in, proj_in, mixer_in_hbm, hidden_in, two_in, acts_in,
    output, input_grad, in_grad, out_grad, gate_grad, up_grad, down_grad, small_grad,
    act, g_down, x_got, z_got, c_got_y, c_got_x, c_two, c_z, two_send, two_recv, two_y, own_two,
    down_send, down_recv, down_y, down_own, grad_mix, hidden, token_rows, feed_gain, small_sum, small_got, small_z,
    load_sem, fx_send, fx_recv, fz_send, fz_recv, c1_send, c1_recv, c2_send, c2_recv, c3_send, c3_recv,
    s_send, s_recv, a_send, a_recv,
):
    place = Place()
    z, x, y, c, t = place.z, place.x, place.y, place.c, place.t
    depth, units = gate_grad.shape
    local, width = own_two.shape
    chip = 2 * local
    half = in_grad.shape[2]
    mine = 2 * half
    tile = 256
    sends = []

    def post(make):
        make().start()
        sends.append(make)
        return make

    def load(src, dst, index):
        copy = pltpu.make_async_copy(src, dst, load_sem.at[index])
        copy.start()
        return copy

    def g_rows(w, start, size):
        if w == 2:
            return g_down.at[rows(start, size), :]
        return act.at[rows(w * width + start, size), :]

    def m(w, k):
        zk = place.zs(k)
        got = x_got.at[w, zk]
        arrived(got, fx_recv.at[w, zk], place.over_x)
        if k:
            got[...] = (g_rows(w, (zk * 2 + x) * depth, depth)[...].astype(F32) + got[...].astype(F32)).astype(BF)

            def add(more):
                held = x_got.at[w, place.zs(k)]
                held[...] = (held[...].astype(F32) + more[...].astype(F32)).astype(BF)

            if k == 2:
                @pl.when(place.middle)
                def _():
                    arrived(z_got.at[w, 0], fz_recv.at[w, 0], place.over_z(1))
                    add(z_got.at[w, 0])

            post(lambda: z_remote(x_got.at[w, place.zs(k)], z_got.at[w], fz_send.at[w], fz_recv.at[w], k))

    def z_remote(held, got, sends_at, recvs_at, k):
        if k == 3:
            slot = jnp.where(place.middle, 3, 0)
            peer = (jnp.where(place.middle, place.zs(3), place.zs(1)) * 2 + x, t)
            return remote(held, got.at[slot], sends_at.at[k], recvs_at.at[slot], peer)
        return remote(held, got.at[k], sends_at.at[k], recvs_at.at[k], place.over_z(k))

    def z_sum(total, got, recvs_at):
        for k in (1, 2):
            arrived(got.at[k], recvs_at.at[k], place.over_z(k))
            total = total + got[k].astype(F32)
        return total

    def z_last(ref, got, recvs_at):
        @pl.when(place.middle)
        def _():
            arrived(got.at[3], recvs_at.at[3], place.over_z(3))
            ref[...] = ref[...] + got[3].astype(F32)

    def gain(r):
        return jnp.concatenate([small_all[d, r : r + 1, :] for d in range(n_dp)], axis=1)

    def norm_back(grad, unit, inverse, scale):
        scaled = grad * scale
        return inverse * (scaled - unit * jnp.mean(scaled * unit, axis=-1, keepdims=True))

    def rms(values):
        return lax.rsqrt(jnp.mean(values * values, axis=-1, keepdims=True) + epsilon)

    def send_slot(i):
        return lambda: remote(two_send.at[i], two_recv.at[i], a_send.at[1 + i], a_recv.at[1 + i], place.over_c)

    first_slot = send_slot(0)

    def fetch_hidden():
        return pltpu.make_async_copy(hidden_in, hidden, load_sem.at[9])

    def fetch_cotangent():
        return pltpu.make_async_copy(cot_own_in, token_rows, load_sem.at[10])

    def fetch_tokens():
        return pltpu.make_async_copy(tokens_in, token_rows, load_sem.at[11])

    def n2():
        fetch_hidden().wait()
        fetch_cotangent().wait()
        arrived(two_y, a_recv.at[3], place.over_y)
        arrived(two_recv.at[1], a_recv.at[2], place.over_c)
        scale = gain(1)

        def step(i, carry):
            at = rows(i * 128, 128)
            grad_two = own_two[at, :] + two_recv[1, at, :].astype(F32) + two_y[at, :].astype(F32)
            values = hidden[at, :]
            inverse = rms(values)
            unit = values * inverse
            grad_hidden = token_rows[at, :].astype(F32) + norm_back(grad_two, unit, inverse, scale)
            hidden[at, :] = grad_hidden
            grad_mix[rows(c * local + i * 128, 128), :] = grad_hidden.astype(BF)
            return carry + jnp.sum(grad_two * unit, axis=0, keepdims=True)

        feed_gain[0:1, :] = lax.fori_loop(0, local // 128, step, jnp.zeros((1, width), F32))
        fetch_tokens().start()

        def make():
            own = grad_mix.at[rows(c * local, local), :]
            return remote(own, own, a_send.at[4], a_recv.at[4], place.over_c)

        post(make)

    def feed_phase(feed_w, cot, acts):
        loads = [load(acts_in.at[0], act, 0), load(cot_in, cot, 1), load(feed_in, feed_w, 2),
                 load(acts_in.at[1], acts.at[0], 3), load(acts_in.at[2], acts.at[1], 4)]
        fetch_hidden().start()
        fetch_cotangent().start()
        greet(place, n_dp)
        waited = set()

        def loaded(*which):
            for i in which:
                if i not in waited:
                    waited.add(i)
                    loads[i].wait()

        def g(w, k):
            at = rows(place.zs(k) * 2 * depth, 2 * depth)
            if w == 2:
                loaded(0, 1)
                g_down[at, :] = tn(cot[:, at], act[...]).astype(BF)
            else:
                if 5 not in waited:
                    loads.append(load(two_in, cot, 5))
                    loaded(5)
                act[rows(w * width + place.zs(k) * 2 * depth, 2 * depth), :] = tn(cot[:, at], acts[w]).astype(BF)

            def make():
                zk = place.zs(k)
                return remote(g_rows(w, (zk * 2 + 1 - x) * depth, depth), x_got.at[w, zk], fx_send.at[w, zk], fx_recv.at[w, zk], place.over_x)

            post(make)

        def back(block, store):
            loaded(1, 2, 3, 4)

            def step(i, carry):
                at = rows(block * local + i * tile, tile)
                grad_act = nn(cot[at, :], feed_w[2])
                grad_gate = (grad_act * acts[0, at, :].astype(F32)).astype(BF)
                acts[0, at, :] = grad_gate
                grad_up = (grad_act * acts[1, at, :].astype(F32)).astype(BF)
                acts[1, at, :] = grad_up
                store(rows(i * tile, tile), nt(grad_gate, feed_w[0]) + nt(grad_up, feed_w[1]))
                return carry

            lax.fori_loop(0, local // tile, step, 0)

        def to_slot(i):
            def store(at, value):
                two_send[i, at, :] = value.astype(BF)

            return store

        def to_own(at, value):
            own_two[at, :] = value

        def a_yc():
            back(place.t_yc, to_slot(0))
            post(first_slot)

        def a_c():
            back(place.t_c, to_slot(1))
            post(send_slot(1))

        def a_y():
            back(place.t_y, to_own)

        def ay():
            arrived(two_recv.at[0], a_recv.at[1], place.over_c)
            two_recv[0] = (own_two[...] + two_recv[0].astype(F32)).astype(BF)
            post(lambda: remote(two_recv.at[0], two_y, a_send.at[3], a_recv.at[3], place.over_y))

        def a_o():
            back(t, to_own)

        def down(block):
            loaded(0, 2)
            return nt(act[rows(block * local, local), :], feed_w[2]).astype(BF)

        def d_yc():
            down_send[0] = down(place.t_yc)
            post(lambda: remote(down_send.at[0], down_recv.at[0], a_send.at[6], a_recv.at[6], place.over_c))

        def d_c():
            down_send[1] = down(place.t_c)
            post(lambda: remote(down_send.at[1], down_recv.at[1], a_send.at[7], a_recv.at[7], place.over_c))

        def d_y():
            down_own[...] = down(place.t_y)

        def dy():
            arrived(down_recv.at[0], a_recv.at[6], place.over_c)
            down_recv[0] = (down_own[...].astype(F32) + down_recv[0].astype(F32)).astype(BF)
            post(lambda: remote(down_recv.at[0], down_y, a_send.at[8], a_recv.at[8], place.over_y))

        def d_o():
            down_own[...] = down(t)

        d_yc()
        d_y()
        a_yc()
        g(2, 3)
        a_y()
        ay()
        g(2, 0)
        g(2, 1)
        g(2, 2)
        m(2, 3)
        a_o()
        a_c()
        dy()
        d_o()
        d_c()
        g(0, 2)
        m(2, 2)
        m(2, 0)
        g(0, 3)
        g(1, 3)
        g(1, 1)
        g(1, 2)
        g(0, 1)
        m(2, 1)
        n2()
        g(1, 0)
        g(0, 0)

    pl.run_scoped(
        feed_phase,
        pltpu.VMEM((FEED, width, units), BF), pltpu.VMEM((4 * local, width), BF), pltpu.VMEM((2, 4 * local, units), BF),
    )

    def conv_phase(conv_w, proj, normed, mixer_in, grad_proj, pad_grad, tap_sum, g_conv, keep, stage):
        loads = [load(conv_in.at[3], conv_w.at[3], 2), load(mixer_in_hbm, mixer_in, 3),
                 load(proj_in, proj, 4), load(normed_in, normed, 5), load(conv_in.at[pl.ds(0, 3)], conv_w.at[pl.ds(0, 3)], 6),
                 load(keep_in, keep, 7)]
        waited = set()

        def loaded(*which):
            for i in which:
                if i not in waited:
                    waited.add(i)
                    loads[i - 2].wait()

        def taps():
            return [jnp.concatenate([small_all[side * 4 + 2 * c + i, r : r + 1, :] for side in range(2) for i in range(2)], axis=1)
                    for r in range(2, 2 + KW)]

        def gm():
            loaded(2, 4)
            arrived(grad_mix.at[rows((1 - c) * local, local), :], a_recv.at[4], place.over_c)
            pad_grad[pl.ds(chip, 8), :] = jnp.zeros((8, mine), F32)

            def step(i, carry):
                at = rows(i * tile, tile)
                grad_in = nn(grad_mix[at, :], conv_w[3])
                grad_proj[1, at, :] = (grad_in * proj[3, at, :].astype(F32)).astype(BF)
                pad_grad[at, :] = grad_in * proj[1, at, :].astype(F32)
                return carry

            lax.fori_loop(0, chip // tile, step, 0)

        def c1_slot(j, zk):
            if Y_FIRST[j]:
                return c_got_y.at[sum(Y_FIRST[:j]), zk]
            return c_got_x.at[j - sum(Y_FIRST[:j]), zk]

        def w(j):
            if j == 3:
                loaded(3)
                g_conv[j] = tn(grad_mix[...], mixer_in[...]).astype(BF)
            else:
                loaded(5)
                g_conv[j] = tn(normed[...], grad_proj[j]).astype(BF)
            for k in (2, 1, 3, 0):
                zk = place.zs(k)
                if Y_FIRST[j]:
                    src, peer = g_conv.at[j, rows(zk * 2 * depth, 2 * depth), rows((1 - y) * half, half)], place.over_y
                else:
                    src, peer = g_conv.at[j, rows((zk * 2 + 1 - x) * depth, depth), :], place.over_x
                post(lambda src=src, peer=peer, zk=zk: remote(src, c1_slot(j, zk), c1_send.at[j, zk], c1_recv.at[j, zk], peer))

        def h2():
            loaded(4, 7)
            tap = taps()
            tap_sum[...] = jnp.zeros_like(tap_sum)
            size = 128

            def step(i, carry):
                at = rows(i * size, size)
                wide = pl.ds(pl.multiple_of(i * size, 8), size + 8)
                window = pad_grad[wide, :]
                b, v = proj[0, at, :].astype(F32), proj[2, at, :].astype(F32)
                mixed = b * v
                now = window[:size, :]
                total = tap[0] * now
                tap_sum[0:1, :] += jnp.sum(now * mixed, axis=0, keepdims=True)
                for k in range(1, KW):
                    mask = jnp.concatenate([keep[k - 1, wide, :]] * (mine // 128), axis=1)
                    ahead = (mask * window)[k : k + size, :]
                    total = total + tap[k] * ahead
                    tap_sum[k : k + 1, :] += jnp.sum(ahead * mixed, axis=0, keepdims=True)
                grad_proj[0, at, :] = (total * v).astype(BF)
                grad_proj[2, at, :] = (total * b).astype(BF)
                return carry

            lax.fori_loop(0, chip // size, step, 0)

        def first_grad(block):
            at = rows(block * local, local)
            return nt(grad_proj[0, at, :], conv_w[0]) + nt(grad_proj[1, at, :], conv_w[1]) + nt(grad_proj[2, at, :], conv_w[2])

        def f1():
            loaded(6)
            first_slot().wait_send()
            sends.remove(first_slot)
            two_send[0] = first_grad(1 - c).astype(BF)
            post(lambda: remote(two_send.at[0], two_recv.at[1], a_send.at[5], a_recv.at[5], place.over_c))
            own_two[...] = first_grad(c)

        def n1():
            fetch_tokens().wait()
            arrived(two_recv.at[1], a_recv.at[5], place.over_c)
            scale = gain(0)

            def step(i, carry):
                at = rows(i * 128, 128)
                grad_one = own_two[at, :] + two_recv[1, at, :].astype(F32)
                values = token_rows[at, :].astype(F32)
                inverse = rms(values)
                unit = values * inverse
                two_recv[1, at, :] = (hidden[at, :] + norm_back(grad_one, unit, inverse, scale)).astype(BF)
                return carry + jnp.sum(grad_one * unit, axis=0, keepdims=True)

            mixer_gain = lax.fori_loop(0, local // 128, step, jnp.zeros((1, width), F32))
            loads.append(load(two_recv.at[1], input_grad, 1))
            loads.append(load(hidden_in, own_two, 0))
            zero = jnp.zeros((1, 128), F32)
            for d in range(n_dp):
                cols = slice(d * 128, d * 128 + 128)
                here = (c == (d % 4) // 2).astype(F32)
                own = (d // 4) * half + (d % 2) * 128
                small_sum[d] = jnp.concatenate(
                    [mixer_gain[:, cols], feed_gain[0:1, cols]]
                    + [here * tap_sum[k : k + 1, own : own + 128] for k in range(KW)] + [zero] * 3, axis=0)

        def c2(j, k):
            zk = place.zs(k)
            got = c1_slot(j, zk)
            if Y_FIRST[j]:
                arrived(got, c1_recv.at[j, zk], place.over_y)
                held = g_conv[j, rows(zk * 2 * depth, 2 * depth), rows(y * half, half)]
                src, peer = got.at[rows((1 - x) * depth, depth), :], place.over_x
            else:
                arrived(got, c1_recv.at[j, zk], place.over_x)
                held = g_conv[j, rows((zk * 2 + x) * depth, depth), :]
                src, peer = got.at[:, rows((1 - y) * half, half)], place.over_y
            got[...] = (held.astype(F32) + got[...].astype(F32)).astype(BF)
            post(lambda: remote(src, c_two.at[j, zk], c2_send.at[j, zk], c2_recv.at[j, zk], peer))

        def held_half(j, zk):
            if Y_FIRST[j]:
                return c1_slot(j, zk)[rows(x * depth, depth), :].astype(F32)
            return c1_slot(j, zk)[:, rows(y * half, half)].astype(F32)

        def c3(j, k):
            zk = place.zs(k)
            got = c_two.at[j, zk]
            arrived(got, c2_recv.at[j, zk], place.over_x if Y_FIRST[j] else place.over_y)
            if k:
                got[...] = (held_half(j, zk) + got[...].astype(F32)).astype(BF)
                if k == 2:
                    @pl.when(place.middle)
                    def _():
                        arrived(c_z.at[j, 0], c3_recv.at[j, 0], place.over_z(1))
                        got[...] = (got[...].astype(F32) + c_z[j, 0].astype(F32)).astype(BF)

                post(lambda: z_remote(got, c_z.at[j], c3_send.at[j], c3_recv.at[j], k))

        def cf(j):
            total = z_sum(held_half(j, z) + c_two[j, z].astype(F32), c_z.at[j], c3_recv.at[j])
            if j == 3:
                stage[0:depth, 0:half] = total
                ref = stage.at[0:depth, 0:half]
                z_last(ref, c_z.at[j], c3_recv.at[j])
                out_grad[...] = jnp.transpose(ref[...])
            else:
                in_grad[j] = total
                z_last(in_grad.at[j], c_z.at[j], c3_recv.at[j])

        def ff(w):
            total = g_rows(w, (z * 2 + x) * depth, depth)[...].astype(F32) + x_got[w, z].astype(F32)
            total = z_sum(total, z_got.at[w], fz_recv.at[w])
            ref = (gate_grad, up_grad, stage)[w]
            ref[...] = total
            z_last(ref, z_got.at[w], fz_recv.at[w])
            if w == 2:
                down_grad[...] = jnp.transpose(stage[...])

        def do():
            loads[-1].wait()
            arrived(down_recv.at[1], a_recv.at[7], place.over_c)
            arrived(down_y, a_recv.at[8], place.over_y)
            total = own_two[...] + down_own[...].astype(F32) + down_recv[1].astype(F32) + down_y[...].astype(F32)
            down_own[...] = total.astype(BF)
            loads.append(load(down_own, output, 2))

        def s0():
            post(lambda: remote(small_sum, small_got.at[0], s_send.at[0], s_recv.at[0], place.over_c))

        def s1():
            arrived(small_got.at[0], s_recv.at[0], place.over_c)
            small_got[0] = small_sum[...] + small_got[0]
            post(lambda: remote(small_got.at[0], small_got.at[1], s_send.at[1], s_recv.at[1], place.over_y))

        def s2():
            arrived(small_got.at[1], s_recv.at[1], place.over_y)
            small_got[1] = small_got[0] + small_got[1]
            for k in range(NZ):
                zk = place.zs(k)
                post(lambda zk=zk, k=k: remote(
                    small_got.at[1, zk * 2 + 1 - x], small_z.at[zk], s_send.at[2 + k], s_recv.at[2 + zk], place.over_x))

        def s3():
            for k in range(NZ):
                zk = place.zs(k)
                arrived(small_z.at[zk], s_recv.at[2 + zk], place.over_x)
                small_z[zk] = small_z[zk] + small_got[1, zk * 2 + x]
                if k:
                    post(lambda zk=zk, k=k: remote(small_z.at[zk], small_z.at[NZ + k], s_send.at[6 + k], s_recv.at[6 + k], place.over_z(k)))

        def s4():
            total = small_z[z]
            for k in range(1, NZ):
                arrived(small_z.at[NZ + k], s_recv.at[6 + k], place.over_z(k))
                total = total + small_z[NZ + k]
            small_grad[...] = total

        gm()
        m(1, 3)
        w(3)
        h2()
        m(1, 1)
        m(0, 3)
        m(1, 2)
        w(1)
        w(2)
        m(0, 1)
        f1()
        m(1, 0)
        m(0, 2)
        c2(1, 2)
        c2(3, 1)
        n1()
        m(0, 0)
        c2(3, 2)
        c2(1, 0)
        c2(1, 3)
        c2(2, 1)
        w(0)
        c2(2, 3)
        c2(2, 2)
        c2(3, 0)
        do()
        c3(1, 3)
        c2(3, 3)
        c3(2, 1)
        c3(2, 3)
        s0()
        c3(2, 2)
        c3(1, 2)
        c2(1, 1)
        c3(3, 3)
        c2(2, 0)
        c3(1, 0)
        ff(1)
        c3(3, 0)
        c2(0, 1)
        c2(0, 3)
        c2(0, 2)
        s1()
        c3(3, 2)
        c3(3, 1)
        c3(2, 0)
        ff(0)
        s2()
        c3(0, 3)
        c3(0, 1)
        c3(1, 1)
        ff(2)
        s3()
        c3(0, 2)
        c2(0, 0)
        cf(3)
        cf(2)
        cf(1)
        s4()
        c3(0, 0)
        cf(0)
        for make in sends:
            make().wait_send()
        loads[-3].wait()
        loads[-1].wait()

    pl.run_scoped(
        conv_phase,
        pltpu.VMEM((CONV, width, mine), BF), pltpu.VMEM((4, chip, mine), BF), pltpu.VMEM((chip, width), BF),
        pltpu.VMEM((chip, mine), BF), pltpu.VMEM((3, chip, mine), BF), pltpu.VMEM((chip + 8, mine), F32), pltpu.VMEM((8, mine), F32),
        pltpu.VMEM((CONV, width, mine), BF),
        pltpu.VMEM((KW - 1, chip + 8, 128), F32), pltpu.VMEM((depth, units), F32),
    )


def backward_call(n_dp, small_all, tokens, cotangent, keep, conv_w, feed_w, *rest):
    local, width = tokens.shape
    units, mine = feed_w.shape[2], conv_w.shape[2]
    chip, half, depth = 2 * local, mine // 2, width // n_dp
    over_y = sum(Y_FIRST)

    def shaped(dims, kind=BF):
        return jax.ShapeDtypeStruct(dims, kind)

    def slots(n, *dims):
        return pltpu.VMEM((max(n, 1), *(dims if n else (NZ, 16, 128))), BF)

    dma = pltpu.SemaphoreType.DMA
    vmem, any_space = pl.BlockSpec(memory_space=pltpu.VMEM), pl.BlockSpec(memory_space=pl.ANY)
    return pl.pallas_call(
        functools.partial(backward_kernel, n_dp),
        name="backward_scatter",
        out_shape=(
            shaped((local, width)), shaped((local, width)), shaped((3, depth, half), F32), shaped((half, depth), F32),
            shaped((depth, units), F32), shaped((depth, units), F32), shaped((units, depth), F32), shaped((8, 128), F32),
        ),
        in_specs=[vmem] + [any_space] * (5 + len(rest)),
        out_specs=(any_space,) * 2 + (vmem,) * 6,
        scratch_shapes=[
            pltpu.VMEM((4 * local, units), BF), pltpu.VMEM((width, units), BF), pltpu.VMEM((FEED, NZ, depth, units), BF),
            pltpu.VMEM((FEED, NZ, depth, units), BF),
            slots(over_y, NZ, 2 * depth, half), slots(CONV - over_y, NZ, depth, mine), pltpu.VMEM((CONV, NZ, depth, half), BF),
            pltpu.VMEM((CONV, NZ, depth, half), BF), pltpu.VMEM((2, local, width), BF), pltpu.VMEM((2, local, width), BF),
            pltpu.VMEM((local, width), BF), pltpu.VMEM((local, width), F32),
            pltpu.VMEM((2, local, width), BF), pltpu.VMEM((2, local, width), BF), pltpu.VMEM((local, width), BF),
            pltpu.VMEM((local, width), BF), pltpu.VMEM((chip, width), BF),
            pltpu.VMEM((local, width), F32), pltpu.VMEM((local, width), BF), pltpu.VMEM((8, width), F32), pltpu.VMEM((n_dp, 8, 128), F32),
            pltpu.VMEM((2, n_dp, 8, 128), F32), pltpu.VMEM((2 * NZ, 8, 128), F32),
            dma((12,)), dma((FEED, NZ)), dma((FEED, NZ)), dma((FEED, NZ)), dma((FEED, NZ)), dma((CONV, NZ)), dma((CONV, NZ)),
            dma((CONV, NZ)), dma((CONV, NZ)), dma((CONV, NZ)), dma((CONV, NZ)), dma((10,)), dma((10,)), dma((9,)), dma((9,)),
        ],
        compiler_params=pltpu.CompilerParams(collective_id=1, has_side_effects=True, vmem_limit_bytes=63 << 20),
    )(small_all, tokens, cotangent, keep, conv_w, feed_w, *rest)


def finish_kernel(n, small, *refs):
    arrays, outs, held, in_sem, out_sem = refs[:n], refs[n : 2 * n + 3], refs[2 * n + 3 : 3 * n + 3], refs[-2], refs[-1]
    loads = [pltpu.make_async_copy(arrays[i], held[i], in_sem.at[i]) for i in range(n)]
    stores = [pltpu.make_async_copy(held[i], outs[i], out_sem.at[i]) for i in range(n)]
    for copy in loads:
        copy.start()
    outs[n][...] = small[0:1, :]
    outs[n + 1][...] = small[1:2, :]
    outs[n + 2][...] = small[2 : 2 + KW, :]
    for load, store in zip(loads, stores):
        load.wait()
        store.start()
    for copy in stores:
        copy.wait()


def finish_call(small, *arrays):
    vmem, any_space = pl.BlockSpec(memory_space=pltpu.VMEM), pl.BlockSpec(memory_space=pl.ANY)
    n = len(arrays)
    row = small.shape[1]
    return pl.pallas_call(
        functools.partial(finish_kernel, n),
        name="finish",
        out_shape=tuple(jax.ShapeDtypeStruct(a.shape, a.dtype) for a in arrays)
        + tuple(jax.ShapeDtypeStruct((r, row), F32) for r in (1, 1, KW)),
        in_specs=[vmem] + [any_space] * n,
        out_specs=(any_space,) * n + (vmem,) * 3,
        scratch_shapes=[pltpu.VMEM(a.shape, a.dtype) for a in arrays] + [pltpu.SemaphoreType.DMA((n,))] * 2,
        compiler_params=pltpu.CompilerParams(vmem_limit_bytes=62 << 20),
    )(small, *arrays)


def block(n_dp, tokens, doc_ids, mixer_norm, in_weight, conv_weight, out_weight, feed_norm, gate_weight, up_weight, down_weight, out_grad):
    small = jnp.concatenate(
        [mixer_norm[None], feed_norm[None], conv_weight, jnp.zeros((6 - KW, mixer_norm.shape[0]), BF)], axis=0).astype(F32)
    conv_w, feed_w, normed, small_all, cot, proj, mixer_in, hidden, two, acts, keep = forward_call(
        n_dp, tokens, out_grad, doc_ids, small, in_weight.transpose(1, 0, 2), out_weight, gate_weight, up_weight, down_weight)
    *large, small_g = backward_call(
        n_dp, small_all, tokens, out_grad, keep, conv_w, feed_w, normed, cot, proj, mixer_in, hidden, two, acts)
    output, input_grad, in_g, out_g, gate_g, up_g, down_g, mixer_g, feed_g, taps_g = finish_call(small_g, *large)
    return (output, input_grad, mixer_g[0], in_g.transpose(1, 0, 2), taps_g, out_g, feed_g[0], gate_g, up_g, down_g)


def shift_down(values, offset):
    if offset == 0:
        return values
    padding = jnp.zeros((offset,) + values.shape[1:], values.dtype)
    return jnp.concatenate([padding, values[:-offset]], axis=0)


def shift_up(values, offset):
    if offset == 0:
        return values
    padding = jnp.zeros((offset,) + values.shape[1:], values.dtype)
    return jnp.concatenate([values[offset:], padding], axis=0)


def tap_masks(doc_rows):
    total_rows = doc_rows.shape[0] * doc_rows.shape[1]
    tap_keep = [jnp.ones((total_rows,), jnp.float32)]
    for offset in range(1, KW):
        matching = doc_rows[:, offset:] == doc_rows[:, :-offset]
        leading = jnp.zeros((doc_rows.shape[0], offset), dtype=bool)
        matching = jnp.concatenate([leading, matching], axis=1)
        tap_keep.append(jnp.where(matching, 1.0, 0.0).astype(jnp.float32).reshape(total_rows))
    return jnp.stack(tap_keep)


def norm_back(grad_out, unit_rows, inverse, gain):
    scaled = grad_out * gain
    return inverse * (scaled - unit_rows * jnp.mean(scaled * unit_rows, axis=-1, keepdims=True))


def body(
    tokens,
    doc_ids,
    mixer_norm,
    in_weight,
    conv_weight,
    out_weight,
    feed_norm,
    gate_weight,
    up_weight,
    down_weight,
    out_grad,
):
    model_width = tokens.shape[1]
    gathered = (
        lax.all_gather(mixer_norm, "dp", axis=0, tiled=True),
        lax.all_gather(in_weight, "dp", axis=0, tiled=True),
        lax.all_gather(conv_weight, "dp", axis=1, tiled=True),
        lax.all_gather(out_weight, "dp", axis=1, tiled=True),
        lax.all_gather(feed_norm, "dp", axis=0, tiled=True),
        lax.all_gather(gate_weight, "dp", axis=0, tiled=True),
        lax.all_gather(up_weight, "dp", axis=0, tiled=True),
        lax.all_gather(down_weight, "dp", axis=1, tiled=True),
    )
    norm_one, in_full, conv_full, out_full, norm_two, gate_full, up_full, down_full = gathered
    channels = in_full.shape[2]
    channel_start = lax.axis_index("tensor") * channels
    tap_keep = tap_masks(doc_ids)
    conv_taps = lax.dynamic_slice_in_dim(conv_full, channel_start, channels, 1).astype(jnp.float32)
    inputs = tokens.astype(jnp.float32)
    inverse_one = lax.rsqrt(jnp.mean(inputs * inputs, axis=-1, keepdims=True) + epsilon)
    unit_one = inputs * inverse_one
    normed_local = (unit_one * norm_one.astype(jnp.float32)).astype(jnp.bfloat16)
    normed = lax.all_gather(normed_local, "tensor", axis=0, tiled=True)
    projected = jnp.einsum("td,dkc->tkc", normed, in_full, preferred_element_type=jnp.float32)
    input_gate = projected[:, 0]
    output_gate = projected[:, 1]
    values = projected[:, 2]
    mixed_input = input_gate * values
    convolved = sum(
        (
            tap_keep[offset][:, None] * conv_taps[offset][None, :] * shift_down(mixed_input, offset)
            for offset in range(KW)
        )
    )
    mixer_in = (output_gate * convolved).astype(jnp.bfloat16)
    mixer_out = lax.psum_scatter(
        jnp.dot(mixer_in, out_full, preferred_element_type=jnp.float32),
        "tensor",
        scatter_dimension=0,
        tiled=True,
    )
    hidden = inputs + mixer_out
    inverse_two = lax.rsqrt(jnp.mean(hidden * hidden, axis=-1, keepdims=True) + epsilon)
    unit_two = hidden * inverse_two
    normed_two_local = (unit_two * norm_two.astype(jnp.float32)).astype(jnp.bfloat16)
    normed_two = lax.all_gather(normed_two_local, "tensor", axis=0, tiled=True)
    gate_pre = jnp.dot(normed_two, gate_full, preferred_element_type=jnp.float32)
    upward = jnp.dot(normed_two, up_full, preferred_element_type=jnp.float32)
    activated = (jax.nn.silu(gate_pre) * upward).astype(jnp.bfloat16)
    feed_out = lax.psum_scatter(
        jnp.dot(activated, down_full, preferred_element_type=jnp.float32).astype(jnp.bfloat16),
        "tensor",
        scatter_dimension=0,
        tiled=True,
    ).astype(jnp.float32)
    output = (hidden + feed_out).astype(jnp.bfloat16)
    regathered = (
        lax.all_gather(mixer_norm, "dp", axis=0, tiled=True),
        lax.all_gather(in_weight, "dp", axis=0, tiled=True),
        lax.all_gather(conv_weight, "dp", axis=1, tiled=True),
        lax.all_gather(out_weight, "dp", axis=1, tiled=True),
        lax.all_gather(feed_norm, "dp", axis=0, tiled=True),
        lax.all_gather(gate_weight, "dp", axis=0, tiled=True),
        lax.all_gather(up_weight, "dp", axis=0, tiled=True),
        lax.all_gather(down_weight, "dp", axis=1, tiled=True),
    )
    norm_one_b, in_again, conv_again, out_again, norm_two_b, gate_again, up_again, down_again = (
        regathered
    )
    gain_one = norm_one_b.astype(jnp.float32)
    gain_two = norm_two_b.astype(jnp.float32)
    taps_again = lax.dynamic_slice_in_dim(conv_again, channel_start, channels, 1).astype(
        jnp.float32
    )
    sigmoid = jax.nn.sigmoid(gate_pre)
    cotangent = lax.all_gather(out_grad, "tensor", axis=0, tiled=True)
    down_grad = jnp.einsum("tf,td->fd", activated, cotangent, preferred_element_type=jnp.float32)
    grad_act = jnp.einsum("td,fd->tf", cotangent, down_again, preferred_element_type=jnp.float32)
    grad_gate = (grad_act * upward * sigmoid * (1.0 + gate_pre * (1.0 - sigmoid))).astype(
        jnp.bfloat16
    )
    grad_up = (grad_act * gate_pre * sigmoid).astype(jnp.bfloat16)
    gate_grad = jnp.einsum("td,tf->df", normed_two, grad_gate, preferred_element_type=jnp.float32)
    up_grad = jnp.einsum("td,tf->df", normed_two, grad_up, preferred_element_type=jnp.float32)
    grad_two = lax.psum_scatter(
        (
            jnp.einsum("tf,df->td", grad_gate, gate_again, preferred_element_type=jnp.float32)
            + jnp.einsum("tf,df->td", grad_up, up_again, preferred_element_type=jnp.float32)
        ).astype(jnp.bfloat16),
        "tensor",
        scatter_dimension=0,
        tiled=True,
    ).astype(jnp.float32)
    feed_gain_part = jnp.sum(grad_two * unit_two, axis=0)
    grad_hidden = out_grad.astype(jnp.float32) + norm_back(
        grad_two, unit_two, inverse_two, gain_two
    )
    grad_mix_local = grad_hidden.astype(jnp.bfloat16)
    grad_mix = lax.all_gather(grad_mix_local, "tensor", axis=0, tiled=True)
    out_grad_part = jnp.einsum("tc,td->cd", mixer_in, grad_mix, preferred_element_type=jnp.float32)
    grad_in = jnp.einsum("td,cd->tc", grad_mix, out_again, preferred_element_type=jnp.float32)
    grad_c = grad_in * convolved
    grad_conv = grad_in * output_gate
    grad_mixed = sum(
        (
            taps_again[offset][None, :] * shift_up(tap_keep[offset][:, None] * grad_conv, offset)
            for offset in range(KW)
        )
    )
    tap_grad = jnp.stack(
        [
            jnp.sum(tap_keep[offset][:, None] * grad_conv * shift_down(mixed_input, offset), axis=0)
            for offset in range(KW)
        ]
    )
    grad_projected = jnp.stack(
        [grad_mixed * values, grad_c, grad_mixed * input_gate], axis=1
    ).astype(jnp.bfloat16)
    in_grad_part = jnp.einsum(
        "td,tkc->dkc", normed, grad_projected, preferred_element_type=jnp.float32
    )
    grad_one = lax.psum_scatter(
        jnp.einsum(
            "tkc,dkc->td", grad_projected, in_again, preferred_element_type=jnp.float32
        ).astype(jnp.bfloat16),
        "tensor",
        scatter_dimension=0,
        tiled=True,
    ).astype(jnp.float32)
    mixer_gain_part = jnp.sum(grad_one * unit_one, axis=0)
    input_grad = (grad_hidden + norm_back(grad_one, unit_one, inverse_one, gain_one)).astype(
        jnp.bfloat16
    )
    conv_part = lax.dynamic_update_slice_in_dim(
        jnp.zeros((KW, model_width), jnp.float32), tap_grad, channel_start, 1
    )
    summed = (
        lax.psum_scatter(mixer_gain_part, "dp", scatter_dimension=0, tiled=True),
        lax.psum_scatter(in_grad_part, "dp", scatter_dimension=0, tiled=True),
        lax.psum_scatter(conv_part, "dp", scatter_dimension=1, tiled=True),
        lax.psum_scatter(out_grad_part, "dp", scatter_dimension=1, tiled=True),
        lax.psum_scatter(feed_gain_part, "dp", scatter_dimension=0, tiled=True),
        lax.psum_scatter(gate_grad, "dp", scatter_dimension=0, tiled=True),
        lax.psum_scatter(up_grad, "dp", scatter_dimension=0, tiled=True),
        lax.psum_scatter(down_grad, "dp", scatter_dimension=1, tiled=True),
    )
    (
        mixer_gain_sum,
        in_weight_grad,
        conv_sum,
        out_weight_grad,
        feed_gain_sum,
        gate_weight_grad,
        up_weight_grad,
        down_weight_grad,
    ) = summed
    mixer_norm_grad, conv_weight_grad, feed_norm_grad = lax.psum(
        (mixer_gain_sum, conv_sum, feed_gain_sum), "tensor"
    )
    return (
        output,
        input_grad,
        mixer_norm_grad,
        in_weight_grad,
        conv_weight_grad,
        out_weight_grad,
        feed_norm_grad,
        gate_weight_grad,
        up_weight_grad,
        down_weight_grad,
    )


def solution(mesh):
    in_specs = (
        P(("dp", "tensor"), None),
        P("dp", None),
        P("dp"),
        P("dp", None, "tensor"),
        P(None, "dp"),
        P("tensor", "dp"),
        P("dp"),
        P("dp", "tensor"),
        P("dp", "tensor"),
        P("tensor", "dp"),
        P(("dp", "tensor"), None),
    )
    out_specs = (
        P(("dp", "tensor"), None),
        P(("dp", "tensor"), None),
        P("dp"),
        P("dp", None, "tensor"),
        P(None, "dp"),
        P("tensor", "dp"),
        P("dp"),
        P("dp", "tensor"),
        P("dp", "tensor"),
        P("tensor", "dp"),
    )
    n_dp = mesh.shape["dp"]
    fits = n_dp == 2 * NZ and mesh.shape["tensor"] == 4
    step = functools.partial(block, n_dp) if fits else body
    return jax.shard_map(step, mesh=mesh, in_specs=in_specs, out_specs=out_specs, check_vma=False)
```

```python
import functools

import jax
import jax.numpy as jnp
from jax import lax
from jax.experimental import pallas as pl
from jax.experimental.pallas import tpu as pltpu
from jax.sharding import PartitionSpec as P

KW = 3
MESH = pl.DeviceIdType.MESH
BF = jnp.bfloat16
F32 = jnp.float32

epsilon = 1e-05

NZ = 4
CONV = 4
FEED = 3
Y_LAST = (True, True, True, False)
X_FIRST = (False, False, True)
Z_FIRST = (False, True, False)
Y_FIRST = (True, True, False, False)


def nn(a, b):
    return lax.dot_general(a, b, (((1,), (0,)), ((), ())), preferred_element_type=F32)


def nt(a, b):
    return lax.dot_general(a, b, (((1,), (1,)), ((), ())), preferred_element_type=F32)


def tn(a, b):
    return lax.dot_general(a, b, (((0,), (0,)), ((), ())), preferred_element_type=F32)


class Place:
    def __init__(self):
        self.dp = lax.axis_index("dp")
        self.t = lax.axis_index("tensor")
        self.z, self.x = lax.div(self.dp, 2), lax.rem(self.dp, 2)
        self.y, self.c = lax.div(self.t, 2), lax.rem(self.t, 2)
        self.over_x = (self.z * 2 + 1 - self.x, self.t)
        self.over_y = (self.dp, (1 - self.y) * 2 + self.c)
        self.over_c = (self.dp, self.y * 2 + 1 - self.c)
        self.t_y = (1 - self.y) * 2 + self.c
        self.t_c = self.y * 2 + 1 - self.c
        self.t_yc = (1 - self.y) * 2 + 1 - self.c
        self.middle = lax.rem(lax.div(self.z + 1, 2), 2) == 1

    def zs(self, k):
        if k == 0:
            return self.z
        if k == 1:
            return self.z + 1 - 2 * lax.rem(self.z, 2)
        if k == 2:
            return lax.rem(self.z + 2, NZ)
        return NZ - 1 - self.z

    def over_z(self, k):
        return (self.zs(k) * 2 + self.x, self.t)


def greet(place, n_dp):
    barrier = pltpu.get_barrier_semaphore()
    for k in range(1, n_dp):
        peer = (lax.rem(place.dp + k, n_dp), place.t)
        pl.semaphore_signal(barrier, inc=1, device_id=peer, device_id_type=MESH)
    for peer in (place.over_c, place.over_y):
        pl.semaphore_signal(barrier, inc=1, device_id=peer, device_id_type=MESH)
    pl.semaphore_wait(barrier, n_dp + 1)


def remote(src, dst, send_sem, recv_sem, peer):
    return pltpu.make_async_remote_copy(
        src_ref=src, dst_ref=dst, send_sem=send_sem, recv_sem=recv_sem, device_id=peer, device_id_type=MESH
    )


def send(*what):
    copy = remote(*what)
    copy.start()
    return copy


def arrived(ref, sem, peer):
    pltpu.make_async_remote_copy(
        src_ref=ref, dst_ref=ref, send_sem=sem, recv_sem=sem, device_id=peer, device_id_type=MESH
    ).wait_recv()


def rows(start, size):
    return pl.ds(pl.multiple_of(start, size), size)


def forward_kernel(
    n_dp,
    tokens, cotangent, doc_rows, small, in_own, out_own, gate_own, up_own, down_own,
    conv_out, feed_out, normed_out, small_out, cot_out, proj_out, mixer_out, hidden_out, two_out, acts_out, keep_out,
    conv_w, feed_w, normed, small_all, mixed_pad, c_keep, proj, mixer_in, part_send, part_recv,
    hidden, two, acts, out_turned, down_turned, keep,
    own_sem, z_send, z_recv, x_send, x_recv, y_send, y_recv, fz_send, fz_recv, fx_send, fx_recv,
    s_send, s_recv, a_send, a_recv, out_sem,
):
    place = Place()
    z, x, y, c, t = place.z, place.x, place.y, place.c, place.t
    depth = gate_own.shape[0]
    local, width = tokens.shape
    chip = 2 * local
    half = in_own.shape[2]
    mine = 2 * half
    tile, pad = 256, 8
    blocks = (t, place.t_c, place.t_y, place.t_yc)
    sends = []
    copies = []
    owned = {}

    def post(make, when=None):
        if when is None:
            make().start()
        else:
            pl.when(when)(lambda: make().start())
        sends.append((make, when))

    def keep_own(src, dst, index):
        owned[index] = pltpu.make_async_copy(src, dst, own_sem.at[index])
        owned[index].start()

    def out(src, dst):
        copy = pltpu.make_async_copy(src, dst, out_sem.at[len(copies)])
        copy.start()
        copies.append(copy)

    def conv_part(j, dp, n, side):
        col = slice(None) if side is None else rows(side * half, half)
        return conv_w.at[j, rows(dp * depth, n * depth), col]

    def feed_part(w, dp, n=1):
        return feed_w.at[w, rows(dp * depth, n * depth), :]

    conv_own = [in_own.at[0], in_own.at[1], in_own.at[2], out_turned]
    feed_own = [gate_own, up_own, down_turned]

    def along_z(src, part, send_sems, recv_sems, index):
        for k in (2, 3, 1):
            post(lambda k=k: remote(src, part(z), send_sems.at[index, k], recv_sems.at[index, z], place.over_z(k)),
                 place.middle if k == 3 else None)

    def from_z(part, send_sems, recv_sems, index, k):
        zk = place.zs(k)
        arrived(part(zk), recv_sems.at[index, zk], place.over_z(k))
        if k == 2:
            post(lambda: remote(part(zk), part(zk), send_sems.at[index, 0], recv_sems.at[index, zk], place.over_z(1)), place.middle)

    def conv_z(j):
        return lambda zk: conv_part(j, zk * 2 + x, 1, y)

    def feed_z(w):
        if X_FIRST[w]:
            return lambda zk: feed_part(w, zk * 2, 2)
        return lambda zk: feed_part(w, zk * 2 + x)

    def conv_second(j, k, src=None):
        zk = place.zs(k)
        part = conv_part(j, zk * 2 + x, 1, y)
        src = part if src is None else src
        if Y_LAST[j]:
            post(lambda: remote(src, part, x_send.at[j, zk], x_recv.at[j, zk], place.over_x))
        else:
            post(lambda: remote(src, part, y_send.at[j, zk], y_recv.at[j, zk], place.over_y))

    def feed_x(w, k, src=None):
        zk = place.zs(k)
        part = feed_part(w, zk * 2 + x)
        src = part if src is None else src
        post(lambda: remote(src, part, fx_send.at[w, zk], fx_recv.at[w, zk], place.over_x))

    def cown(j):
        along_z(conv_own[j], conv_z(j), z_send, z_recv, j)
        conv_second(j, 0, conv_own[j])

    def cz(j, k):
        from_z(conv_z(j), z_send, z_recv, j, k)
        conv_second(j, k)

    def ct(j, k):
        zk = place.zs(k)
        if k == 0:
            owned[j].wait()
        if Y_LAST[j]:
            arrived(conv_part(j, zk * 2 + 1 - x, 1, y), x_recv.at[j, zk], place.over_x)
            pair = conv_part(j, zk * 2, 2, y)
            post(lambda: remote(pair, pair, y_send.at[j, zk], y_recv.at[j, zk], place.over_y))
        else:
            arrived(conv_part(j, zk * 2 + x, 1, 1 - y), y_recv.at[j, zk], place.over_y)
            pair = conv_part(j, zk * 2 + x, 1, None)
            post(lambda: remote(pair, pair, x_send.at[j, zk], x_recv.at[j, zk], place.over_x))

    def fx(w):
        feed_x(w, 0, feed_own[w])

    def fz(w):
        if X_FIRST[w]:
            arrived(feed_part(w, z * 2 + 1 - x), fx_recv.at[w, z], place.over_x)
            owned[CONV + w].wait()
            along_z(feed_part(w, z * 2, 2), feed_z(w), fz_send, fz_recv, w)
        else:
            along_z(feed_own[w], feed_z(w), fz_send, fz_recv, w)

    def fp(w, k):
        from_z(feed_z(w), fz_send, fz_recv, w, k)
        if not X_FIRST[w]:
            feed_x(w, k)

    def feed_ready(w):
        if not X_FIRST[w]:
            for k in range(NZ):
                zk = place.zs(k)
                arrived(feed_part(w, zk * 2 + 1 - x), fx_recv.at[w, zk], place.over_x)
            owned[CONV + w].wait()
        out(feed_w.at[w], feed_out.at[w])

    def cot_block(block):
        return cot_out.at[rows(block * local, local), :]

    def cotc():
        post(lambda: remote(cotangent, cot_block(t), a_send.at[0], a_recv.at[0], place.over_c))

    def coty():
        post(lambda: remote(cotangent, cot_block(t), a_send.at[2], a_recv.at[2], place.over_y))

    def cotf():
        there = cot_block(place.t_y)
        arrived(there, a_recv.at[2], place.over_y)
        post(lambda: remote(there, there, a_send.at[6], a_recv.at[6], place.over_c))

    def turn():
        down_turned[...] = jnp.transpose(down_own[...])
        for w in range(FEED):
            keep_own(feed_own[w], feed_part(w, place.dp), CONV + w)
        own = doc_rows[pl.ds(y, 1), :].astype(F32)
        position = lax.broadcasted_iota(jnp.int32, (1, chip), 1)
        for k in range(1, KW):
            same = jnp.where((own == pltpu.roll(own, k, 1)) & (position >= k), 1.0, 0.0)
            keep[k - 1, 0:chip, :] = jnp.transpose(jnp.broadcast_to(same, (128, chip)))
            keep[k - 1, chip : chip + pad, :] = jnp.zeros((pad, 128), F32)
        out(keep, keep_out)

    def gain(r):
        return jnp.concatenate([small_all[d, r : r + 1, :] for d in range(n_dp)], axis=1)

    def norm():
        for k in range(1, n_dp):
            peer = lax.rem(place.dp + k, n_dp)
            arrived(small_all.at[peer], s_recv.at[peer], (peer, t))
        inputs = tokens[...].astype(F32)
        inverse = lax.rsqrt(jnp.mean(inputs * inputs, axis=-1, keepdims=True) + epsilon)
        normed[rows(c * local, local), :] = (inputs * inverse * gain(0)).astype(BF)
        own = normed.at[rows(c * local, local), :]
        post(lambda: remote(own, own, a_send.at[1], a_recv.at[1], place.over_c))

    def p1():
        arrived(normed.at[rows((1 - c) * local, local), :], a_recv.at[1], place.over_c)
        for j in range(CONV):
            for k in range(NZ):
                zk = place.zs(k)
                if Y_LAST[j]:
                    arrived(conv_part(j, zk * 2, 2, 1 - y), y_recv.at[j, zk], place.over_y)
                else:
                    arrived(conv_part(j, zk * 2 + 1 - x, 1, None), x_recv.at[j, zk], place.over_x)
        out(conv_w, conv_out)
        out(normed, normed_out)
        mixed_pad[0:pad, :] = jnp.zeros((pad, mine), F32)

        def project(i, carry):
            at = rows(i * tile, tile)
            lhs = normed[at, :]
            b = nn(lhs, conv_w[0])
            proj[0, at, :] = b.astype(BF)
            v = nn(lhs, conv_w[2])
            proj[2, at, :] = v.astype(BF)
            mixed_pad[pl.ds(pl.multiple_of(i * tile + pad, 8), tile), :] = b * v
            g = nn(lhs, conv_w[1])
            proj[1, at, :] = g.astype(BF)
            c_keep[at, :] = g
            return carry

        lax.fori_loop(0, chip // tile, project, 0)

    def p2():
        taps = []
        for r in range(2, 2 + KW):
            taps.append(jnp.concatenate(
                [small_all[side * 4 + 2 * c + i, r : r + 1, :] for side in range(2) for i in range(2)], axis=1))

        def convolve(i, carry):
            at = rows(i * tile, tile)
            window = mixed_pad[pl.ds(pl.multiple_of(i * tile, 8), tile + pad), :]
            total = taps[0] * window[pad:, :]
            for k in range(1, KW):
                mask = jnp.concatenate([keep[k - 1, at, :]] * (mine // 128), axis=1)
                total = total + mask * taps[k] * window[pad - k : pad - k + tile, :]
            proj[3, at, :] = total.astype(BF)
            mixer_in[at, :] = (c_keep[at, :] * total).astype(BF)
            return carry

        lax.fori_loop(0, chip // tile, convolve, 0)
        out(proj, proj_out)
        out(mixer_in, mixer_out)
        part_send[...] = nt(mixer_in[rows((1 - c) * local, local), :], conv_w[3]).astype(BF)
        post(lambda: remote(part_send, part_recv, a_send.at[3], a_recv.at[3], place.over_c))
        hidden[...] = tokens[...].astype(F32) + nt(mixer_in[rows(c * local, local), :], conv_w[3])

    def p3():
        arrived(part_recv, a_recv.at[3], place.over_c)
        total = hidden[...] + part_recv[...].astype(F32)
        hidden[...] = total
        inverse = lax.rsqrt(jnp.mean(total * total, axis=-1, keepdims=True) + epsilon)
        two[rows(t * local, local), :] = (total * inverse * gain(1)).astype(BF)
        own = two.at[rows(t * local, local), :]
        post(lambda: remote(own, own, a_send.at[5], a_recv.at[5], place.over_y))
        post(lambda: remote(own, own, a_send.at[4], a_recv.at[4], place.over_c))
        out(hidden, hidden_out)

    def t2():
        there = two.at[rows(place.t_y * local, local), :]
        arrived(there, a_recv.at[5], place.over_y)
        post(lambda: remote(there, there, a_send.at[7], a_recv.at[7], place.over_c))

    def g(b):
        if b == 0:
            feed_ready(0)
        if b == 1:
            arrived(two.at[rows(place.t_c * local, local), :], a_recv.at[4], place.over_c)
        if b == 3:
            arrived(two.at[rows(place.t_yc * local, local), :], a_recv.at[7], place.over_c)

        def step(i, carry):
            at = rows(blocks[b] * local + i * tile, tile)
            gate = nn(two[at, :], feed_w[0])
            s = jax.nn.sigmoid(gate)
            silu = gate * s
            acts[1, at, :] = (s + silu * (1.0 - s)).astype(BF)
            acts[2, at, :] = silu.astype(BF)
            return carry

        lax.fori_loop(0, local // tile, step, 0)

    def u(b):
        if b == 0:
            feed_ready(1)

        def step(i, carry):
            at = rows(blocks[b] * local + i * tile, tile)
            upward = nn(two[at, :], feed_w[1])
            acts[0, at, :] = (acts[2, at, :].astype(F32) * upward).astype(BF)
            acts[1, at, :] = (acts[1, at, :].astype(F32) * upward).astype(BF)
            return carry

        lax.fori_loop(0, local // tile, step, 0)
        at = rows(blocks[b] * local, local)
        out(acts.at[:, at, :], acts_out.at[:, at, :])
        out(two.at[at, :], two_out.at[at, :])

    small_all[place.dp] = small[...]
    out_turned[...] = jnp.transpose(out_own[...])
    greet(place, n_dp)
    for k in range(1, n_dp):
        post(lambda k=k: remote(small, small_all.at[place.dp], s_send.at[k], s_recv.at[place.dp], (lax.rem(place.dp + k, n_dp), t)))
    for j in range(CONV):
        keep_own(conv_own[j], conv_part(j, place.dp, 1, y), j)
    keep_own(cotangent, cot_block(t), CONV + FEED)
    cown(1)
    cown(3)
    cown(0)
    fx(0)
    ct(1, 0)
    cz(1, 2)
    ct(0, 0)
    cown(2)
    cz(3, 2)
    cz(3, 1)
    cz(1, 1)
    cz(1, 3)
    ct(1, 2)
    turn()
    cz(0, 2)
    cz(3, 3)
    cz(0, 1)
    ct(1, 3)
    cz(2, 2)
    fz(0)
    ct(2, 0)
    ct(3, 2)
    cz(2, 1)
    fx(2)
    fz(1)
    cz(2, 3)
    cz(0, 3)
    ct(0, 2)
    norm()
    ct(1, 1)
    ct(2, 1)
    ct(0, 1)
    ct(3, 0)
    ct(2, 3)
    ct(3, 1)
    ct(2, 2)
    ct(3, 3)
    ct(0, 3)
    cotc()
    fp(0, 1)
    coty()
    fp(0, 2)
    p1()
    fp(1, 2)
    fp(1, 1)
    fp(0, 3)
    fz(2)
    p2()
    p3()
    fp(1, 3)
    cotf()
    g(0)
    fx(1)
    fp(2, 2)
    g(1)
    u(0)
    u(1)
    t2()
    g(2)
    u(2)
    fp(2, 1)
    g(3)
    u(3)
    fp(2, 3)
    feed_ready(2)
    small_out[...] = small_all[...]
    arrived(cot_block(place.t_c), a_recv.at[0], place.over_c)
    arrived(cot_block(place.t_yc), a_recv.at[6], place.over_c)
    owned[CONV + FEED].wait()
    for make, when in sends:
        if when is None:
            make().wait_send()
        else:
            pl.when(when)(lambda make=make: make().wait_send())
    for copy in copies:
        copy.wait()


def forward_call(n_dp, *operands):
    tokens, _, _, _, in_own, _, gate_own, _, _ = operands
    local, width = tokens.shape
    half, units = in_own.shape[2], gate_own.shape[1]
    chip, group, mine = 2 * local, 4 * local, 2 * half

    def shaped(dims, kind=BF):
        return jax.ShapeDtypeStruct(dims, kind)

    dma = pltpu.SemaphoreType.DMA
    vmem, any_space = pl.BlockSpec(memory_space=pltpu.VMEM), pl.BlockSpec(memory_space=pl.ANY)
    return pl.pallas_call(
        functools.partial(forward_kernel, n_dp),
        name="gather_forward",
        out_shape=(
            shaped((CONV, width, mine)), shaped((FEED, width, units)), shaped((chip, width)), shaped((n_dp, 8, 128), F32),
            shaped((group, width)), shaped((4, chip, mine)), shaped((chip, mine)), shaped((local, width), F32),
            shaped((group, width)), shaped((3, group, units)), shaped((KW - 1, chip + 8, 128), F32),
        ),
        in_specs=[vmem] * 4 + [any_space, vmem, any_space, any_space, vmem],
        out_specs=tuple(vmem if i == 3 else any_space for i in range(11)),
        scratch_shapes=[
            pltpu.VMEM((CONV, width, mine), BF), pltpu.VMEM((FEED, width, units), BF), pltpu.VMEM((chip, width), BF),
            pltpu.VMEM((n_dp, 8, 128), F32), pltpu.VMEM((chip + 8, mine), F32),
            pltpu.VMEM((chip, mine), F32), pltpu.VMEM((4, chip, mine), BF), pltpu.VMEM((chip, mine), BF),
            pltpu.VMEM((local, width), BF), pltpu.VMEM((local, width), BF), pltpu.VMEM((local, width), F32),
            pltpu.VMEM((group, width), BF), pltpu.VMEM((3, group, units), BF),
            pltpu.VMEM((width // n_dp, half), BF), pltpu.VMEM((width // n_dp, units), BF), pltpu.VMEM((KW - 1, chip + 8, 128), F32),
            dma((8,)), dma((CONV, NZ)), dma((CONV, NZ)), dma((CONV, NZ)), dma((CONV, NZ)), dma((CONV, NZ)), dma((CONV, NZ)),
            dma((FEED, NZ)), dma((FEED, NZ)), dma((FEED, NZ)), dma((FEED, NZ)),
            dma((n_dp,)), dma((n_dp,)), dma((8,)), dma((8,)), dma((20,)),
        ],
        compiler_params=pltpu.CompilerParams(collective_id=0, has_side_effects=True, vmem_limit_bytes=62 << 20),
    )(*operands)


def backward_kernel(
    n_dp,
    small_all, tokens_in, cot_own_in, keep_in, conv_in, feed_in, normed_in, cot_in, proj_in, mixer_in_hbm, hidden_in, two_in, acts_in,
    output, input_grad, in_grad, out_grad, gate_grad, up_grad, down_grad, small_grad,
    act, g_down, x_got, z_got, pair_got, x_last, c_got_y, c_got_x, c_two, c_z, two_send, two_recv, two_y, own_two,
    down_send, down_recv, down_y, down_own, grad_mix, hidden, token_rows, feed_gain, small_sum, small_got, small_z,
    load_sem, fx_send, fx_recv, fz_send, fz_recv, c1_send, c1_recv, c2_send, c2_recv, c3_send, c3_recv,
    s_send, s_recv, a_send, a_recv,
):
    place = Place()
    z, x, y, c, t = place.z, place.x, place.y, place.c, place.t
    depth, units = gate_grad.shape
    local, width = own_two.shape
    chip = 2 * local
    half = in_grad.shape[2]
    mine = 2 * half
    tile = 256
    sends = []

    def post(make):
        make().start()
        sends.append(make)
        return make

    def load(src, dst, index):
        copy = pltpu.make_async_copy(src, dst, load_sem.at[index])
        copy.start()
        return copy

    def g_rows(w, start, size):
        if w == 2:
            return g_down.at[rows(start, size), :]
        return act.at[rows(w * width + start, size), :]

    def x_slot(w):
        return w - sum(Z_FIRST[:w])

    def pair_rows(w, k):
        return g_rows(w, place.zs(k) * 2 * depth, 2 * depth)

    def pair_add(w, k, slots):
        def step(i, carry):
            at = rows(i * 64, 64)
            held = pair_rows(w, k).at[at, :]
            total = held[...].astype(F32)
            for slot in slots:
                total = total + pair_got[slot, at, :].astype(F32)
            held[...] = total.astype(BF)
            return carry

        lax.fori_loop(0, 2 * depth // 64, step, 0)

    def pair_send(w, k):
        return z_remote(pair_rows(w, k), pair_got, fz_send.at[w], fz_recv.at[w], k)

    def m(w, k):
        if Z_FIRST[w]:
            if k == 2:
                @pl.when(place.middle)
                def _():
                    arrived(pair_got.at[0], fz_recv.at[w, 0], place.over_z(1))
                    pair_add(w, k, (0,))
                    pair_send(w, k).start()

            return
        zk = place.zs(k)
        got = x_got.at[x_slot(w), zk]
        arrived(got, fx_recv.at[w, zk], place.over_x)
        if k:
            got[...] = (g_rows(w, (zk * 2 + x) * depth, depth)[...].astype(F32) + got[...].astype(F32)).astype(BF)

            def add(more):
                held = x_got.at[x_slot(w), place.zs(k)]
                held[...] = (held[...].astype(F32) + more[...].astype(F32)).astype(BF)

            if k == 2:
                @pl.when(place.middle)
                def _():
                    arrived(z_got.at[x_slot(w), 0], fz_recv.at[w, 0], place.over_z(1))
                    add(z_got.at[x_slot(w), 0])

            post(lambda: z_remote(x_got.at[x_slot(w), place.zs(k)], z_got.at[x_slot(w)], fz_send.at[w], fz_recv.at[w], k))

    def z_remote(held, got, sends_at, recvs_at, k):
        if k == 3:
            slot = jnp.where(place.middle, 3, 0)
            peer = (jnp.where(place.middle, place.zs(3), place.zs(1)) * 2 + x, t)
            return remote(held, got.at[slot], sends_at.at[k], recvs_at.at[slot], peer)
        return remote(held, got.at[k], sends_at.at[k], recvs_at.at[k], place.over_z(k))

    def z_sum(total, got, recvs_at):
        for k in (1, 2):
            arrived(got.at[k], recvs_at.at[k], place.over_z(k))
            total = total + got[k].astype(F32)
        return total

    def z_last(ref, got, recvs_at):
        @pl.when(place.middle)
        def _():
            arrived(got.at[3], recvs_at.at[3], place.over_z(3))
            ref[...] = ref[...] + got[3].astype(F32)

    def gain(r):
        return jnp.concatenate([small_all[d, r : r + 1, :] for d in range(n_dp)], axis=1)

    def norm_back(grad, unit, inverse, scale):
        scaled = grad * scale
        return inverse * (scaled - unit * jnp.mean(scaled * unit, axis=-1, keepdims=True))

    def rms(values):
        return lax.rsqrt(jnp.mean(values * values, axis=-1, keepdims=True) + epsilon)

    def send_slot(i):
        return lambda: remote(two_send.at[i], two_recv.at[i], a_send.at[1 + i], a_recv.at[1 + i], place.over_c)

    first_slot = send_slot(0)

    def fetch_hidden():
        return pltpu.make_async_copy(hidden_in, hidden, load_sem.at[9])

    def fetch_cotangent():
        return pltpu.make_async_copy(cot_own_in, token_rows, load_sem.at[10])

    def fetch_tokens():
        return pltpu.make_async_copy(tokens_in, token_rows, load_sem.at[11])

    def n2():
        fetch_hidden().wait()
        fetch_cotangent().wait()
        arrived(two_y, a_recv.at[3], place.over_y)
        arrived(two_recv.at[1], a_recv.at[2], place.over_c)
        scale = gain(1)

        def step(i, carry):
            at = rows(i * 128, 128)
            grad_two = own_two[at, :] + two_recv[1, at, :].astype(F32) + two_y[at, :].astype(F32)
            values = hidden[at, :]
            inverse = rms(values)
            unit = values * inverse
            grad_hidden = token_rows[at, :].astype(F32) + norm_back(grad_two, unit, inverse, scale)
            hidden[at, :] = grad_hidden
            grad_mix[rows(c * local + i * 128, 128), :] = grad_hidden.astype(BF)
            return carry + jnp.sum(grad_two * unit, axis=0, keepdims=True)

        feed_gain[0:1, :] = lax.fori_loop(0, local // 128, step, jnp.zeros((1, width), F32))
        fetch_tokens().start()

        def make():
            own = grad_mix.at[rows(c * local, local), :]
            return remote(own, own, a_send.at[4], a_recv.at[4], place.over_c)

        post(make)

    def feed_phase(feed_w, cot, acts):
        plan = [(acts_in.at[0], act), (cot_in, cot), (feed_in.at[2], feed_w.at[2]), (acts_in.at[1], acts.at[0]),
                (acts_in.at[2], acts.at[1]), (feed_in.at[pl.ds(0, 2)], feed_w.at[pl.ds(0, 2)])]
        loads = {}
        waited = set()

        def begin(*which):
            for i in which:
                if i not in loads:
                    loads[i] = load(*plan[i], i)

        def loaded(*which):
            begin(*which)
            for i in which:
                if i not in waited:
                    waited.add(i)
                    loads[i].wait()
            if len(loads) < len(plan):
                begin(*range(len(plan)))
                fetch_hidden().start()
                fetch_cotangent().start()

        begin(0, 1)
        greet(place, n_dp)

        def g(w, k):
            at = rows(place.zs(k) * 2 * depth, 2 * depth)
            if w == 2:
                loaded(0, 1)
                g_down[at, :] = tn(cot[:, at], act[...]).astype(BF)
            else:
                if "two" not in waited:
                    waited.add("two")
                    load(two_in, cot, 8).wait()
                act[rows(w * width + place.zs(k) * 2 * depth, 2 * depth), :] = tn(cot[:, at], acts[w]).astype(BF)

            def make():
                zk = place.zs(k)
                return remote(
                    g_rows(w, (zk * 2 + 1 - x) * depth, depth), x_got.at[x_slot(w), zk], fx_send.at[w, zk], fx_recv.at[w, zk], place.over_x)

            if not Z_FIRST[w]:
                post(make)
            elif k == 2:
                pl.when(jnp.logical_not(place.middle))(lambda: pair_send(w, k).start())
                sends.append(lambda: pair_send(w, k))
            elif k:
                post(lambda: pair_send(w, k))

        def back(block, store):
            loaded(1, 2, 3, 4, 5)

            def step(i, carry):
                at = rows(block * local + i * tile, tile)
                grad_act = nn(cot[at, :], feed_w[2])
                grad_gate = (grad_act * acts[0, at, :].astype(F32)).astype(BF)
                acts[0, at, :] = grad_gate
                grad_up = (grad_act * acts[1, at, :].astype(F32)).astype(BF)
                acts[1, at, :] = grad_up
                store(rows(i * tile, tile), nt(grad_gate, feed_w[0]) + nt(grad_up, feed_w[1]))
                return carry

            lax.fori_loop(0, local // tile, step, 0)

        def to_slot(i):
            def store(at, value):
                two_send[i, at, :] = value.astype(BF)

            return store

        def to_own(at, value):
            own_two[at, :] = value

        def a_yc():
            back(place.t_yc, to_slot(0))
            post(first_slot)

        def a_c():
            back(place.t_c, to_slot(1))
            post(send_slot(1))

        def a_y():
            back(place.t_y, to_own)

        def ay():
            arrived(two_recv.at[0], a_recv.at[1], place.over_c)
            two_recv[0] = (own_two[...] + two_recv[0].astype(F32)).astype(BF)
            post(lambda: remote(two_recv.at[0], two_y, a_send.at[3], a_recv.at[3], place.over_y))

        def a_o():
            back(t, to_own)

        def down(block):
            loaded(0, 2)
            return nt(act[rows(block * local, local), :], feed_w[2]).astype(BF)

        def d_yc():
            down_send[0] = down(place.t_yc)
            post(lambda: remote(down_send.at[0], down_recv.at[0], a_send.at[6], a_recv.at[6], place.over_c))

        def d_c():
            down_send[1] = down(place.t_c)
            post(lambda: remote(down_send.at[1], down_recv.at[1], a_send.at[7], a_recv.at[7], place.over_c))

        def d_y():
            down_own[...] = down(place.t_y)

        def dy():
            arrived(down_recv.at[0], a_recv.at[6], place.over_c)
            down_recv[0] = (down_own[...].astype(F32) + down_recv[0].astype(F32)).astype(BF)
            post(lambda: remote(down_recv.at[0], down_y, a_send.at[8], a_recv.at[8], place.over_y))

        def d_o():
            down_own[...] = down(t)

        g(2, 3)
        g(2, 1)
        d_yc()
        m(2, 3)
        g(2, 2)
        a_yc()
        m(2, 1)
        d_y()
        a_y()
        ay()
        a_o()
        m(2, 2)
        dy()
        a_c()
        d_c()
        g(2, 0)
        d_o()
        g(1, 3)
        g(0, 2)
        g(1, 0)
        g(1, 2)
        g(1, 1)
        g(0, 0)
        g(0, 1)
        n2()
        g(0, 3)

    pl.run_scoped(
        feed_phase,
        pltpu.VMEM((FEED, width, units), BF), pltpu.VMEM((4 * local, width), BF), pltpu.VMEM((2, 4 * local, units), BF),
    )

    def conv_phase(conv_w, proj, normed, mixer_in, grad_proj, pad_grad, tap_sum, g_conv, keep, stage):
        plan = [(conv_in.at[3], conv_w.at[3]), (proj_in.at[3], proj.at[3]), (proj_in.at[1], proj.at[1]), (mixer_in_hbm, mixer_in),
                (normed_in, normed), (proj_in.at[0], proj.at[0]), (proj_in.at[2], proj.at[2]), (keep_in, keep),
                (conv_in.at[pl.ds(0, 3)], conv_w.at[pl.ds(0, 3)])]
        loads = {}
        waited = set()
        stores = []

        def begin(*which):
            for i in which:
                if i not in loads:
                    loads[i] = load(*plan[i], 12 + i)

        def loaded(*which):
            for i in which:
                if i not in waited:
                    waited.add(i)
                    loads[i].wait()
            begin(*range(len(plan)))

        begin(0, 1, 2)

        def taps():
            return [jnp.concatenate([small_all[side * 4 + 2 * c + i, r : r + 1, :] for side in range(2) for i in range(2)], axis=1)
                    for r in range(2, 2 + KW)]

        def gm():
            loaded(0, 1, 2)
            arrived(grad_mix.at[rows((1 - c) * local, local), :], a_recv.at[4], place.over_c)
            pad_grad[pl.ds(chip, 8), :] = jnp.zeros((8, mine), F32)

            def step(i, carry):
                at = rows(i * tile, tile)
                grad_in = nn(grad_mix[at, :], conv_w[3])
                grad_proj[1, at, :] = (grad_in * proj[3, at, :].astype(F32)).astype(BF)
                pad_grad[at, :] = grad_in * proj[1, at, :].astype(F32)
                return carry

            lax.fori_loop(0, chip // tile, step, 0)

        def c1_slot(j, zk):
            if Y_FIRST[j]:
                return c_got_y.at[sum(Y_FIRST[:j]), zk]
            return c_got_x.at[j - sum(Y_FIRST[:j]), zk]

        def w(j):
            if j == 3:
                loaded(3)
                for part in (slice(0, width // 2), slice(width // 2, width)):
                    g_conv[j, part, :] = tn(grad_mix[:, part], mixer_in[...]).astype(BF)
            else:
                loaded(4)
                for part in (slice(0, width // 2), slice(width // 2, width)):
                    g_conv[j, part, :] = tn(normed[:, part], grad_proj[j]).astype(BF)
            for k in (2, 1, 3, 0):
                zk = place.zs(k)
                if Y_FIRST[j]:
                    src, peer = g_conv.at[j, rows(zk * 2 * depth, 2 * depth), rows((1 - y) * half, half)], place.over_y
                else:
                    src, peer = g_conv.at[j, rows((zk * 2 + 1 - x) * depth, depth), :], place.over_x
                post(lambda src=src, peer=peer, zk=zk: remote(src, c1_slot(j, zk), c1_send.at[j, zk], c1_recv.at[j, zk], peer))

        def h2():
            loaded(5, 6, 7)
            tap = taps()
            tap_sum[...] = jnp.zeros_like(tap_sum)
            size = 128

            def step(i, carry):
                at = rows(i * size, size)
                wide = pl.ds(pl.multiple_of(i * size, 8), size + 8)
                window = pad_grad[wide, :]
                b, v = proj[0, at, :].astype(F32), proj[2, at, :].astype(F32)
                mixed = b * v
                now = window[:size, :]
                total = tap[0] * now
                tap_sum[0:1, :] += jnp.sum(now * mixed, axis=0, keepdims=True)
                for k in range(1, KW):
                    mask = jnp.concatenate([keep[k - 1, wide, :]] * (mine // 128), axis=1)
                    ahead = (mask * window)[k : k + size, :]
                    total = total + tap[k] * ahead
                    tap_sum[k : k + 1, :] += jnp.sum(ahead * mixed, axis=0, keepdims=True)
                grad_proj[0, at, :] = (total * v).astype(BF)
                grad_proj[2, at, :] = (total * b).astype(BF)
                return carry

            lax.fori_loop(0, chip // size, step, 0)

        def first_grad(block, store):
            def step(i, carry):
                at = rows(block * local + i * tile, tile)
                store(rows(i * tile, tile), nt(grad_proj[0, at, :], conv_w[0]) + nt(grad_proj[1, at, :], conv_w[1]) + nt(grad_proj[2, at, :], conv_w[2]))
                return carry

            lax.fori_loop(0, local // tile, step, 0)

        def f1():
            loaded(8)
            first_slot().wait_send()
            sends.remove(first_slot)

            def to_send(at, value):
                two_send[0, at, :] = value.astype(BF)

            def to_own(at, value):
                own_two[at, :] = value

            first_grad(1 - c, to_send)
            post(lambda: remote(two_send.at[0], two_recv.at[1], a_send.at[5], a_recv.at[5], place.over_c))
            first_grad(c, to_own)

        def n1():
            fetch_tokens().wait()
            arrived(two_recv.at[1], a_recv.at[5], place.over_c)
            scale = gain(0)

            def step(i, carry):
                at = rows(i * 128, 128)
                grad_one = own_two[at, :] + two_recv[1, at, :].astype(F32)
                values = token_rows[at, :].astype(F32)
                inverse = rms(values)
                unit = values * inverse
                two_recv[1, at, :] = (hidden[at, :] + norm_back(grad_one, unit, inverse, scale)).astype(BF)
                return carry + jnp.sum(grad_one * unit, axis=0, keepdims=True)

            mixer_gain = lax.fori_loop(0, local // 128, step, jnp.zeros((1, width), F32))
            stores.append(load(two_recv.at[1], input_grad, 1))
            stores.append(load(hidden_in, own_two, 0))
            zero = jnp.zeros((1, 128), F32)
            for d in range(n_dp):
                cols = slice(d * 128, d * 128 + 128)
                here = (c == (d % 4) // 2).astype(F32)
                own = (d // 4) * half + (d % 2) * 128
                small_sum[d] = jnp.concatenate(
                    [mixer_gain[:, cols], feed_gain[0:1, cols]]
                    + [here * tap_sum[k : k + 1, own : own + 128] for k in range(KW)] + [zero] * 3, axis=0)

        def c2(j, k):
            zk = place.zs(k)
            got = c1_slot(j, zk)
            if Y_FIRST[j]:
                arrived(got, c1_recv.at[j, zk], place.over_y)
                held = g_conv[j, rows(zk * 2 * depth, 2 * depth), rows(y * half, half)]
                src, peer = got.at[rows((1 - x) * depth, depth), :], place.over_x
            else:
                arrived(got, c1_recv.at[j, zk], place.over_x)
                held = g_conv[j, rows((zk * 2 + x) * depth, depth), :]
                src, peer = got.at[:, rows((1 - y) * half, half)], place.over_y
            got[...] = (held.astype(F32) + got[...].astype(F32)).astype(BF)
            post(lambda: remote(src, c_two.at[j, zk], c2_send.at[j, zk], c2_recv.at[j, zk], peer))

        def held_half(j, zk):
            if Y_FIRST[j]:
                return c1_slot(j, zk)[rows(x * depth, depth), :].astype(F32)
            return c1_slot(j, zk)[:, rows(y * half, half)].astype(F32)

        def c3(j, k):
            zk = place.zs(k)
            got = c_two.at[j, zk]
            arrived(got, c2_recv.at[j, zk], place.over_x if Y_FIRST[j] else place.over_y)
            if k:
                got[...] = (held_half(j, zk) + got[...].astype(F32)).astype(BF)
                if k == 2:
                    @pl.when(place.middle)
                    def _():
                        arrived(c_z.at[j, 0], c3_recv.at[j, 0], place.over_z(1))
                        got[...] = (got[...].astype(F32) + c_z[j, 0].astype(F32)).astype(BF)

                post(lambda: z_remote(got, c_z.at[j], c3_send.at[j], c3_recv.at[j], k))

        def cf(j):
            total = z_sum(held_half(j, z) + c_two[j, z].astype(F32), c_z.at[j], c3_recv.at[j])
            if j == 3:
                stage[0:depth, 0:half] = total
                ref = stage.at[0:depth, 0:half]
                z_last(ref, c_z.at[j], c3_recv.at[j])
                out_grad[...] = jnp.transpose(ref[...])
            else:
                in_grad[j] = total
                z_last(in_grad.at[j], c_z.at[j], c3_recv.at[j])

        def fe(w):
            for k in (1, 2):
                arrived(pair_got.at[k], fz_recv.at[w, k], place.over_z(k))
            pair_add(w, 0, (1, 2))

            @pl.when(place.middle)
            def _():
                arrived(pair_got.at[3], fz_recv.at[w, 3], place.over_z(3))
                pair_add(w, 0, (3,))

            post(lambda: remote(g_rows(w, (z * 2 + 1 - x) * depth, depth), x_last, fx_send.at[w, 0], fx_recv.at[w, 0], place.over_x))

        def ff(w):
            ref = (gate_grad, up_grad, stage)[w]
            total = g_rows(w, (z * 2 + x) * depth, depth)[...].astype(F32)
            if Z_FIRST[w]:
                arrived(x_last, fx_recv.at[w, 0], place.over_x)
                ref[...] = total + x_last[...].astype(F32)
            else:
                ref[...] = z_sum(total + x_got[x_slot(w), z].astype(F32), z_got.at[x_slot(w)], fz_recv.at[w])
                z_last(ref, z_got.at[x_slot(w)], fz_recv.at[w])
            if w == 2:
                down_grad[...] = jnp.transpose(stage[...])

        def do():
            stores[1].wait()
            arrived(down_recv.at[1], a_recv.at[7], place.over_c)
            arrived(down_y, a_recv.at[8], place.over_y)

            def step(i, carry):
                at = rows(i * 128, 128)
                total = own_two[at, :] + down_own[at, :].astype(F32) + down_recv[1, at, :].astype(F32) + down_y[at, :].astype(F32)
                down_own[at, :] = total.astype(BF)
                return carry

            lax.fori_loop(0, local // 128, step, 0)
            stores.append(load(down_own, output, 2))

        def s0():
            post(lambda: remote(small_sum, small_got.at[0], s_send.at[0], s_recv.at[0], place.over_c))

        def s1():
            arrived(small_got.at[0], s_recv.at[0], place.over_c)
            small_got[0] = small_sum[...] + small_got[0]
            post(lambda: remote(small_got.at[0], small_got.at[1], s_send.at[1], s_recv.at[1], place.over_y))

        def s2():
            arrived(small_got.at[1], s_recv.at[1], place.over_y)
            small_got[1] = small_got[0] + small_got[1]
            for k in range(NZ):
                zk = place.zs(k)
                post(lambda zk=zk, k=k: remote(
                    small_got.at[1, zk * 2 + 1 - x], small_z.at[zk], s_send.at[2 + k], s_recv.at[2 + zk], place.over_x))

        def s3():
            for k in range(NZ):
                zk = place.zs(k)
                arrived(small_z.at[zk], s_recv.at[2 + zk], place.over_x)
                small_z[zk] = small_z[zk] + small_got[1, zk * 2 + x]
                if k:
                    post(lambda zk=zk, k=k: remote(small_z.at[zk], small_z.at[NZ + k], s_send.at[6 + k], s_recv.at[6 + k], place.over_z(k)))

        def s4():
            total = small_z[z]
            for k in range(1, NZ):
                arrived(small_z.at[NZ + k], s_recv.at[6 + k], place.over_z(k))
                total = total + small_z[NZ + k]
            small_grad[...] = total

        gm()
        w(3)
        h2()
        w(1)
        m(1, 2)
        w(2)
        c2(1, 2)
        m(0, 3)
        w(0)
        m(0, 1)
        c2(1, 1)
        m(0, 2)
        f1()
        c2(0, 3)
        c2(1, 0)
        c2(1, 3)
        c2(3, 1)
        c2(2, 3)
        c2(3, 3)
        c2(2, 2)
        n1()
        m(2, 0)
        c2(0, 2)
        c2(3, 2)
        c2(0, 0)
        c3(2, 3)
        c3(1, 3)
        c3(0, 3)
        c3(1, 0)
        c3(3, 1)
        m(0, 0)
        c2(0, 1)
        c3(3, 3)
        c2(2, 0)
        fe(1)
        s0()
        ff(2)
        c2(2, 1)
        c3(1, 1)
        c3(1, 2)
        c2(3, 0)
        s1()
        c3(2, 2)
        c3(3, 0)
        c3(0, 1)
        s2()
        do()
        ff(0)
        c3(2, 1)
        s3()
        c3(0, 0)
        c3(2, 0)
        c3(3, 2)
        c3(0, 2)
        cf(2)
        ff(1)
        cf(3)
        s4()
        cf(1)
        cf(0)
        for make in sends:
            make().wait_send()
        stores[0].wait()
        stores[2].wait()

    pl.run_scoped(
        conv_phase,
        pltpu.VMEM((CONV, width, mine), BF), pltpu.VMEM((4, chip, mine), BF), pltpu.VMEM((chip, width), BF),
        pltpu.VMEM((chip, mine), BF), pltpu.VMEM((3, chip, mine), BF), pltpu.VMEM((chip + 8, mine), F32), pltpu.VMEM((8, mine), F32),
        pltpu.VMEM((CONV, width, mine), BF),
        pltpu.VMEM((KW - 1, chip + 8, 128), F32), pltpu.VMEM((depth, units), F32),
    )


def backward_call(n_dp, small_all, tokens, cotangent, keep, conv_w, feed_w, *rest):
    local, width = tokens.shape
    units, mine = feed_w.shape[2], conv_w.shape[2]
    chip, half, depth = 2 * local, mine // 2, width // n_dp
    over_y, over_x = sum(Y_FIRST), FEED - sum(Z_FIRST)
    pair = (pltpu.VMEM((NZ, 2 * depth, units), BF), pltpu.VMEM((depth, units), BF))

    def shaped(dims, kind=BF):
        return jax.ShapeDtypeStruct(dims, kind)

    def slots(n, *dims):
        return pltpu.VMEM((max(n, 1), *(dims if n else (NZ, 16, 128))), BF)

    dma = pltpu.SemaphoreType.DMA
    vmem, any_space = pl.BlockSpec(memory_space=pltpu.VMEM), pl.BlockSpec(memory_space=pl.ANY)
    return pl.pallas_call(
        functools.partial(backward_kernel, n_dp),
        name="backward_scatter",
        out_shape=(
            shaped((local, width)), shaped((local, width)), shaped((3, depth, half), F32), shaped((half, depth), F32),
            shaped((depth, units), F32), shaped((depth, units), F32), shaped((units, depth), F32), shaped((8, 128), F32),
        ),
        in_specs=[vmem] + [any_space] * (5 + len(rest)),
        out_specs=(any_space,) * 2 + (vmem,) * 6,
        scratch_shapes=[
            pltpu.VMEM((4 * local, units), BF), pltpu.VMEM((width, units), BF), pltpu.VMEM((over_x, NZ, depth, units), BF),
            pltpu.VMEM((over_x, NZ, depth, units), BF), *pair,
            slots(over_y, NZ, 2 * depth, half), slots(CONV - over_y, NZ, depth, mine), pltpu.VMEM((CONV, NZ, depth, half), BF),
            pltpu.VMEM((CONV, NZ, depth, half), BF), pltpu.VMEM((2, local, width), BF), pltpu.VMEM((2, local, width), BF),
            pltpu.VMEM((local, width), BF), pltpu.VMEM((local, width), F32),
            pltpu.VMEM((2, local, width), BF), pltpu.VMEM((2, local, width), BF), pltpu.VMEM((local, width), BF),
            pltpu.VMEM((local, width), BF), pltpu.VMEM((chip, width), BF),
            pltpu.VMEM((local, width), F32), pltpu.VMEM((local, width), BF), pltpu.VMEM((8, width), F32), pltpu.VMEM((n_dp, 8, 128), F32),
            pltpu.VMEM((2, n_dp, 8, 128), F32), pltpu.VMEM((2 * NZ, 8, 128), F32),
            dma((21,)), dma((FEED, NZ)), dma((FEED, NZ)), dma((FEED, NZ)), dma((FEED, NZ)), dma((CONV, NZ)), dma((CONV, NZ)),
            dma((CONV, NZ)), dma((CONV, NZ)), dma((CONV, NZ)), dma((CONV, NZ)), dma((10,)), dma((10,)), dma((9,)), dma((9,)),
        ],
        compiler_params=pltpu.CompilerParams(collective_id=1, has_side_effects=True, vmem_limit_bytes=63 << 20),
    )(small_all, tokens, cotangent, keep, conv_w, feed_w, *rest)


def finish_kernel(n, small, *refs):
    arrays, outs, held, in_sem, out_sem = refs[:n], refs[n : 2 * n + 3], refs[2 * n + 3 : 3 * n + 3], refs[-2], refs[-1]
    loads = [pltpu.make_async_copy(arrays[i], held[i], in_sem.at[i]) for i in range(n)]
    stores = [pltpu.make_async_copy(held[i], outs[i], out_sem.at[i]) for i in range(n)]
    for copy in loads:
        copy.start()
    outs[n][...] = small[0:1, :]
    outs[n + 1][...] = small[1:2, :]
    outs[n + 2][...] = small[2 : 2 + KW, :]
    for load, store in zip(loads, stores):
        load.wait()
        store.start()
    for copy in stores:
        copy.wait()


def finish_call(small, *arrays):
    vmem, any_space = pl.BlockSpec(memory_space=pltpu.VMEM), pl.BlockSpec(memory_space=pl.ANY)
    n = len(arrays)
    row = small.shape[1]
    return pl.pallas_call(
        functools.partial(finish_kernel, n),
        name="finish",
        out_shape=tuple(jax.ShapeDtypeStruct(a.shape, a.dtype) for a in arrays)
        + tuple(jax.ShapeDtypeStruct((r, row), F32) for r in (1, 1, KW)),
        in_specs=[vmem] + [any_space] * n,
        out_specs=(any_space,) * n + (vmem,) * 3,
        scratch_shapes=[pltpu.VMEM(a.shape, a.dtype) for a in arrays] + [pltpu.SemaphoreType.DMA((n,))] * 2,
        compiler_params=pltpu.CompilerParams(vmem_limit_bytes=62 << 20),
    )(small, *arrays)


def block(n_dp, tokens, doc_ids, mixer_norm, in_weight, conv_weight, out_weight, feed_norm, gate_weight, up_weight, down_weight, out_grad):
    small = jnp.concatenate(
        [mixer_norm[None], feed_norm[None], conv_weight, jnp.zeros((6 - KW, mixer_norm.shape[0]), BF)], axis=0).astype(F32)
    conv_w, feed_w, normed, small_all, cot, proj, mixer_in, hidden, two, acts, keep = forward_call(
        n_dp, tokens, out_grad, doc_ids, small, in_weight.transpose(1, 0, 2), out_weight, gate_weight, up_weight, down_weight)
    *large, small_g = backward_call(
        n_dp, small_all, tokens, out_grad, keep, conv_w, feed_w, normed, cot, proj, mixer_in, hidden, two, acts)
    output, input_grad, in_g, out_g, gate_g, up_g, down_g, mixer_g, feed_g, taps_g = finish_call(small_g, *large)
    return (output, input_grad, mixer_g[0], in_g.transpose(1, 0, 2), taps_g, out_g, feed_g[0], gate_g, up_g, down_g)


def shift_down(values, offset):
    if offset == 0:
        return values
    padding = jnp.zeros((offset,) + values.shape[1:], values.dtype)
    return jnp.concatenate([padding, values[:-offset]], axis=0)


def shift_up(values, offset):
    if offset == 0:
        return values
    padding = jnp.zeros((offset,) + values.shape[1:], values.dtype)
    return jnp.concatenate([values[offset:], padding], axis=0)


def tap_masks(doc_rows):
    total_rows = doc_rows.shape[0] * doc_rows.shape[1]
    tap_keep = [jnp.ones((total_rows,), jnp.float32)]
    for offset in range(1, KW):
        matching = doc_rows[:, offset:] == doc_rows[:, :-offset]
        leading = jnp.zeros((doc_rows.shape[0], offset), dtype=bool)
        matching = jnp.concatenate([leading, matching], axis=1)
        tap_keep.append(jnp.where(matching, 1.0, 0.0).astype(jnp.float32).reshape(total_rows))
    return jnp.stack(tap_keep)


def norm_back(grad_out, unit_rows, inverse, gain):
    scaled = grad_out * gain
    return inverse * (scaled - unit_rows * jnp.mean(scaled * unit_rows, axis=-1, keepdims=True))


def body(
    tokens,
    doc_ids,
    mixer_norm,
    in_weight,
    conv_weight,
    out_weight,
    feed_norm,
    gate_weight,
    up_weight,
    down_weight,
    out_grad,
):
    model_width = tokens.shape[1]
    gathered = (
        lax.all_gather(mixer_norm, "dp", axis=0, tiled=True),
        lax.all_gather(in_weight, "dp", axis=0, tiled=True),
        lax.all_gather(conv_weight, "dp", axis=1, tiled=True),
        lax.all_gather(out_weight, "dp", axis=1, tiled=True),
        lax.all_gather(feed_norm, "dp", axis=0, tiled=True),
        lax.all_gather(gate_weight, "dp", axis=0, tiled=True),
        lax.all_gather(up_weight, "dp", axis=0, tiled=True),
        lax.all_gather(down_weight, "dp", axis=1, tiled=True),
    )
    norm_one, in_full, conv_full, out_full, norm_two, gate_full, up_full, down_full = gathered
    channels = in_full.shape[2]
    channel_start = lax.axis_index("tensor") * channels
    tap_keep = tap_masks(doc_ids)
    conv_taps = lax.dynamic_slice_in_dim(conv_full, channel_start, channels, 1).astype(jnp.float32)
    inputs = tokens.astype(jnp.float32)
    inverse_one = lax.rsqrt(jnp.mean(inputs * inputs, axis=-1, keepdims=True) + epsilon)
    unit_one = inputs * inverse_one
    normed_local = (unit_one * norm_one.astype(jnp.float32)).astype(jnp.bfloat16)
    normed = lax.all_gather(normed_local, "tensor", axis=0, tiled=True)
    projected = jnp.einsum("td,dkc->tkc", normed, in_full, preferred_element_type=jnp.float32)
    input_gate = projected[:, 0]
    output_gate = projected[:, 1]
    values = projected[:, 2]
    mixed_input = input_gate * values
    convolved = sum(
        (
            tap_keep[offset][:, None] * conv_taps[offset][None, :] * shift_down(mixed_input, offset)
            for offset in range(KW)
        )
    )
    mixer_in = (output_gate * convolved).astype(jnp.bfloat16)
    mixer_out = lax.psum_scatter(
        jnp.dot(mixer_in, out_full, preferred_element_type=jnp.float32),
        "tensor",
        scatter_dimension=0,
        tiled=True,
    )
    hidden = inputs + mixer_out
    inverse_two = lax.rsqrt(jnp.mean(hidden * hidden, axis=-1, keepdims=True) + epsilon)
    unit_two = hidden * inverse_two
    normed_two_local = (unit_two * norm_two.astype(jnp.float32)).astype(jnp.bfloat16)
    normed_two = lax.all_gather(normed_two_local, "tensor", axis=0, tiled=True)
    gate_pre = jnp.dot(normed_two, gate_full, preferred_element_type=jnp.float32)
    upward = jnp.dot(normed_two, up_full, preferred_element_type=jnp.float32)
    activated = (jax.nn.silu(gate_pre) * upward).astype(jnp.bfloat16)
    feed_out = lax.psum_scatter(
        jnp.dot(activated, down_full, preferred_element_type=jnp.float32).astype(jnp.bfloat16),
        "tensor",
        scatter_dimension=0,
        tiled=True,
    ).astype(jnp.float32)
    output = (hidden + feed_out).astype(jnp.bfloat16)
    regathered = (
        lax.all_gather(mixer_norm, "dp", axis=0, tiled=True),
        lax.all_gather(in_weight, "dp", axis=0, tiled=True),
        lax.all_gather(conv_weight, "dp", axis=1, tiled=True),
        lax.all_gather(out_weight, "dp", axis=1, tiled=True),
        lax.all_gather(feed_norm, "dp", axis=0, tiled=True),
        lax.all_gather(gate_weight, "dp", axis=0, tiled=True),
        lax.all_gather(up_weight, "dp", axis=0, tiled=True),
        lax.all_gather(down_weight, "dp", axis=1, tiled=True),
    )
    norm_one_b, in_again, conv_again, out_again, norm_two_b, gate_again, up_again, down_again = (
        regathered
    )
    gain_one = norm_one_b.astype(jnp.float32)
    gain_two = norm_two_b.astype(jnp.float32)
    taps_again = lax.dynamic_slice_in_dim(conv_again, channel_start, channels, 1).astype(
        jnp.float32
    )
    sigmoid = jax.nn.sigmoid(gate_pre)
    cotangent = lax.all_gather(out_grad, "tensor", axis=0, tiled=True)
    down_grad = jnp.einsum("tf,td->fd", activated, cotangent, preferred_element_type=jnp.float32)
    grad_act = jnp.einsum("td,fd->tf", cotangent, down_again, preferred_element_type=jnp.float32)
    grad_gate = (grad_act * upward * sigmoid * (1.0 + gate_pre * (1.0 - sigmoid))).astype(
        jnp.bfloat16
    )
    grad_up = (grad_act * gate_pre * sigmoid).astype(jnp.bfloat16)
    gate_grad = jnp.einsum("td,tf->df", normed_two, grad_gate, preferred_element_type=jnp.float32)
    up_grad = jnp.einsum("td,tf->df", normed_two, grad_up, preferred_element_type=jnp.float32)
    grad_two = lax.psum_scatter(
        (
            jnp.einsum("tf,df->td", grad_gate, gate_again, preferred_element_type=jnp.float32)
            + jnp.einsum("tf,df->td", grad_up, up_again, preferred_element_type=jnp.float32)
        ).astype(jnp.bfloat16),
        "tensor",
        scatter_dimension=0,
        tiled=True,
    ).astype(jnp.float32)
    feed_gain_part = jnp.sum(grad_two * unit_two, axis=0)
    grad_hidden = out_grad.astype(jnp.float32) + norm_back(
        grad_two, unit_two, inverse_two, gain_two
    )
    grad_mix_local = grad_hidden.astype(jnp.bfloat16)
    grad_mix = lax.all_gather(grad_mix_local, "tensor", axis=0, tiled=True)
    out_grad_part = jnp.einsum("tc,td->cd", mixer_in, grad_mix, preferred_element_type=jnp.float32)
    grad_in = jnp.einsum("td,cd->tc", grad_mix, out_again, preferred_element_type=jnp.float32)
    grad_c = grad_in * convolved
    grad_conv = grad_in * output_gate
    grad_mixed = sum(
        (
            taps_again[offset][None, :] * shift_up(tap_keep[offset][:, None] * grad_conv, offset)
            for offset in range(KW)
        )
    )
    tap_grad = jnp.stack(
        [
            jnp.sum(tap_keep[offset][:, None] * grad_conv * shift_down(mixed_input, offset), axis=0)
            for offset in range(KW)
        ]
    )
    grad_projected = jnp.stack(
        [grad_mixed * values, grad_c, grad_mixed * input_gate], axis=1
    ).astype(jnp.bfloat16)
    in_grad_part = jnp.einsum(
        "td,tkc->dkc", normed, grad_projected, preferred_element_type=jnp.float32
    )
    grad_one = lax.psum_scatter(
        jnp.einsum(
            "tkc,dkc->td", grad_projected, in_again, preferred_element_type=jnp.float32
        ).astype(jnp.bfloat16),
        "tensor",
        scatter_dimension=0,
        tiled=True,
    ).astype(jnp.float32)
    mixer_gain_part = jnp.sum(grad_one * unit_one, axis=0)
    input_grad = (grad_hidden + norm_back(grad_one, unit_one, inverse_one, gain_one)).astype(
        jnp.bfloat16
    )
    conv_part = lax.dynamic_update_slice_in_dim(
        jnp.zeros((KW, model_width), jnp.float32), tap_grad, channel_start, 1
    )
    summed = (
        lax.psum_scatter(mixer_gain_part, "dp", scatter_dimension=0, tiled=True),
        lax.psum_scatter(in_grad_part, "dp", scatter_dimension=0, tiled=True),
        lax.psum_scatter(conv_part, "dp", scatter_dimension=1, tiled=True),
        lax.psum_scatter(out_grad_part, "dp", scatter_dimension=1, tiled=True),
        lax.psum_scatter(feed_gain_part, "dp", scatter_dimension=0, tiled=True),
        lax.psum_scatter(gate_grad, "dp", scatter_dimension=0, tiled=True),
        lax.psum_scatter(up_grad, "dp", scatter_dimension=0, tiled=True),
        lax.psum_scatter(down_grad, "dp", scatter_dimension=1, tiled=True),
    )
    (
        mixer_gain_sum,
        in_weight_grad,
        conv_sum,
        out_weight_grad,
        feed_gain_sum,
        gate_weight_grad,
        up_weight_grad,
        down_weight_grad,
    ) = summed
    mixer_norm_grad, conv_weight_grad, feed_norm_grad = lax.psum(
        (mixer_gain_sum, conv_sum, feed_gain_sum), "tensor"
    )
    return (
        output,
        input_grad,
        mixer_norm_grad,
        in_weight_grad,
        conv_weight_grad,
        out_weight_grad,
        feed_norm_grad,
        gate_weight_grad,
        up_weight_grad,
        down_weight_grad,
    )


def solution(mesh):
    in_specs = (
        P(("dp", "tensor"), None),
        P("dp", None),
        P("dp"),
        P("dp", None, "tensor"),
        P(None, "dp"),
        P("tensor", "dp"),
        P("dp"),
        P("dp", "tensor"),
        P("dp", "tensor"),
        P("tensor", "dp"),
        P(("dp", "tensor"), None),
    )
    out_specs = (
        P(("dp", "tensor"), None),
        P(("dp", "tensor"), None),
        P("dp"),
        P("dp", None, "tensor"),
        P(None, "dp"),
        P("tensor", "dp"),
        P("dp"),
        P("dp", "tensor"),
        P("dp", "tensor"),
        P("tensor", "dp"),
    )
    n_dp = mesh.shape["dp"]
    fits = n_dp == 2 * NZ and mesh.shape["tensor"] == 4
    step = functools.partial(block, n_dp) if fits else body
    return jax.shard_map(step, mesh=mesh, in_specs=in_specs, out_specs=out_specs, check_vma=False)
```

```python
import functools

import jax
import jax.numpy as jnp
from jax import lax
from jax.experimental import pallas as pl
from jax.experimental.pallas import tpu as pltpu
from jax.sharding import PartitionSpec as P

KW = 3
MESH = pl.DeviceIdType.MESH
BF = jnp.bfloat16
F32 = jnp.float32

epsilon = 1e-05

NZ = 4
CONV = 4
FEED = 3
Y_LAST = (True, True, True, False)
X_FIRST = (False, False, True)
Z_FIRST = (False, True, False)
Y_FIRST = (True, True, False, False)


def nn(a, b):
    return lax.dot_general(a, b, (((1,), (0,)), ((), ())), preferred_element_type=F32)


def nt(a, b):
    return lax.dot_general(a, b, (((1,), (1,)), ((), ())), preferred_element_type=F32)


def tn(a, b):
    return lax.dot_general(a, b, (((0,), (0,)), ((), ())), preferred_element_type=F32)


class Place:
    def __init__(self):
        self.dp = lax.axis_index("dp")
        self.t = lax.axis_index("tensor")
        self.z, self.x = lax.div(self.dp, 2), lax.rem(self.dp, 2)
        self.y, self.c = lax.div(self.t, 2), lax.rem(self.t, 2)
        self.over_x = (self.z * 2 + 1 - self.x, self.t)
        self.over_y = (self.dp, (1 - self.y) * 2 + self.c)
        self.over_c = (self.dp, self.y * 2 + 1 - self.c)
        self.t_y = (1 - self.y) * 2 + self.c
        self.t_c = self.y * 2 + 1 - self.c
        self.t_yc = (1 - self.y) * 2 + 1 - self.c
        self.middle = lax.rem(lax.div(self.z + 1, 2), 2) == 1

    def zs(self, k):
        if k == 0:
            return self.z
        if k == 1:
            return self.z + 1 - 2 * lax.rem(self.z, 2)
        if k == 2:
            return lax.rem(self.z + 2, NZ)
        return NZ - 1 - self.z

    def over_z(self, k):
        return (self.zs(k) * 2 + self.x, self.t)


def greet(place, n_dp):
    barrier = pltpu.get_barrier_semaphore()
    for k in range(1, n_dp):
        peer = (lax.rem(place.dp + k, n_dp), place.t)
        pl.semaphore_signal(barrier, inc=1, device_id=peer, device_id_type=MESH)
    for peer in (place.over_c, place.over_y):
        pl.semaphore_signal(barrier, inc=1, device_id=peer, device_id_type=MESH)
    pl.semaphore_wait(barrier, n_dp + 1)


def remote(src, dst, send_sem, recv_sem, peer):
    return pltpu.make_async_remote_copy(
        src_ref=src, dst_ref=dst, send_sem=send_sem, recv_sem=recv_sem, device_id=peer, device_id_type=MESH
    )


def send(*what):
    copy = remote(*what)
    copy.start()
    return copy


def arrived(ref, sem, peer):
    pltpu.make_async_remote_copy(
        src_ref=ref, dst_ref=ref, send_sem=sem, recv_sem=sem, device_id=peer, device_id_type=MESH
    ).wait_recv()


def rows(start, size):
    return pl.ds(pl.multiple_of(start, size), size)


def forward_kernel(
    n_dp,
    tokens, cotangent, doc_rows, small, in_own, out_own, gate_own, up_own, down_own,
    conv_out, feed_out, normed_out, small_out, cot_out, proj_out, mixer_out, hidden_out, two_out, acts_out, keep_out,
    conv_w, feed_w, normed, small_all, mixed_pad, c_keep, proj, mixer_in, part_send, part_recv,
    hidden, two, acts, out_turned, down_turned, keep,
    own_sem, z_send, z_recv, x_send, x_recv, y_send, y_recv, fz_send, fz_recv, fx_send, fx_recv,
    s_send, s_recv, a_send, a_recv, out_sem,
):
    place = Place()
    z, x, y, c, t = place.z, place.x, place.y, place.c, place.t
    depth = gate_own.shape[0]
    local, width = tokens.shape
    chip = 2 * local
    half = in_own.shape[2]
    mine = 2 * half
    tile, pad = 256, 8
    blocks = (t, place.t_c, place.t_y, place.t_yc)
    sends = []
    copies = []
    owned = {}

    def post(make, when=None):
        if when is None:
            make().start()
        else:
            pl.when(when)(lambda: make().start())
        sends.append((make, when))

    def keep_own(src, dst, index):
        owned[index] = pltpu.make_async_copy(src, dst, own_sem.at[index])
        owned[index].start()

    def out(src, dst):
        copy = pltpu.make_async_copy(src, dst, out_sem.at[len(copies)])
        copy.start()
        copies.append(copy)

    def conv_part(j, dp, n, side):
        col = slice(None) if side is None else rows(side * half, half)
        return conv_w.at[j, rows(dp * depth, n * depth), col]

    def feed_part(w, dp, n=1):
        return feed_w.at[w, rows(dp * depth, n * depth), :]

    conv_own = [in_own.at[0], in_own.at[1], in_own.at[2], out_turned]
    feed_own = [gate_own, up_own, down_turned]

    def along_z(src, part, send_sems, recv_sems, index):
        for k in (2, 3, 1):
            post(lambda k=k: remote(src, part(z), send_sems.at[index, k], recv_sems.at[index, z], place.over_z(k)),
                 place.middle if k == 3 else None)

    def from_z(part, send_sems, recv_sems, index, k):
        zk = place.zs(k)
        arrived(part(zk), recv_sems.at[index, zk], place.over_z(k))
        if k == 2:
            post(lambda: remote(part(zk), part(zk), send_sems.at[index, 0], recv_sems.at[index, zk], place.over_z(1)), place.middle)

    def conv_z(j):
        return lambda zk: conv_part(j, zk * 2 + x, 1, y)

    def feed_z(w):
        if X_FIRST[w]:
            return lambda zk: feed_part(w, zk * 2, 2)
        return lambda zk: feed_part(w, zk * 2 + x)

    def conv_second(j, k, src=None):
        zk = place.zs(k)
        part = conv_part(j, zk * 2 + x, 1, y)
        src = part if src is None else src
        if Y_LAST[j]:
            post(lambda: remote(src, part, x_send.at[j, zk], x_recv.at[j, zk], place.over_x))
        else:
            post(lambda: remote(src, part, y_send.at[j, zk], y_recv.at[j, zk], place.over_y))

    def feed_x(w, k, src=None):
        zk = place.zs(k)
        part = feed_part(w, zk * 2 + x)
        src = part if src is None else src
        post(lambda: remote(src, part, fx_send.at[w, zk], fx_recv.at[w, zk], place.over_x))

    def cown(j):
        along_z(conv_own[j], conv_z(j), z_send, z_recv, j)
        conv_second(j, 0, conv_own[j])

    def cz(j, k):
        from_z(conv_z(j), z_send, z_recv, j, k)
        conv_second(j, k)

    def ct(j, k):
        zk = place.zs(k)
        if k == 0:
            owned[j].wait()
        if Y_LAST[j]:
            arrived(conv_part(j, zk * 2 + 1 - x, 1, y), x_recv.at[j, zk], place.over_x)
            pair = conv_part(j, zk * 2, 2, y)
            post(lambda: remote(pair, pair, y_send.at[j, zk], y_recv.at[j, zk], place.over_y))
        else:
            arrived(conv_part(j, zk * 2 + x, 1, 1 - y), y_recv.at[j, zk], place.over_y)
            pair = conv_part(j, zk * 2 + x, 1, None)
            post(lambda: remote(pair, pair, x_send.at[j, zk], x_recv.at[j, zk], place.over_x))

    def fx(w):
        feed_x(w, 0, feed_own[w])

    def fz(w):
        if X_FIRST[w]:
            arrived(feed_part(w, z * 2 + 1 - x), fx_recv.at[w, z], place.over_x)
            owned[CONV + w].wait()
            along_z(feed_part(w, z * 2, 2), feed_z(w), fz_send, fz_recv, w)
        else:
            along_z(feed_own[w], feed_z(w), fz_send, fz_recv, w)

    def fp(w, k):
        from_z(feed_z(w), fz_send, fz_recv, w, k)
        if not X_FIRST[w]:
            feed_x(w, k)

    def feed_ready(w):
        if not X_FIRST[w]:
            for k in range(NZ):
                zk = place.zs(k)
                arrived(feed_part(w, zk * 2 + 1 - x), fx_recv.at[w, zk], place.over_x)
            owned[CONV + w].wait()
        out(feed_w.at[w], feed_out.at[w])

    def cot_block(block):
        return cot_out.at[rows(block * local, local), :]

    def cotc():
        post(lambda: remote(cotangent, cot_block(t), a_send.at[0], a_recv.at[0], place.over_c))

    def coty():
        post(lambda: remote(cotangent, cot_block(t), a_send.at[2], a_recv.at[2], place.over_y))

    def cotf():
        there = cot_block(place.t_y)
        arrived(there, a_recv.at[2], place.over_y)
        post(lambda: remote(there, there, a_send.at[6], a_recv.at[6], place.over_c))

    def turn():
        down_turned[...] = jnp.transpose(down_own[...])
        for w in range(FEED):
            keep_own(feed_own[w], feed_part(w, place.dp), CONV + w)
        own = doc_rows[pl.ds(y, 1), :].astype(F32)
        position = lax.broadcasted_iota(jnp.int32, (1, chip), 1)
        for k in range(1, KW):
            same = jnp.where((own == pltpu.roll(own, k, 1)) & (position >= k), 1.0, 0.0)
            keep[k - 1, 0:chip, :] = jnp.transpose(jnp.broadcast_to(same, (128, chip)))
            keep[k - 1, chip : chip + pad, :] = jnp.zeros((pad, 128), F32)
        out(keep, keep_out)

    def gain(r):
        return jnp.concatenate([small_all[d, r : r + 1, :] for d in range(n_dp)], axis=1)

    def norm():
        for k in range(1, n_dp):
            peer = lax.rem(place.dp + k, n_dp)
            arrived(small_all.at[peer], s_recv.at[peer], (peer, t))
        inputs = tokens[...].astype(F32)
        inverse = lax.rsqrt(jnp.mean(inputs * inputs, axis=-1, keepdims=True) + epsilon)
        normed[rows(c * local, local), :] = (inputs * inverse * gain(0)).astype(BF)
        own = normed.at[rows(c * local, local), :]
        post(lambda: remote(own, own, a_send.at[1], a_recv.at[1], place.over_c))

    def p1():
        arrived(normed.at[rows((1 - c) * local, local), :], a_recv.at[1], place.over_c)
        for j in range(CONV):
            for k in range(NZ):
                zk = place.zs(k)
                if Y_LAST[j]:
                    arrived(conv_part(j, zk * 2, 2, 1 - y), y_recv.at[j, zk], place.over_y)
                else:
                    arrived(conv_part(j, zk * 2 + 1 - x, 1, None), x_recv.at[j, zk], place.over_x)
        out(conv_w, conv_out)
        out(normed, normed_out)
        mixed_pad[0:pad, :] = jnp.zeros((pad, mine), F32)

        def project(i, carry):
            at = rows(i * tile, tile)
            lhs = normed[at, :]
            b = nn(lhs, conv_w[0])
            proj[0, at, :] = b.astype(BF)
            v = nn(lhs, conv_w[2])
            proj[2, at, :] = v.astype(BF)
            mixed_pad[pl.ds(pl.multiple_of(i * tile + pad, 8), tile), :] = b * v
            g = nn(lhs, conv_w[1])
            proj[1, at, :] = g.astype(BF)
            c_keep[at, :] = g
            return carry

        lax.fori_loop(0, chip // tile, project, 0)

    def p2():
        taps = []
        for r in range(2, 2 + KW):
            taps.append(jnp.concatenate(
                [small_all[side * 4 + 2 * c + i, r : r + 1, :] for side in range(2) for i in range(2)], axis=1))

        def convolve(i, carry):
            at = rows(i * tile, tile)
            window = mixed_pad[pl.ds(pl.multiple_of(i * tile, 8), tile + pad), :]
            total = taps[0] * window[pad:, :]
            for k in range(1, KW):
                mask = jnp.concatenate([keep[k - 1, at, :]] * (mine // 128), axis=1)
                total = total + mask * taps[k] * window[pad - k : pad - k + tile, :]
            proj[3, at, :] = total.astype(BF)
            mixer_in[at, :] = (c_keep[at, :] * total).astype(BF)
            return carry

        lax.fori_loop(0, chip // tile, convolve, 0)
        out(proj, proj_out)
        out(mixer_in, mixer_out)
        part_send[...] = nt(mixer_in[rows((1 - c) * local, local), :], conv_w[3]).astype(BF)
        post(lambda: remote(part_send, part_recv, a_send.at[3], a_recv.at[3], place.over_c))
        hidden[...] = tokens[...].astype(F32) + nt(mixer_in[rows(c * local, local), :], conv_w[3])

    def p3():
        arrived(part_recv, a_recv.at[3], place.over_c)
        total = hidden[...] + part_recv[...].astype(F32)
        hidden[...] = total
        inverse = lax.rsqrt(jnp.mean(total * total, axis=-1, keepdims=True) + epsilon)
        two[rows(t * local, local), :] = (total * inverse * gain(1)).astype(BF)
        own = two.at[rows(t * local, local), :]
        post(lambda: remote(own, own, a_send.at[5], a_recv.at[5], place.over_y))
        post(lambda: remote(own, own, a_send.at[4], a_recv.at[4], place.over_c))
        out(hidden, hidden_out)

    def t2():
        there = two.at[rows(place.t_y * local, local), :]
        arrived(there, a_recv.at[5], place.over_y)
        post(lambda: remote(there, there, a_send.at[7], a_recv.at[7], place.over_c))

    def g(b):
        if b == 0:
            feed_ready(0)
        if b == 1:
            arrived(two.at[rows(place.t_c * local, local), :], a_recv.at[4], place.over_c)
        if b == 3:
            arrived(two.at[rows(place.t_yc * local, local), :], a_recv.at[7], place.over_c)

        def step(i, carry):
            at = rows(blocks[b] * local + i * tile, tile)
            gate = nn(two[at, :], feed_w[0])
            s = jax.nn.sigmoid(gate)
            silu = gate * s
            acts[1, at, :] = (s + silu * (1.0 - s)).astype(BF)
            acts[2, at, :] = silu.astype(BF)
            return carry

        lax.fori_loop(0, local // tile, step, 0)

    def u(b):
        if b == 0:
            feed_ready(1)

        def step(i, carry):
            at = rows(blocks[b] * local + i * tile, tile)
            upward = nn(two[at, :], feed_w[1])
            acts[0, at, :] = (acts[2, at, :].astype(F32) * upward).astype(BF)
            acts[1, at, :] = (acts[1, at, :].astype(F32) * upward).astype(BF)
            return carry

        lax.fori_loop(0, local // tile, step, 0)
        at = rows(blocks[b] * local, local)
        out(acts.at[:, at, :], acts_out.at[:, at, :])
        out(two.at[at, :], two_out.at[at, :])

    small_all[place.dp] = small[...]
    out_turned[...] = jnp.transpose(out_own[...])
    greet(place, n_dp)
    for k in range(1, n_dp):
        post(lambda k=k: remote(small, small_all.at[place.dp], s_send.at[k], s_recv.at[place.dp], (lax.rem(place.dp + k, n_dp), t)))
    for j in range(CONV):
        keep_own(conv_own[j], conv_part(j, place.dp, 1, y), j)
    keep_own(cotangent, cot_block(t), CONV + FEED)
    cown(1)
    cown(3)
    cown(0)
    fx(0)
    ct(1, 0)
    cz(1, 2)
    ct(0, 0)
    cown(2)
    cz(3, 2)
    cz(3, 1)
    cz(1, 1)
    cz(1, 3)
    ct(1, 2)
    turn()
    cz(0, 2)
    cz(3, 3)
    cz(0, 1)
    ct(1, 3)
    cz(2, 2)
    fz(0)
    ct(2, 0)
    ct(3, 2)
    cz(2, 1)
    fx(2)
    fz(1)
    cz(2, 3)
    cz(0, 3)
    ct(0, 2)
    norm()
    ct(1, 1)
    ct(2, 1)
    ct(0, 1)
    ct(3, 0)
    ct(2, 3)
    ct(3, 1)
    ct(2, 2)
    ct(3, 3)
    ct(0, 3)
    cotc()
    fp(0, 1)
    coty()
    fp(0, 2)
    p1()
    fp(1, 2)
    fp(1, 1)
    fp(0, 3)
    fz(2)
    p2()
    p3()
    fp(1, 3)
    cotf()
    g(0)
    fx(1)
    fp(2, 2)
    g(1)
    u(0)
    u(1)
    t2()
    g(2)
    u(2)
    fp(2, 1)
    g(3)
    u(3)
    fp(2, 3)
    feed_ready(2)
    small_out[...] = small_all[...]
    arrived(cot_block(place.t_c), a_recv.at[0], place.over_c)
    arrived(cot_block(place.t_yc), a_recv.at[6], place.over_c)
    owned[CONV + FEED].wait()
    for make, when in sends:
        if when is None:
            make().wait_send()
        else:
            pl.when(when)(lambda make=make: make().wait_send())
    for copy in copies:
        copy.wait()


def forward_call(n_dp, *operands):
    tokens, _, _, _, in_own, _, gate_own, _, _ = operands
    local, width = tokens.shape
    half, units = in_own.shape[2], gate_own.shape[1]
    chip, group, mine = 2 * local, 4 * local, 2 * half

    def shaped(dims, kind=BF):
        return jax.ShapeDtypeStruct(dims, kind)

    dma = pltpu.SemaphoreType.DMA
    vmem, any_space = pl.BlockSpec(memory_space=pltpu.VMEM), pl.BlockSpec(memory_space=pl.ANY)
    return pl.pallas_call(
        functools.partial(forward_kernel, n_dp),
        name="gather_forward",
        out_shape=(
            shaped((CONV, width, mine)), shaped((FEED, width, units)), shaped((chip, width)), shaped((n_dp, 8, 128), F32),
            shaped((group, width)), shaped((4, chip, mine)), shaped((chip, mine)), shaped((local, width), F32),
            shaped((group, width)), shaped((3, group, units)), shaped((KW - 1, chip + 8, 128), F32),
        ),
        in_specs=[vmem] * 4 + [any_space, vmem, any_space, any_space, vmem],
        out_specs=tuple(vmem if i == 3 else any_space for i in range(11)),
        scratch_shapes=[
            pltpu.VMEM((CONV, width, mine), BF), pltpu.VMEM((FEED, width, units), BF), pltpu.VMEM((chip, width), BF),
            pltpu.VMEM((n_dp, 8, 128), F32), pltpu.VMEM((chip + 8, mine), F32),
            pltpu.VMEM((chip, mine), F32), pltpu.VMEM((4, chip, mine), BF), pltpu.VMEM((chip, mine), BF),
            pltpu.VMEM((local, width), BF), pltpu.VMEM((local, width), BF), pltpu.VMEM((local, width), F32),
            pltpu.VMEM((group, width), BF), pltpu.VMEM((3, group, units), BF),
            pltpu.VMEM((width // n_dp, half), BF), pltpu.VMEM((width // n_dp, units), BF), pltpu.VMEM((KW - 1, chip + 8, 128), F32),
            dma((8,)), dma((CONV, NZ)), dma((CONV, NZ)), dma((CONV, NZ)), dma((CONV, NZ)), dma((CONV, NZ)), dma((CONV, NZ)),
            dma((FEED, NZ)), dma((FEED, NZ)), dma((FEED, NZ)), dma((FEED, NZ)),
            dma((n_dp,)), dma((n_dp,)), dma((8,)), dma((8,)), dma((20,)),
        ],
        compiler_params=pltpu.CompilerParams(collective_id=0, has_side_effects=True, vmem_limit_bytes=62 << 20),
    )(*operands)


def backward_kernel(
    n_dp,
    small_all, tokens_in, cot_own_in, keep_in, conv_in, feed_in, normed_in, cot_in, proj_in, mixer_in_hbm, hidden_in, two_in, acts_in,
    output, input_grad, in_grad, out_grad, gate_grad, up_grad, down_grad, small_grad,
    act, g_down, x_got, z_got, pair_got, x_last, c_got_y, c_got_x, c_two, c_z, two_send, two_recv, two_y, own_two,
    down_send, down_recv, down_y, down_own, grad_mix, hidden, token_rows, feed_gain, small_sum, small_got, small_z,
    load_sem, fx_send, fx_recv, fz_send, fz_recv, c1_send, c1_recv, c2_send, c2_recv, c3_send, c3_recv,
    s_send, s_recv, a_send, a_recv,
):
    place = Place()
    z, x, y, c, t = place.z, place.x, place.y, place.c, place.t
    depth, units = gate_grad.shape
    local, width = own_two.shape
    chip = 2 * local
    half = in_grad.shape[2]
    mine = 2 * half
    tile = 256
    sends = []

    def post(make):
        make().start()
        sends.append(make)
        return make

    def load(src, dst, index):
        copy = pltpu.make_async_copy(src, dst, load_sem.at[index])
        copy.start()
        return copy

    def g_rows(w, start, size):
        if w == 2:
            return g_down.at[rows(start, size), :]
        return act.at[rows(w * width + start, size), :]

    def x_slot(w):
        return w - sum(Z_FIRST[:w])

    def pair_rows(w, k):
        return g_rows(w, place.zs(k) * 2 * depth, 2 * depth)

    def pair_add(w, k, slots):
        def step(i, carry):
            at = rows(i * 64, 64)
            held = pair_rows(w, k).at[at, :]
            total = held[...].astype(F32)
            for slot in slots:
                total = total + pair_got[slot, at, :].astype(F32)
            held[...] = total.astype(BF)
            return carry

        lax.fori_loop(0, 2 * depth // 64, step, 0)

    def pair_send(w, k):
        return z_remote(pair_rows(w, k), pair_got, fz_send.at[w], fz_recv.at[w], k)

    def m(w, k):
        if Z_FIRST[w]:
            if k == 2:
                @pl.when(place.middle)
                def _():
                    arrived(pair_got.at[0], fz_recv.at[w, 0], place.over_z(1))
                    pair_add(w, k, (0,))
                    pair_send(w, k).start()

            return
        zk = place.zs(k)
        got = x_got.at[x_slot(w), zk]
        arrived(got, fx_recv.at[w, zk], place.over_x)
        if k:
            got[...] = (g_rows(w, (zk * 2 + x) * depth, depth)[...].astype(F32) + got[...].astype(F32)).astype(BF)

            def add(more):
                held = x_got.at[x_slot(w), place.zs(k)]
                held[...] = (held[...].astype(F32) + more[...].astype(F32)).astype(BF)

            if k == 2:
                @pl.when(place.middle)
                def _():
                    arrived(z_got.at[x_slot(w), 0], fz_recv.at[w, 0], place.over_z(1))
                    add(z_got.at[x_slot(w), 0])

            post(lambda: z_remote(x_got.at[x_slot(w), place.zs(k)], z_got.at[x_slot(w)], fz_send.at[w], fz_recv.at[w], k))

    def z_remote(held, got, sends_at, recvs_at, k):
        if k == 3:
            slot = jnp.where(place.middle, 3, 0)
            peer = (jnp.where(place.middle, place.zs(3), place.zs(1)) * 2 + x, t)
            return remote(held, got.at[slot], sends_at.at[k], recvs_at.at[slot], peer)
        return remote(held, got.at[k], sends_at.at[k], recvs_at.at[k], place.over_z(k))

    def z_sum(total, got, recvs_at):
        for k in (1, 2):
            arrived(got.at[k], recvs_at.at[k], place.over_z(k))
            total = total + got[k].astype(F32)
        return total

    def z_last(ref, got, recvs_at):
        @pl.when(place.middle)
        def _():
            arrived(got.at[3], recvs_at.at[3], place.over_z(3))
            ref[...] = ref[...] + got[3].astype(F32)

    def gain(r):
        return jnp.concatenate([small_all[d, r : r + 1, :] for d in range(n_dp)], axis=1)

    def norm_back(grad, unit, inverse, scale):
        scaled = grad * scale
        return inverse * (scaled - unit * jnp.mean(scaled * unit, axis=-1, keepdims=True))

    def rms(values):
        return lax.rsqrt(jnp.mean(values * values, axis=-1, keepdims=True) + epsilon)

    def send_slot(i):
        return lambda: remote(two_send.at[i], two_recv.at[i], a_send.at[1 + i], a_recv.at[1 + i], place.over_c)

    first_slot = send_slot(0)

    def fetch_hidden():
        return pltpu.make_async_copy(hidden_in, hidden, load_sem.at[9])

    def fetch_cotangent():
        return pltpu.make_async_copy(cot_own_in, token_rows, load_sem.at[10])

    def fetch_tokens():
        return pltpu.make_async_copy(tokens_in, token_rows, load_sem.at[11])

    def n2():
        fetch_hidden().wait()
        fetch_cotangent().wait()
        arrived(two_y, a_recv.at[3], place.over_y)
        arrived(two_recv.at[1], a_recv.at[2], place.over_c)
        scale = gain(1)

        def step(i, carry):
            at = rows(i * 128, 128)
            grad_two = own_two[at, :] + two_recv[1, at, :].astype(F32) + two_y[at, :].astype(F32)
            values = hidden[at, :]
            inverse = rms(values)
            unit = values * inverse
            grad_hidden = token_rows[at, :].astype(F32) + norm_back(grad_two, unit, inverse, scale)
            hidden[at, :] = grad_hidden
            grad_mix[rows(c * local + i * 128, 128), :] = grad_hidden.astype(BF)
            return carry + jnp.sum(grad_two * unit, axis=0, keepdims=True)

        feed_gain[0:1, :] = lax.fori_loop(0, local // 128, step, jnp.zeros((1, width), F32))
        fetch_tokens().start()

        def make():
            own = grad_mix.at[rows(c * local, local), :]
            return remote(own, own, a_send.at[4], a_recv.at[4], place.over_c)

        post(make)

    def feed_phase(feed_w, cot, acts):
        plan = [(acts_in.at[0], act), (cot_in, cot), (feed_in.at[2], feed_w.at[2]), (acts_in.at[1], acts.at[0]),
                (acts_in.at[2], acts.at[1]), (feed_in.at[pl.ds(0, 2)], feed_w.at[pl.ds(0, 2)])]
        loads = {}
        waited = set()

        def begin(*which):
            for i in which:
                if i not in loads:
                    loads[i] = load(*plan[i], i)

        def loaded(*which):
            begin(*which)
            for i in which:
                if i not in waited:
                    waited.add(i)
                    loads[i].wait()
            if len(loads) < len(plan):
                begin(*range(len(plan)))
                fetch_hidden().start()
                fetch_cotangent().start()

        begin(0, 1)
        greet(place, n_dp)

        def g(w, k):
            at = rows(place.zs(k) * 2 * depth, 2 * depth)
            if w == 2:
                loaded(0, 1)
                g_down[at, :] = tn(cot[:, at], act[...]).astype(BF)
            else:
                if "two" not in waited:
                    waited.add("two")
                    load(two_in, cot, 8).wait()
                act[rows(w * width + place.zs(k) * 2 * depth, 2 * depth), :] = tn(cot[:, at], acts[w]).astype(BF)

            def make():
                zk = place.zs(k)
                return remote(
                    g_rows(w, (zk * 2 + 1 - x) * depth, depth), x_got.at[x_slot(w), zk], fx_send.at[w, zk], fx_recv.at[w, zk], place.over_x)

            if not Z_FIRST[w]:
                post(make)
            elif k == 2:
                pl.when(jnp.logical_not(place.middle))(lambda: pair_send(w, k).start())
                sends.append(lambda: pair_send(w, k))
            elif k:
                post(lambda: pair_send(w, k))

        def back(block, store):
            loaded(1, 2, 3, 4, 5)

            def step(i, carry):
                at = rows(block * local + i * tile, tile)
                grad_act = nn(cot[at, :], feed_w[2])
                grad_gate = (grad_act * acts[0, at, :].astype(F32)).astype(BF)
                acts[0, at, :] = grad_gate
                grad_up = (grad_act * acts[1, at, :].astype(F32)).astype(BF)
                acts[1, at, :] = grad_up
                store(rows(i * tile, tile), nt(grad_gate, feed_w[0]) + nt(grad_up, feed_w[1]))
                return carry

            lax.fori_loop(0, local // tile, step, 0)

        def to_slot(i):
            def store(at, value):
                two_send[i, at, :] = value.astype(BF)

            return store

        def to_own(at, value):
            own_two[at, :] = value

        def a_yc():
            back(place.t_yc, to_slot(0))
            post(first_slot)

        def a_c():
            back(place.t_c, to_slot(1))
            post(send_slot(1))

        def a_y():
            back(place.t_y, to_own)

        def ay():
            arrived(two_recv.at[0], a_recv.at[1], place.over_c)
            two_recv[0] = (own_two[...] + two_recv[0].astype(F32)).astype(BF)
            post(lambda: remote(two_recv.at[0], two_y, a_send.at[3], a_recv.at[3], place.over_y))

        def a_o():
            back(t, to_own)

        def down(block):
            loaded(0, 2)
            return nt(act[rows(block * local, local), :], feed_w[2]).astype(BF)

        def d_yc():
            down_send[0] = down(place.t_yc)
            post(lambda: remote(down_send.at[0], down_recv.at[0], a_send.at[6], a_recv.at[6], place.over_c))

        def d_c():
            down_send[1] = down(place.t_c)
            post(lambda: remote(down_send.at[1], down_recv.at[1], a_send.at[7], a_recv.at[7], place.over_c))

        def d_y():
            down_own[...] = down(place.t_y)

        def dy():
            arrived(down_recv.at[0], a_recv.at[6], place.over_c)
            down_recv[0] = (down_own[...].astype(F32) + down_recv[0].astype(F32)).astype(BF)
            post(lambda: remote(down_recv.at[0], down_y, a_send.at[8], a_recv.at[8], place.over_y))

        def d_o():
            down_own[...] = down(t)

        d_y()
        d_yc()
        g(2, 3)
        a_yc()
        g(2, 2)
        a_y()
        m(2, 3)
        g(2, 1)
        ay()
        g(2, 0)
        dy()
        d_o()
        m(2, 2)
        a_o()
        m(2, 1)
        d_c()
        a_c()
        m(2, 0)
        g(1, 3)
        g(1, 1)
        g(0, 3)
        g(0, 1)
        m(0, 3)
        g(1, 2)
        n2()
        g(0, 0)
        g(1, 0)
        g(0, 2)

    pl.run_scoped(
        feed_phase,
        pltpu.VMEM((FEED, width, units), BF), pltpu.VMEM((4 * local, width), BF), pltpu.VMEM((2, 4 * local, units), BF),
    )

    def conv_phase(conv_w, proj, normed, mixer_in, grad_proj, pad_grad, tap_sum, g_conv, keep, stage):
        plan = [(conv_in.at[3], conv_w.at[3]), (proj_in.at[3], proj.at[3]), (proj_in.at[1], proj.at[1]), (mixer_in_hbm, mixer_in),
                (normed_in, normed), (proj_in.at[0], proj.at[0]), (proj_in.at[2], proj.at[2]), (keep_in, keep),
                (conv_in.at[pl.ds(0, 3)], conv_w.at[pl.ds(0, 3)])]
        loads = {}
        waited = set()
        stores = []

        def begin(*which):
            for i in which:
                if i not in loads:
                    loads[i] = load(*plan[i], 12 + i)

        def loaded(*which):
            for i in which:
                if i not in waited:
                    waited.add(i)
                    loads[i].wait()
            begin(*range(len(plan)))

        begin(0, 1, 2)

        def taps():
            return [jnp.concatenate([small_all[side * 4 + 2 * c + i, r : r + 1, :] for side in range(2) for i in range(2)], axis=1)
                    for r in range(2, 2 + KW)]

        def gm():
            loaded(0, 1, 2)
            arrived(grad_mix.at[rows((1 - c) * local, local), :], a_recv.at[4], place.over_c)
            pad_grad[pl.ds(chip, 8), :] = jnp.zeros((8, mine), F32)

            def step(i, carry):
                at = rows(i * tile, tile)
                grad_in = nn(grad_mix[at, :], conv_w[3])
                grad_proj[1, at, :] = (grad_in * proj[3, at, :].astype(F32)).astype(BF)
                pad_grad[at, :] = grad_in * proj[1, at, :].astype(F32)
                return carry

            lax.fori_loop(0, chip // tile, step, 0)

        def c1_slot(j, zk):
            if Y_FIRST[j]:
                return c_got_y.at[sum(Y_FIRST[:j]), zk]
            return c_got_x.at[j - sum(Y_FIRST[:j]), zk]

        def w(j):
            if j == 3:
                loaded(3)
                for part in (slice(0, width // 2), slice(width // 2, width)):
                    g_conv[j, part, :] = tn(grad_mix[:, part], mixer_in[...]).astype(BF)
            else:
                loaded(4)
                for part in (slice(0, width // 2), slice(width // 2, width)):
                    g_conv[j, part, :] = tn(normed[:, part], grad_proj[j]).astype(BF)
            for k in (2, 1, 3, 0):
                zk = place.zs(k)
                if Y_FIRST[j]:
                    src, peer = g_conv.at[j, rows(zk * 2 * depth, 2 * depth), rows((1 - y) * half, half)], place.over_y
                else:
                    src, peer = g_conv.at[j, rows((zk * 2 + 1 - x) * depth, depth), :], place.over_x
                post(lambda src=src, peer=peer, zk=zk: remote(src, c1_slot(j, zk), c1_send.at[j, zk], c1_recv.at[j, zk], peer))

        def h2():
            loaded(5, 6, 7)
            tap = taps()
            tap_sum[...] = jnp.zeros_like(tap_sum)
            size = 128

            def step(i, carry):
                at = rows(i * size, size)
                wide = pl.ds(pl.multiple_of(i * size, 8), size + 8)
                window = pad_grad[wide, :]
                b, v = proj[0, at, :].astype(F32), proj[2, at, :].astype(F32)
                mixed = b * v
                now = window[:size, :]
                total = tap[0] * now
                tap_sum[0:1, :] += jnp.sum(now * mixed, axis=0, keepdims=True)
                for k in range(1, KW):
                    mask = jnp.concatenate([keep[k - 1, wide, :]] * (mine // 128), axis=1)
                    ahead = (mask * window)[k : k + size, :]
                    total = total + tap[k] * ahead
                    tap_sum[k : k + 1, :] += jnp.sum(ahead * mixed, axis=0, keepdims=True)
                grad_proj[0, at, :] = (total * v).astype(BF)
                grad_proj[2, at, :] = (total * b).astype(BF)
                return carry

            lax.fori_loop(0, chip // size, step, 0)

        def first_grad(block, store):
            def step(i, carry):
                at = rows(block * local + i * tile, tile)
                store(rows(i * tile, tile), nt(grad_proj[0, at, :], conv_w[0]) + nt(grad_proj[1, at, :], conv_w[1]) + nt(grad_proj[2, at, :], conv_w[2]))
                return carry

            lax.fori_loop(0, local // tile, step, 0)

        def f1():
            loaded(8)
            first_slot().wait_send()
            sends.remove(first_slot)

            def to_send(at, value):
                two_send[0, at, :] = value.astype(BF)

            def to_own(at, value):
                own_two[at, :] = value

            first_grad(1 - c, to_send)
            post(lambda: remote(two_send.at[0], two_recv.at[1], a_send.at[5], a_recv.at[5], place.over_c))
            first_grad(c, to_own)

        def n1():
            fetch_tokens().wait()
            arrived(two_recv.at[1], a_recv.at[5], place.over_c)
            scale = gain(0)

            def step(i, carry):
                at = rows(i * 128, 128)
                grad_one = own_two[at, :] + two_recv[1, at, :].astype(F32)
                values = token_rows[at, :].astype(F32)
                inverse = rms(values)
                unit = values * inverse
                two_recv[1, at, :] = (hidden[at, :] + norm_back(grad_one, unit, inverse, scale)).astype(BF)
                return carry + jnp.sum(grad_one * unit, axis=0, keepdims=True)

            mixer_gain = lax.fori_loop(0, local // 128, step, jnp.zeros((1, width), F32))
            stores.append(load(two_recv.at[1], input_grad, 1))
            stores.append(load(hidden_in, own_two, 0))
            zero = jnp.zeros((1, 128), F32)
            for d in range(n_dp):
                cols = slice(d * 128, d * 128 + 128)
                here = (c == (d % 4) // 2).astype(F32)
                own = (d // 4) * half + (d % 2) * 128
                small_sum[d] = jnp.concatenate(
                    [mixer_gain[:, cols], feed_gain[0:1, cols]]
                    + [here * tap_sum[k : k + 1, own : own + 128] for k in range(KW)] + [zero] * 3, axis=0)

        def c2(j, k):
            zk = place.zs(k)
            got = c1_slot(j, zk)
            if Y_FIRST[j]:
                arrived(got, c1_recv.at[j, zk], place.over_y)
                held = g_conv[j, rows(zk * 2 * depth, 2 * depth), rows(y * half, half)]
                src, peer = got.at[rows((1 - x) * depth, depth), :], place.over_x
            else:
                arrived(got, c1_recv.at[j, zk], place.over_x)
                held = g_conv[j, rows((zk * 2 + x) * depth, depth), :]
                src, peer = got.at[:, rows((1 - y) * half, half)], place.over_y
            got[...] = (held.astype(F32) + got[...].astype(F32)).astype(BF)
            post(lambda: remote(src, c_two.at[j, zk], c2_send.at[j, zk], c2_recv.at[j, zk], peer))

        def held_half(j, zk):
            if Y_FIRST[j]:
                return c1_slot(j, zk)[rows(x * depth, depth), :].astype(F32)
            return c1_slot(j, zk)[:, rows(y * half, half)].astype(F32)

        def c3(j, k):
            zk = place.zs(k)
            got = c_two.at[j, zk]
            arrived(got, c2_recv.at[j, zk], place.over_x if Y_FIRST[j] else place.over_y)
            if k:
                got[...] = (held_half(j, zk) + got[...].astype(F32)).astype(BF)
                if k == 2:
                    @pl.when(place.middle)
                    def _():
                        arrived(c_z.at[j, 0], c3_recv.at[j, 0], place.over_z(1))
                        got[...] = (got[...].astype(F32) + c_z[j, 0].astype(F32)).astype(BF)

                post(lambda: z_remote(got, c_z.at[j], c3_send.at[j], c3_recv.at[j], k))

        def cf(j):
            total = z_sum(held_half(j, z) + c_two[j, z].astype(F32), c_z.at[j], c3_recv.at[j])
            if j == 3:
                stage[0:depth, 0:half] = total
                ref = stage.at[0:depth, 0:half]
                z_last(ref, c_z.at[j], c3_recv.at[j])
                out_grad[...] = jnp.transpose(ref[...])
            else:
                in_grad[j] = total
                z_last(in_grad.at[j], c_z.at[j], c3_recv.at[j])

        def fe(w):
            for k in (1, 2):
                arrived(pair_got.at[k], fz_recv.at[w, k], place.over_z(k))
            pair_add(w, 0, (1, 2))

            @pl.when(place.middle)
            def _():
                arrived(pair_got.at[3], fz_recv.at[w, 3], place.over_z(3))
                pair_add(w, 0, (3,))

            post(lambda: remote(g_rows(w, (z * 2 + 1 - x) * depth, depth), x_last, fx_send.at[w, 0], fx_recv.at[w, 0], place.over_x))

        def ff(w):
            ref = (gate_grad, up_grad, stage)[w]
            total = g_rows(w, (z * 2 + x) * depth, depth)[...].astype(F32)
            if Z_FIRST[w]:
                arrived(x_last, fx_recv.at[w, 0], place.over_x)
                ref[...] = total + x_last[...].astype(F32)
            else:
                ref[...] = z_sum(total + x_got[x_slot(w), z].astype(F32), z_got.at[x_slot(w)], fz_recv.at[w])
                z_last(ref, z_got.at[x_slot(w)], fz_recv.at[w])
            if w == 2:
                down_grad[...] = jnp.transpose(stage[...])

        def do():
            stores[1].wait()
            arrived(down_recv.at[1], a_recv.at[7], place.over_c)
            arrived(down_y, a_recv.at[8], place.over_y)

            def step(i, carry):
                at = rows(i * 128, 128)
                total = own_two[at, :] + down_own[at, :].astype(F32) + down_recv[1, at, :].astype(F32) + down_y[at, :].astype(F32)
                down_own[at, :] = total.astype(BF)
                return carry

            lax.fori_loop(0, local // 128, step, 0)
            stores.append(load(down_own, output, 2))

        def s0():
            post(lambda: remote(small_sum, small_got.at[0], s_send.at[0], s_recv.at[0], place.over_c))

        def s1():
            arrived(small_got.at[0], s_recv.at[0], place.over_c)
            small_got[0] = small_sum[...] + small_got[0]
            post(lambda: remote(small_got.at[0], small_got.at[1], s_send.at[1], s_recv.at[1], place.over_y))

        def s2():
            arrived(small_got.at[1], s_recv.at[1], place.over_y)
            small_got[1] = small_got[0] + small_got[1]
            for k in range(NZ):
                zk = place.zs(k)
                post(lambda zk=zk, k=k: remote(
                    small_got.at[1, zk * 2 + 1 - x], small_z.at[zk], s_send.at[2 + k], s_recv.at[2 + zk], place.over_x))

        def s3():
            for k in range(NZ):
                zk = place.zs(k)
                arrived(small_z.at[zk], s_recv.at[2 + zk], place.over_x)
                small_z[zk] = small_z[zk] + small_got[1, zk * 2 + x]
                if k:
                    post(lambda zk=zk, k=k: remote(small_z.at[zk], small_z.at[NZ + k], s_send.at[6 + k], s_recv.at[6 + k], place.over_z(k)))

        def s4():
            total = small_z[z]
            for k in range(1, NZ):
                arrived(small_z.at[NZ + k], s_recv.at[6 + k], place.over_z(k))
                total = total + small_z[NZ + k]
            small_grad[...] = total

        m(1, 2)
        gm()
        w(3)
        w(1)
        c2(3, 1)
        m(0, 0)
        c2(1, 1)
        c2(3, 3)
        m(0, 1)
        c2(1, 3)
        h2()
        w(2)
        w(0)
        c3(3, 3)
        m(0, 2)
        f1()
        ff(2)
        c2(0, 1)
        c2(2, 3)
        n1()
        do()
        s0()
        c2(0, 3)
        c2(3, 2)
        c2(1, 0)
        c2(3, 0)
        c3(3, 2)
        c3(0, 3)
        s1()
        c2(0, 2)
        c2(1, 2)
        c3(1, 1)
        c2(2, 1)
        c3(2, 3)
        s2()
        c3(0, 1)
        c2(2, 0)
        c3(3, 0)
        c3(1, 3)
        c3(2, 1)
        c3(0, 2)
        s3()
        c2(0, 0)
        c3(1, 0)
        c3(2, 0)
        c2(2, 2)
        fe(1)
        c3(3, 1)
        c3(0, 0)
        c3(1, 2)
        c3(2, 2)
        cf(0)
        s4()
        ff(1)
        cf(1)
        ff(0)
        cf(3)
        cf(2)
        for make in sends:
            make().wait_send()
        stores[0].wait()
        stores[2].wait()

    pl.run_scoped(
        conv_phase,
        pltpu.VMEM((CONV, width, mine), BF), pltpu.VMEM((4, chip, mine), BF), pltpu.VMEM((chip, width), BF),
        pltpu.VMEM((chip, mine), BF), pltpu.VMEM((3, chip, mine), BF), pltpu.VMEM((chip + 8, mine), F32), pltpu.VMEM((8, mine), F32),
        pltpu.VMEM((CONV, width, mine), BF),
        pltpu.VMEM((KW - 1, chip + 8, 128), F32), pltpu.VMEM((depth, units), F32),
    )


def backward_call(n_dp, small_all, tokens, cotangent, keep, conv_w, feed_w, *rest):
    local, width = tokens.shape
    units, mine = feed_w.shape[2], conv_w.shape[2]
    chip, half, depth = 2 * local, mine // 2, width // n_dp
    over_y, over_x = sum(Y_FIRST), FEED - sum(Z_FIRST)
    pair = (pltpu.VMEM((NZ, 2 * depth, units), BF), pltpu.VMEM((depth, units), BF))

    def shaped(dims, kind=BF):
        return jax.ShapeDtypeStruct(dims, kind)

    def slots(n, *dims):
        return pltpu.VMEM((max(n, 1), *(dims if n else (NZ, 16, 128))), BF)

    dma = pltpu.SemaphoreType.DMA
    vmem, any_space = pl.BlockSpec(memory_space=pltpu.VMEM), pl.BlockSpec(memory_space=pl.ANY)
    return pl.pallas_call(
        functools.partial(backward_kernel, n_dp),
        name="backward_scatter",
        out_shape=(
            shaped((local, width)), shaped((local, width)), shaped((3, depth, half), F32), shaped((half, depth), F32),
            shaped((depth, units), F32), shaped((depth, units), F32), shaped((units, depth), F32), shaped((8, 128), F32),
        ),
        in_specs=[vmem] + [any_space] * (5 + len(rest)),
        out_specs=(any_space,) * 2 + (vmem,) * 6,
        scratch_shapes=[
            pltpu.VMEM((4 * local, units), BF), pltpu.VMEM((width, units), BF), pltpu.VMEM((over_x, NZ, depth, units), BF),
            pltpu.VMEM((over_x, NZ, depth, units), BF), *pair,
            slots(over_y, NZ, 2 * depth, half), slots(CONV - over_y, NZ, depth, mine), pltpu.VMEM((CONV, NZ, depth, half), BF),
            pltpu.VMEM((CONV, NZ, depth, half), BF), pltpu.VMEM((2, local, width), BF), pltpu.VMEM((2, local, width), BF),
            pltpu.VMEM((local, width), BF), pltpu.VMEM((local, width), F32),
            pltpu.VMEM((2, local, width), BF), pltpu.VMEM((2, local, width), BF), pltpu.VMEM((local, width), BF),
            pltpu.VMEM((local, width), BF), pltpu.VMEM((chip, width), BF),
            pltpu.VMEM((local, width), F32), pltpu.VMEM((local, width), BF), pltpu.VMEM((8, width), F32), pltpu.VMEM((n_dp, 8, 128), F32),
            pltpu.VMEM((2, n_dp, 8, 128), F32), pltpu.VMEM((2 * NZ, 8, 128), F32),
            dma((21,)), dma((FEED, NZ)), dma((FEED, NZ)), dma((FEED, NZ)), dma((FEED, NZ)), dma((CONV, NZ)), dma((CONV, NZ)),
            dma((CONV, NZ)), dma((CONV, NZ)), dma((CONV, NZ)), dma((CONV, NZ)), dma((10,)), dma((10,)), dma((9,)), dma((9,)),
        ],
        compiler_params=pltpu.CompilerParams(collective_id=1, has_side_effects=True, vmem_limit_bytes=63 << 20),
    )(small_all, tokens, cotangent, keep, conv_w, feed_w, *rest)


def finish_kernel(n, small, *refs):
    arrays, outs, held, in_sem, out_sem = refs[:n], refs[n : 2 * n + 3], refs[2 * n + 3 : 3 * n + 3], refs[-2], refs[-1]
    loads = [pltpu.make_async_copy(arrays[i], held[i], in_sem.at[i]) for i in range(n)]
    stores = [pltpu.make_async_copy(held[i], outs[i], out_sem.at[i]) for i in range(n)]
    for copy in loads:
        copy.start()
    outs[n][...] = small[0:1, :]
    outs[n + 1][...] = small[1:2, :]
    outs[n + 2][...] = small[2 : 2 + KW, :]
    for load, store in zip(loads, stores):
        load.wait()
        store.start()
    for copy in stores:
        copy.wait()


def finish_call(small, *arrays):
    vmem, any_space = pl.BlockSpec(memory_space=pltpu.VMEM), pl.BlockSpec(memory_space=pl.ANY)
    n = len(arrays)
    row = small.shape[1]
    return pl.pallas_call(
        functools.partial(finish_kernel, n),
        name="finish",
        out_shape=tuple(jax.ShapeDtypeStruct(a.shape, a.dtype) for a in arrays)
        + tuple(jax.ShapeDtypeStruct((r, row), F32) for r in (1, 1, KW)),
        in_specs=[vmem] + [any_space] * n,
        out_specs=(any_space,) * n + (vmem,) * 3,
        scratch_shapes=[pltpu.VMEM(a.shape, a.dtype) for a in arrays] + [pltpu.SemaphoreType.DMA((n,))] * 2,
        compiler_params=pltpu.CompilerParams(vmem_limit_bytes=62 << 20),
    )(small, *arrays)


def block(n_dp, tokens, doc_ids, mixer_norm, in_weight, conv_weight, out_weight, feed_norm, gate_weight, up_weight, down_weight, out_grad):
    small = jnp.concatenate(
        [mixer_norm[None], feed_norm[None], conv_weight, jnp.zeros((6 - KW, mixer_norm.shape[0]), BF)], axis=0).astype(F32)
    conv_w, feed_w, normed, small_all, cot, proj, mixer_in, hidden, two, acts, keep = forward_call(
        n_dp, tokens, out_grad, doc_ids, small, in_weight.transpose(1, 0, 2), out_weight, gate_weight, up_weight, down_weight)
    *large, small_g = backward_call(
        n_dp, small_all, tokens, out_grad, keep, conv_w, feed_w, normed, cot, proj, mixer_in, hidden, two, acts)
    output, input_grad, in_g, out_g, gate_g, up_g, down_g, mixer_g, feed_g, taps_g = finish_call(small_g, *large)
    return (output, input_grad, mixer_g[0], in_g.transpose(1, 0, 2), taps_g, out_g, feed_g[0], gate_g, up_g, down_g)


def shift_down(values, offset):
    if offset == 0:
        return values
    padding = jnp.zeros((offset,) + values.shape[1:], values.dtype)
    return jnp.concatenate([padding, values[:-offset]], axis=0)


def shift_up(values, offset):
    if offset == 0:
        return values
    padding = jnp.zeros((offset,) + values.shape[1:], values.dtype)
    return jnp.concatenate([values[offset:], padding], axis=0)


def tap_masks(doc_rows):
    total_rows = doc_rows.shape[0] * doc_rows.shape[1]
    tap_keep = [jnp.ones((total_rows,), jnp.float32)]
    for offset in range(1, KW):
        matching = doc_rows[:, offset:] == doc_rows[:, :-offset]
        leading = jnp.zeros((doc_rows.shape[0], offset), dtype=bool)
        matching = jnp.concatenate([leading, matching], axis=1)
        tap_keep.append(jnp.where(matching, 1.0, 0.0).astype(jnp.float32).reshape(total_rows))
    return jnp.stack(tap_keep)


def norm_back(grad_out, unit_rows, inverse, gain):
    scaled = grad_out * gain
    return inverse * (scaled - unit_rows * jnp.mean(scaled * unit_rows, axis=-1, keepdims=True))


def body(
    tokens,
    doc_ids,
    mixer_norm,
    in_weight,
    conv_weight,
    out_weight,
    feed_norm,
    gate_weight,
    up_weight,
    down_weight,
    out_grad,
):
    model_width = tokens.shape[1]
    gathered = (
        lax.all_gather(mixer_norm, "dp", axis=0, tiled=True),
        lax.all_gather(in_weight, "dp", axis=0, tiled=True),
        lax.all_gather(conv_weight, "dp", axis=1, tiled=True),
        lax.all_gather(out_weight, "dp", axis=1, tiled=True),
        lax.all_gather(feed_norm, "dp", axis=0, tiled=True),
        lax.all_gather(gate_weight, "dp", axis=0, tiled=True),
        lax.all_gather(up_weight, "dp", axis=0, tiled=True),
        lax.all_gather(down_weight, "dp", axis=1, tiled=True),
    )
    norm_one, in_full, conv_full, out_full, norm_two, gate_full, up_full, down_full = gathered
    channels = in_full.shape[2]
    channel_start = lax.axis_index("tensor") * channels
    tap_keep = tap_masks(doc_ids)
    conv_taps = lax.dynamic_slice_in_dim(conv_full, channel_start, channels, 1).astype(jnp.float32)
    inputs = tokens.astype(jnp.float32)
    inverse_one = lax.rsqrt(jnp.mean(inputs * inputs, axis=-1, keepdims=True) + epsilon)
    unit_one = inputs * inverse_one
    normed_local = (unit_one * norm_one.astype(jnp.float32)).astype(jnp.bfloat16)
    normed = lax.all_gather(normed_local, "tensor", axis=0, tiled=True)
    projected = jnp.einsum("td,dkc->tkc", normed, in_full, preferred_element_type=jnp.float32)
    input_gate = projected[:, 0]
    output_gate = projected[:, 1]
    values = projected[:, 2]
    mixed_input = input_gate * values
    convolved = sum(
        (
            tap_keep[offset][:, None] * conv_taps[offset][None, :] * shift_down(mixed_input, offset)
            for offset in range(KW)
        )
    )
    mixer_in = (output_gate * convolved).astype(jnp.bfloat16)
    mixer_out = lax.psum_scatter(
        jnp.dot(mixer_in, out_full, preferred_element_type=jnp.float32),
        "tensor",
        scatter_dimension=0,
        tiled=True,
    )
    hidden = inputs + mixer_out
    inverse_two = lax.rsqrt(jnp.mean(hidden * hidden, axis=-1, keepdims=True) + epsilon)
    unit_two = hidden * inverse_two
    normed_two_local = (unit_two * norm_two.astype(jnp.float32)).astype(jnp.bfloat16)
    normed_two = lax.all_gather(normed_two_local, "tensor", axis=0, tiled=True)
    gate_pre = jnp.dot(normed_two, gate_full, preferred_element_type=jnp.float32)
    upward = jnp.dot(normed_two, up_full, preferred_element_type=jnp.float32)
    activated = (jax.nn.silu(gate_pre) * upward).astype(jnp.bfloat16)
    feed_out = lax.psum_scatter(
        jnp.dot(activated, down_full, preferred_element_type=jnp.float32).astype(jnp.bfloat16),
        "tensor",
        scatter_dimension=0,
        tiled=True,
    ).astype(jnp.float32)
    output = (hidden + feed_out).astype(jnp.bfloat16)
    regathered = (
        lax.all_gather(mixer_norm, "dp", axis=0, tiled=True),
        lax.all_gather(in_weight, "dp", axis=0, tiled=True),
        lax.all_gather(conv_weight, "dp", axis=1, tiled=True),
        lax.all_gather(out_weight, "dp", axis=1, tiled=True),
        lax.all_gather(feed_norm, "dp", axis=0, tiled=True),
        lax.all_gather(gate_weight, "dp", axis=0, tiled=True),
        lax.all_gather(up_weight, "dp", axis=0, tiled=True),
        lax.all_gather(down_weight, "dp", axis=1, tiled=True),
    )
    norm_one_b, in_again, conv_again, out_again, norm_two_b, gate_again, up_again, down_again = (
        regathered
    )
    gain_one = norm_one_b.astype(jnp.float32)
    gain_two = norm_two_b.astype(jnp.float32)
    taps_again = lax.dynamic_slice_in_dim(conv_again, channel_start, channels, 1).astype(
        jnp.float32
    )
    sigmoid = jax.nn.sigmoid(gate_pre)
    cotangent = lax.all_gather(out_grad, "tensor", axis=0, tiled=True)
    down_grad = jnp.einsum("tf,td->fd", activated, cotangent, preferred_element_type=jnp.float32)
    grad_act = jnp.einsum("td,fd->tf", cotangent, down_again, preferred_element_type=jnp.float32)
    grad_gate = (grad_act * upward * sigmoid * (1.0 + gate_pre * (1.0 - sigmoid))).astype(
        jnp.bfloat16
    )
    grad_up = (grad_act * gate_pre * sigmoid).astype(jnp.bfloat16)
    gate_grad = jnp.einsum("td,tf->df", normed_two, grad_gate, preferred_element_type=jnp.float32)
    up_grad = jnp.einsum("td,tf->df", normed_two, grad_up, preferred_element_type=jnp.float32)
    grad_two = lax.psum_scatter(
        (
            jnp.einsum("tf,df->td", grad_gate, gate_again, preferred_element_type=jnp.float32)
            + jnp.einsum("tf,df->td", grad_up, up_again, preferred_element_type=jnp.float32)
        ).astype(jnp.bfloat16),
        "tensor",
        scatter_dimension=0,
        tiled=True,
    ).astype(jnp.float32)
    feed_gain_part = jnp.sum(grad_two * unit_two, axis=0)
    grad_hidden = out_grad.astype(jnp.float32) + norm_back(
        grad_two, unit_two, inverse_two, gain_two
    )
    grad_mix_local = grad_hidden.astype(jnp.bfloat16)
    grad_mix = lax.all_gather(grad_mix_local, "tensor", axis=0, tiled=True)
    out_grad_part = jnp.einsum("tc,td->cd", mixer_in, grad_mix, preferred_element_type=jnp.float32)
    grad_in = jnp.einsum("td,cd->tc", grad_mix, out_again, preferred_element_type=jnp.float32)
    grad_c = grad_in * convolved
    grad_conv = grad_in * output_gate
    grad_mixed = sum(
        (
            taps_again[offset][None, :] * shift_up(tap_keep[offset][:, None] * grad_conv, offset)
            for offset in range(KW)
        )
    )
    tap_grad = jnp.stack(
        [
            jnp.sum(tap_keep[offset][:, None] * grad_conv * shift_down(mixed_input, offset), axis=0)
            for offset in range(KW)
        ]
    )
    grad_projected = jnp.stack(
        [grad_mixed * values, grad_c, grad_mixed * input_gate], axis=1
    ).astype(jnp.bfloat16)
    in_grad_part = jnp.einsum(
        "td,tkc->dkc", normed, grad_projected, preferred_element_type=jnp.float32
    )
    grad_one = lax.psum_scatter(
        jnp.einsum(
            "tkc,dkc->td", grad_projected, in_again, preferred_element_type=jnp.float32
        ).astype(jnp.bfloat16),
        "tensor",
        scatter_dimension=0,
        tiled=True,
    ).astype(jnp.float32)
    mixer_gain_part = jnp.sum(grad_one * unit_one, axis=0)
    input_grad = (grad_hidden + norm_back(grad_one, unit_one, inverse_one, gain_one)).astype(
        jnp.bfloat16
    )
    conv_part = lax.dynamic_update_slice_in_dim(
        jnp.zeros((KW, model_width), jnp.float32), tap_grad, channel_start, 1
    )
    summed = (
        lax.psum_scatter(mixer_gain_part, "dp", scatter_dimension=0, tiled=True),
        lax.psum_scatter(in_grad_part, "dp", scatter_dimension=0, tiled=True),
        lax.psum_scatter(conv_part, "dp", scatter_dimension=1, tiled=True),
        lax.psum_scatter(out_grad_part, "dp", scatter_dimension=1, tiled=True),
        lax.psum_scatter(feed_gain_part, "dp", scatter_dimension=0, tiled=True),
        lax.psum_scatter(gate_grad, "dp", scatter_dimension=0, tiled=True),
        lax.psum_scatter(up_grad, "dp", scatter_dimension=0, tiled=True),
        lax.psum_scatter(down_grad, "dp", scatter_dimension=1, tiled=True),
    )
    (
        mixer_gain_sum,
        in_weight_grad,
        conv_sum,
        out_weight_grad,
        feed_gain_sum,
        gate_weight_grad,
        up_weight_grad,
        down_weight_grad,
    ) = summed
    mixer_norm_grad, conv_weight_grad, feed_norm_grad = lax.psum(
        (mixer_gain_sum, conv_sum, feed_gain_sum), "tensor"
    )
    return (
        output,
        input_grad,
        mixer_norm_grad,
        in_weight_grad,
        conv_weight_grad,
        out_weight_grad,
        feed_norm_grad,
        gate_weight_grad,
        up_weight_grad,
        down_weight_grad,
    )


def solution(mesh):
    in_specs = (
        P(("dp", "tensor"), None),
        P("dp", None),
        P("dp"),
        P("dp", None, "tensor"),
        P(None, "dp"),
        P("tensor", "dp"),
        P("dp"),
        P("dp", "tensor"),
        P("dp", "tensor"),
        P("tensor", "dp"),
        P(("dp", "tensor"), None),
    )
    out_specs = (
        P(("dp", "tensor"), None),
        P(("dp", "tensor"), None),
        P("dp"),
        P("dp", None, "tensor"),
        P(None, "dp"),
        P("tensor", "dp"),
        P("dp"),
        P("dp", "tensor"),
        P("dp", "tensor"),
        P("tensor", "dp"),
    )
    n_dp = mesh.shape["dp"]
    fits = n_dp == 2 * NZ and mesh.shape["tensor"] == 4
    step = functools.partial(block, n_dp) if fits else body
    return jax.shard_map(step, mesh=mesh, in_specs=in_specs, out_specs=out_specs, check_vma=False)
```
